32 devices in a mesh: rec: 8 (over z, core), frame: 4 (over y, x).
Axes of the slice: x: 2, y: 2, z: 4, core: 2. Of those that a mesh axis runs over, the one named last changes fastest.
Arguments:
- frames: bfloat16 [8, 6144, 256], P('rec', 'frame'), may hold values from -10 to 10
- texts: bfloat16 [16, 224, 256], P('rec', 'frame'), may hold values from -100 to 100
- pair_rec: int32 [16, 1], replicated, may hold values from 0 to 7, as said below
- pair_text: int32 [16], replicated, may hold values from 0 to 15, as said below
- pair_label: int32 [16], replicated, may hold values 0 or 1
Outputs:
- loss: float32 [], replicated
- grad_frames: bfloat16 [8, 6144, 256], P('rec', 'frame')
- grad_texts: bfloat16 [16, 224, 256], P('rec', 'frame')
The draws below stay inside these ranges and needn't reach their ends.
Inputs may be any that keep to these rules, and one draw needn't show every extreme that they name: `pair_rec`: no recording is named by more than 6 pairs, some recording by exactly 6, and every recording by at least one. A pair's text is held by the index of rec one after, one before, or 4 after its recording (counted round): pair_text // 2 = (pair_rec + k) mod 8 with k one of 1, 7, 4.
All inputs are finite; a program needn't handle non-finite values.
Results may differ from the reference program's by a relative error of at most 0.0085.
Values may be sent and summed in bfloat16 or wider, within the bound.
No kernel may reach another device: no remote copies, remote signals or barrier semaphores. Data moves between devices by JAX's collectives and lax.ppermute only.
A program may use at most 64 MiB of HBM per device.

```python
import jax
import jax.numpy as jnp
from jax import lax

D = 256
L = 224
MOST = 6
TXT_DEV = 2
RECS = 8
FRAMES = 6144
TEXTS = 16
PAIRS = 16


LOG_EIGHT = 2.0794415


def recording_offset(key):
    direction = jnp.clip(jax.random.normal(jax.random.fold_in(key, 5), (RECS, D), jnp.float32), -4.0, 4.0)
    strength = jax.random.uniform(jax.random.fold_in(key, 6), (RECS, 1), jnp.float32, 0.3, 0.9)
    return strength * direction


def token_scales(key, top):
    exponent = jax.random.uniform(jax.random.fold_in(key, 7), (TEXTS, L, 1), jnp.float32, 0.0, top)
    return jnp.exp(exponent)


def draw_frames(key, part):
    offset = recording_offset(key)
    base = jnp.clip(jax.random.normal(jax.random.fold_in(key, 1), (RECS, FRAMES, D), jnp.float32), -6.0, 6.0)
    base = base + offset[:, None, :]
    return jnp.clip(base, -10.0, 10.0).astype(jnp.bfloat16)


def draw_texts(key, part):
    base = jnp.clip(jax.random.normal(jax.random.fold_in(key, 3), (TEXTS, L, D), jnp.float32), -6.0, 6.0)
    base = base * token_scales(key, LOG_EIGHT)
    return base.astype(jnp.bfloat16)


def pair_lists(key):
    order_table = jax.random.permutation(jax.random.fold_in(key, 211), RECS).astype(jnp.int32)
    position = jnp.arange(RECS, dtype=jnp.int32)
    extra_count = PAIRS - MOST - (RECS - 1)
    counts = jnp.where(position == 0, MOST, 1 + ((position >= 1) & (position <= extra_count)).astype(jnp.int32))
    boundary = jnp.cumsum(counts)
    pair_index = jnp.arange(PAIRS, dtype=jnp.int32)
    group_index = jnp.sum((pair_index[:, None] >= boundary[None, :]).astype(jnp.int32), axis=1)
    record = order_table[group_index]
    shuffle = jax.random.permutation(jax.random.fold_in(key, 223), PAIRS)
    record = record[shuffle]
    offset_draw = jax.random.randint(jax.random.fold_in(key, 227), (PAIRS,), 0, 8)
    offset = jnp.where(offset_draw < 3, 1, jnp.where(offset_draw < 6, RECS - 1, RECS // 2))
    text_owner = (record + offset) % RECS
    pair_texts = TXT_DEV * text_owner + jax.random.randint(jax.random.fold_in(key, 229), (PAIRS,), 0, TXT_DEV)
    return (record.astype(jnp.int32), pair_texts.astype(jnp.int32))


def draw_pair_rec(key, part):
    record, pair_texts = pair_lists(key)
    return record[:, None]


def draw_pair_text(key, part):
    record, pair_texts = pair_lists(key)
    return pair_texts


def touch_ends(result, rng, low, top_value):
    index_at = [jax.random.randint(jax.random.fold_in(rng, axis), (), 0, length) for axis, length in enumerate(result.shape)]
    main_axis = result.shape.index(max(result.shape))
    beside = index_at[:main_axis] + [(index_at[main_axis] + 1) % result.shape[main_axis]] + index_at[main_axis + 1:]
    return result.at[tuple(index_at)].set(low).at[tuple(beside)].set(top_value)


def setup_inputs(seed: int = 0) -> dict:
    seeds = jax.random.split(jax.random.key(seed), 6)
    return {
        "frames": draw_frames(jax.random.fold_in(seeds[5], 71), 0),
        "texts": draw_texts(jax.random.fold_in(seeds[5], 71), 0),
        "pair_rec": draw_pair_rec(jax.random.fold_in(seeds[5], 71), 0),
        "pair_text": draw_pair_text(jax.random.fold_in(seeds[5], 71), 0),
        "pair_label": touch_ends((jax.random.randint(seeds[4], (PAIRS,), 0, 2) < 1).astype(jnp.int32), jax.random.fold_in(seeds[4], 1), 0, 1),
    }


EPS = 1e-06
TEMP = 10.0
BIAS = -1.0
LOSS_SCALE = 2048.0

def slot_tables(pair_rec, pair_text, pair_label, here, most):
    record = pair_rec[:, 0]
    count = record.shape[0]
    order = jnp.arange(count, dtype=jnp.int32)
    same = (record[:, None] == record[None, :]).astype(jnp.int32)
    earlier = (order[None, :] < order[:, None]).astype(jnp.int32)
    rank = lax.optimization_barrier(jnp.sum(same * earlier, axis=1))
    places = jnp.arange(most, dtype=jnp.int32)
    chosen = ((record[None, :] == here) & (rank[None, :] == places[:, None])).astype(jnp.int32)
    valid = lax.optimization_barrier(jnp.sum(chosen, axis=1))
    slot_text = lax.optimization_barrier(jnp.sum(chosen * pair_text[None, :], axis=1))
    sign = lax.optimization_barrier(jnp.sum(chosen * (2 * pair_label[None, :] - 1), axis=1))
    return (valid, slot_text, sign)

def slot_pass(upstream_signal, query_vectors, valid, sign):
    logit_scale = D ** (-0.5)
    pair_scores = jnp.dot(query_vectors, upstream_signal.T, preferred_element_type=jnp.float32) * logit_scale
    row_max = lax.optimization_barrier(jnp.max(pair_scores, axis=1))
    expo = jnp.exp(pair_scores - row_max[:, None])
    batch_weights = expo.astype(jnp.bfloat16)
    context = jnp.dot(batch_weights, upstream_signal, preferred_element_type=jnp.float32)
    query_f = query_vectors.astype(jnp.float32)
    q_norm = lax.rsqrt(lax.optimization_barrier(jnp.sum(query_f * query_f, axis=1)) + EPS)
    c_norm = lax.rsqrt(lax.optimization_barrier(jnp.sum(context * context, axis=1)) + EPS)
    q_unit = query_f * q_norm[:, None]
    c_unit = context * c_norm[:, None]
    cos = lax.optimization_barrier(jnp.sum(q_unit * c_unit, axis=1))
    score = jnp.mean(cos)
    margin = -sign * (TEMP * score + BIAS)
    loss_part = valid * jax.nn.softplus(margin)
    grad_cos = -LOSS_SCALE * TEMP * valid * sign * jax.nn.sigmoid(margin) / L
    d_context = grad_cos * (q_unit - cos[:, None] * c_unit) * c_norm[:, None]
    direct = grad_cos * (c_unit - cos[:, None] * q_unit) * q_norm[:, None]
    context_batch_gradient = d_context.astype(jnp.bfloat16)
    weight_gradient = jnp.dot(context_batch_gradient, upstream_signal.T, preferred_element_type=jnp.float32)
    score_gradient = (expo * weight_gradient * logit_scale).astype(jnp.bfloat16)
    d_query = jnp.dot(score_gradient, upstream_signal, preferred_element_type=jnp.float32) + direct
    d_frames = jnp.dot(score_gradient.T, query_vectors, preferred_element_type=jnp.float32)
    d_frames = d_frames + jnp.dot(batch_weights.T, context_batch_gradient, preferred_element_type=jnp.float32)
    return (loss_part, d_query, d_frames)

def reference(frames, texts, pair_rec, pair_text, pair_label):

    def per_record(carry, inputs):
        text_grad, loss = carry
        upstream_signal, here = inputs
        valid, slot_text, sign = slot_tables(pair_rec, pair_text, pair_label, here, MOST)
        query_vectors = jnp.take(texts, slot_text, axis=0)

        def per_slot(frame_grad, slot_in):
            one_query, one_valid, one_sign = slot_in

            def active(operands):
                return slot_pass(upstream_signal, operands[0], operands[1], operands[2])

            def silent(operands):
                return (jnp.zeros((), jnp.float32), jnp.zeros((L, D), jnp.float32), jnp.zeros((FRAMES, D), jnp.float32))
            loss_part, d_query, d_frames = lax.cond(one_valid > 0, active, silent, (one_query, one_valid, one_sign))
            return (frame_grad + d_frames, (loss_part, d_query))
        frame_grad, outputs = lax.scan(per_slot, jnp.zeros((FRAMES, D), jnp.float32), (query_vectors, valid.astype(jnp.float32), sign.astype(jnp.float32)))
        losses, d_query = outputs
        text_grad = text_grad.at[slot_text].add(d_query * valid.astype(jnp.float32)[:, None, None])
        return ((text_grad, loss + jnp.sum(losses)), frame_grad.astype(jnp.bfloat16))
    start = (jnp.zeros((TEXTS, L, D), jnp.float32), jnp.zeros((), jnp.float32))
    final, grad_frames = lax.scan(per_record, start, (frames, jnp.arange(RECS, dtype=jnp.int32)))
    text_grad, loss = final
    return (loss, grad_frames, text_grad.astype(jnp.bfloat16))
```

```python
import functools

import jax
import jax.numpy as jnp
from jax import lax
from jax.experimental import pallas as pl
from jax.experimental.pallas import tpu as pltpu
from jax.sharding import PartitionSpec as P

MOST = 6
EPS = 1e-06
TEMP = 10.0
BIAS = -1.0
LOSS_SCALE = 2048.0

F32 = jnp.float32
BF16 = jnp.bfloat16
EXTRA = 16
AXES = ("rec", "frame")
VMEM = pl.BlockSpec(memory_space=pltpu.VMEM)
SMEM = pl.BlockSpec(memory_space=pltpu.SMEM)


def nt(a, b):
    return lax.dot_general(a, b, (((1,), (1,)), ((), ())), preferred_element_type=F32)


def nn(a, b):
    return lax.dot_general(a, b, (((1,), (0,)), ((), ())), preferred_element_type=F32)


def tn(a, b):
    return lax.dot_general(a, b, (((0,), (0,)), ((), ())), preferred_element_type=F32)


def lines(rows, width):
    return -(-rows // width)


def on_diagonal(rows, width, k):
    r = lax.broadcasted_iota(jnp.int32, (rows, width), 0)
    c = lax.broadcasted_iota(jnp.int32, (rows, width), 1)
    return r == c + k * width


def pack(columns, width):
    rows = columns[0].shape[0]
    place = lax.broadcasted_iota(jnp.int32, (EXTRA, width), 0)
    out = jnp.zeros((EXTRA, width), F32)
    at = 0
    for k in range(lines(rows, width)):
        diagonal = on_diagonal(rows, width, k)
        for column in columns:
            rest = jnp.sum(jnp.where(diagonal, column, 0.0), axis=0, keepdims=True)
            for _ in range(3):
                piece = rest.astype(BF16).astype(F32)
                out = jnp.where(place == at, piece, out)
                rest = rest - piece
                at += 1
    return out.astype(BF16)


def unpack_line(extra, k, i, n):
    at = 3 * (k * n + i)
    place = lax.broadcasted_iota(jnp.int32, extra.shape, 0)
    got = [jnp.sum(jnp.where(place == at + j, extra, 0.0), axis=0, keepdims=True) for j in range(3)]
    return (got[0] + got[1]) + got[2]


def unpack_column(extra, rows, i, n):
    width = extra.shape[1]
    out = jnp.zeros((rows, 1), F32)
    for k in range(lines(rows, width)):
        line = unpack_line(extra, k, i, n)
        out = out + jnp.sum(jnp.where(on_diagonal(rows, width, k), line, 0.0), axis=1, keepdims=True)
    return out


def table_kernel(rec_ref, text_ref, label_ref, me_ref, out_ref, count_ref, *, recs, owned):
    pairs = text_ref.shape[0]
    here = me_ref[0]
    near, far, cross = here ^ 1, me_ref[1], me_ref[2]
    n_cand = 3 * owned
    for i in range(4 * n_cand + 1):
        out_ref[i] = 0
    for r in range(recs):
        count_ref[r] = 0

    def pair(p, carry):
        rec, text, label = rec_ref[p, 0], text_ref[p], label_ref[p]
        repeats = lax.fori_loop(
            0, p, lambda q, n: n + jnp.where((rec_ref[q, 0] == rec) & (text_ref[q] == text), 1, 0), 0
        )
        count_ref[rec] = count_ref[rec] + jnp.where(repeats == 0, 1, 0)
        out_ref[4 * n_cand] = jnp.maximum(out_ref[4 * n_cand], count_ref[rec])
        mine = jnp.where(rec == here, 1, 0)
        for w, owner in enumerate((near, far, cross)):
            for j in range(owned):
                hit = mine * jnp.where(text == owner * owned + j, 1, 0)
                c = w * owned + j
                out_ref[c] = out_ref[c] + hit * label
                out_ref[n_cand + c] = out_ref[n_cand + c] + hit * (1 - label)
        return carry

    lax.fori_loop(0, pairs, pair, 0)
    for s in range(n_cand):
        out_ref[3 * n_cand + s] = -1
    at = jnp.int32(0)
    for c in range(n_cand):
        used = (out_ref[c] + out_ref[n_cand + c]) > 0
        out_ref[2 * n_cand + c] = jnp.where(used, at, -1)

        @pl.when(used)
        def _(at=at, c=c):
            out_ref[3 * n_cand + at] = c

        at = at + jnp.where(used, 1, 0)


def select_kernel(table_ref, a_ref, b_ref, c_ref, out_ref, *, slots, n_cand):
    owned, w, _ = a_ref.shape
    for s in range(slots):
        c = table_ref[3 * n_cand + s]
        out_ref[s] = jnp.zeros(out_ref.shape[1:], out_ref.dtype)
        for i, ref in enumerate((a_ref, b_ref, c_ref)):

            @pl.when((c >= i * owned) & (c < (i + 1) * owned))
            def _(ref=ref, i=i, s=s, c=c):
                out_ref[s] = ref[c - i * owned]


class Parts:
    def __init__(self, count, stacked):
        self.count, self.stacked = count, stacked
        self.refs = 1 if stacked else count

    def at(self, refs, j):
        return refs[0].at[j] if self.stacked else refs[j]

    def each(self, body):
        if self.stacked:
            lax.fori_loop(0, self.count, lambda j, _: (body(j), 0)[1], 0)
        else:
            for j in range(self.count):
                body(j)

    def shape(self, shape, dtype):
        if self.stacked:
            return [jax.ShapeDtypeStruct((self.count,) + shape, dtype)]
        return [jax.ShapeDtypeStruct(shape, dtype)] * self.count


def forward_kernel(f_ref, *refs, parts, scale):
    q_refs, out_refs = refs[: parts.refs], refs[parts.refs :]

    def part(j):
        q_ref, out_ref = parts.at(q_refs, j), parts.at(out_refs, j)
        rows, width = q_ref.shape
        s = nt(q_ref[...], f_ref[...]) * scale
        top = jnp.max(s, axis=1, keepdims=True)
        weights = jnp.exp(s - top).astype(BF16)
        out_ref[:rows] = nn(weights, f_ref[...]).astype(BF16)
        out_ref[rows:] = pack([top], width)

    parts.each(part)


def token_kernel(q_ref, *refs, parts):
    in_refs, (u_ref, direct_ref, c_ref, m_ref) = refs[: parts.refs], refs[parts.refs :]
    rows, width = q_ref.shape
    m_ref[...] = jnp.full(m_ref.shape, -jnp.inf, F32)

    def top(j):
        extra = parts.at(in_refs, j)[rows:].astype(F32)
        m_ref[...] = jnp.maximum(m_ref[...], unpack_column(extra, rows, 0, 1))

    parts.each(top)
    m = m_ref[...]
    c_ref[...] = jnp.zeros(c_ref.shape, F32)

    def add(j):
        ref = parts.at(in_refs, j)
        extra = ref[rows:].astype(F32)
        share = jnp.exp(unpack_column(extra, rows, 0, 1) - m)
        c_ref[...] = c_ref[...] + share * ref[:rows].astype(F32)

    parts.each(add)
    c = c_ref[...]
    q = q_ref[...].astype(F32)
    q_norm = lax.rsqrt(jnp.sum(q * q, axis=1, keepdims=True) + EPS)
    c_norm = lax.rsqrt(jnp.sum(c * c, axis=1, keepdims=True) + EPS)
    q_unit, c_unit = q * q_norm, c * c_norm
    cos = jnp.sum(q_unit * c_unit, axis=1, keepdims=True)
    u_ref[:rows] = ((q_unit - cos * c_unit) * c_norm).astype(BF16)
    u_ref[rows:] = pack([m, cos], width)
    direct_ref[...] = (c_unit - cos * q_unit) * q_norm


def backward_kernel(table_ref, own_ref, f_ref, direct_ref, *refs, parts, slots, w, tokens, scale, n_cand):
    n = parts.refs
    q_refs, u_refs = refs[:n], refs[n : 2 * n]
    dq_refs, ds_refs, gw_refs = refs[2 * n : 3 * n], refs[3 * n : 4 * n], refs[4 * n : 5 * n]
    own_dq_ref, loss_ref, line_ref = refs[5 * n :]
    rows, width = direct_ref.shape
    k_lines = lines(rows, width)

    line_ref[...] = jnp.zeros(line_ref.shape, F32)

    def add(j):
        extra = parts.at(u_refs, j)[rows:].astype(F32)
        for k in range(k_lines):
            line_ref[pl.ds(k, 1)] = line_ref[pl.ds(k, 1)] + unpack_line(extra, k, 1, 2)

    parts.each(add)
    lane = lax.broadcasted_iota(jnp.int32, (1, width), 1)
    row = lax.broadcasted_iota(jnp.int32, (rows, 1), 0)
    g = jnp.zeros((rows, 1), F32)
    loss = jnp.zeros((1, 1), F32)
    for s in range(slots):
        total = jnp.zeros((1, 1), F32)
        for k in range(k_lines):
            token = lane + k * width
            inside = (token >= s * w) & (token < (s + 1) * w)
            total = total + jnp.sum(jnp.where(inside, line_ref[pl.ds(k, 1)], 0.0), axis=1, keepdims=True)
        logit = TEMP * (total / tokens) + BIAS
        c = table_ref[3 * n_cand + s]
        at = jnp.maximum(c, 0)
        used = jnp.where(c >= 0, 1, 0)
        pos = (used * table_ref[at]).astype(F32)
        neg = (used * table_ref[n_cand + at]).astype(F32)
        tail = jnp.log1p(jnp.exp(-jnp.abs(logit)))
        loss = loss + pos * (jnp.maximum(-logit, 0.0) + tail) + neg * (jnp.maximum(logit, 0.0) + tail)
        slope = pos * jax.nn.sigmoid(-logit) - neg * jax.nn.sigmoid(logit)
        here = (row >= s * w) & (row < (s + 1) * w)
        g = jnp.where(here, (-LOSS_SCALE * TEMP / tokens) * slope, g)
    loss_ref[...] = jnp.broadcast_to(loss, loss_ref.shape)

    def part(j):
        q_ref, u_ref = parts.at(q_refs, j), parts.at(u_refs, j)
        m = unpack_column(u_ref[rows:].astype(F32), rows, 0, 2)
        s = nt(q_ref[...], f_ref[...]) * scale
        gw = jnp.exp(s - m) * g
        parts.at(gw_refs, j)[...] = gw.astype(BF16)
        dw = nt(u_ref[:rows], f_ref[...])
        ds = (gw * dw * scale).astype(BF16)
        parts.at(ds_refs, j)[...] = ds
        dq = nn(ds, f_ref[...])
        parts.at(dq_refs, j)[...] = dq.astype(BF16)
        if parts.stacked:

            @pl.when(j == own_ref[0])
            def _():
                own_dq_ref[...] = dq + g * direct_ref[...]

        elif j == 0:
            own_dq_ref[...] = dq + g * direct_ref[...]

    parts.each(part)


def frames_kernel(*refs, parts):
    n = parts.refs
    q_refs, u_refs, ds_refs, gw_refs = refs[:n], refs[n : 2 * n], refs[2 * n : 3 * n], refs[3 * n : 4 * n]
    out_ref, acc_ref = refs[4 * n :]
    if not parts.stacked:
        rows = q_refs[0].shape[0]
        total = None
        for j in range(parts.count):
            term = tn(ds_refs[j][...], q_refs[j][...]) + tn(gw_refs[j][...], u_refs[j][:rows])
            total = term if total is None else total + term
        out_ref[0] = total.astype(BF16)
        return
    acc_ref[...] = jnp.zeros(acc_ref.shape, F32)

    def part(j):
        q_ref, u_ref = parts.at(q_refs, j), parts.at(u_refs, j)
        rows = q_ref.shape[0]
        acc_ref[...] = acc_ref[...] + tn(parts.at(ds_refs, j)[...], q_ref[...])
        acc_ref[...] = acc_ref[...] + tn(parts.at(gw_refs, j)[...], u_ref[:rows])

    parts.each(part)
    out_ref[0] = acc_ref[...].astype(BF16)


def finish_kernel(table_ref, own_ref, own_dq_ref, *refs, parts, slots, w, n_cand):
    n = parts.refs if parts.stacked else parts.refs - 1
    in_refs, outs, total_ref, slot_ref = refs[:n], refs[n : n + 3], refs[n + 3], refs[n + 4]
    owned = n_cand // 3
    total_ref[...] = own_dq_ref[...]
    if parts.stacked:

        def add(j, carry):
            @pl.when(j != own_ref[0])
            def _():
                total_ref[...] = total_ref[...] + in_refs[0][j].astype(F32)

            return carry

        lax.fori_loop(0, parts.count, add, 0)
    else:
        total = total_ref[...]
        for ref in in_refs:
            total = total + ref[...].astype(F32)
        total_ref[...] = total
    for s in range(slots):
        slot_ref[s] = total_ref[s * w : (s + 1) * w]
    for c in range(n_cand):
        s = table_ref[2 * n_cand + c]
        ref, j = outs[c // owned], c % owned
        ref[j] = jnp.zeros(ref.shape[1:], ref.dtype)

        @pl.when(s >= 0)
        def _(ref=ref, j=j, s=s):
            ref[j] = slot_ref[s].astype(ref.dtype)


def call(kernel, name, out_shape, in_specs, *args, scratch=(), flops=0, nbytes=1 << 20):
    many = isinstance(out_shape, (list, tuple))
    return pl.pallas_call(
        kernel,
        name=name,
        out_shape=out_shape,
        in_specs=in_specs,
        out_specs=[VMEM] * len(out_shape) if many else VMEM,
        scratch_shapes=list(scratch),
        cost_estimate=pl.CostEstimate(flops=flops, bytes_accessed=nbytes, transcendentals=0),
    )(*args)


def permute(x, recs, group, move):
    pairs = []
    for r in range(recs):
        for f in range(group):
            to_r, to_f = move(r, f)
            pairs.append((r * group + f, to_r * group + to_f))
    return lax.ppermute(x, AXES, pairs)


def near_of(r, recs):
    return r ^ 1


def far_of(r, recs):
    return (r - 1) % recs if r % 2 == 0 else (r + 1) % recs


def cross_of(r, recs):
    return (r + recs // 2) % recs


def slot_body(slots, parts, w, tokens, recs, frames, near, far, cross, table, own):
    group = parts.count
    owned, _, width = near.shape
    n_cand = 3 * owned
    rows = slots * w
    depth = frames.shape[1]
    f = frames[0]
    scale = width ** (-0.5)
    unit = 2 * rows * group * depth * width

    q = call(
        functools.partial(select_kernel, slots=slots, n_cand=n_cand),
        "select",
        jax.ShapeDtypeStruct((slots, w, width), BF16),
        [SMEM, VMEM, VMEM, VMEM],
        table, near, far, cross,
    ).reshape(rows, width)

    def spread(x):
        if parts.stacked:
            return [lax.all_gather(x, "frame", axis=0)]
        return [x] + [permute(x, recs, group, lambda r, g, j=j: (r, g ^ j)) for j in range(1, group)]

    def exchange(blocks):
        if parts.stacked:
            return [lax.all_to_all(blocks[0], "frame", 0, 0, tiled=True)]
        return [permute(blocks[j], recs, group, lambda r, g, j=j: (r, g ^ j)) for j in range(1, group)]

    qs = spread(q)
    contexts = call(
        functools.partial(forward_kernel, parts=parts, scale=scale),
        "forward",
        parts.shape((rows + EXTRA, width), BF16),
        [VMEM] * (1 + parts.refs),
        f, *qs, flops=2 * unit,
    )
    mine = exchange(contexts)
    if not parts.stacked:
        mine = [contexts[0]] + mine
    u, direct = call(
        functools.partial(token_kernel, parts=parts),
        "tokens",
        [jax.ShapeDtypeStruct((rows + EXTRA, width), BF16), jax.ShapeDtypeStruct((rows, width), F32)],
        [VMEM] * (1 + parts.refs),
        q, *mine,
        scratch=[pltpu.VMEM((rows, width), F32), pltpu.VMEM((rows, 1), F32)],
    )
    us = spread(u)
    n = parts.refs
    results = call(
        functools.partial(
            backward_kernel, parts=parts, slots=slots, w=w, tokens=tokens, scale=scale, n_cand=n_cand
        ),
        "backward",
        parts.shape((rows, width), BF16)
        + parts.shape((rows, depth), BF16) * 2
        + [jax.ShapeDtypeStruct((rows, width), F32), jax.ShapeDtypeStruct((1, 128), F32)],
        [SMEM, SMEM] + [VMEM] * (2 + 2 * n),
        table, own, f, direct, *qs, *us,
        scratch=[pltpu.VMEM((8, width), F32)],
        flops=3 * unit,
    )
    dqs, dss, gws = results[:n], results[n : 2 * n], results[2 * n : 3 * n]
    own_dq, loss = results[3 * n :]
    parts_dq = exchange(dqs)
    grad_frames = call(
        functools.partial(frames_kernel, parts=parts),
        "frames",
        jax.ShapeDtypeStruct(frames.shape, BF16),
        [VMEM] * (4 * n),
        *qs, *us, *dss, *gws,
        scratch=[pltpu.VMEM((depth, width) if parts.stacked else (8, 128), F32)],
        flops=2 * unit,
    )
    step = 1
    while step < recs:
        loss = loss + permute(loss, recs, group, lambda r, g, k=step: (r ^ k, g))
        step *= 2
    back = call(
        functools.partial(finish_kernel, parts=parts, slots=slots, w=w, n_cand=n_cand),
        "finish",
        [jax.ShapeDtypeStruct((owned, w, width), BF16)] * 3,
        [SMEM, SMEM] + [VMEM] * (1 + len(parts_dq)),
        table, own, own_dq, *parts_dq,
        scratch=[pltpu.VMEM((rows, width), F32), pltpu.VMEM((slots, w, width), F32)],
    )
    texts = 0
    for x, where in zip(back, (near_of, far_of, cross_of)):
        texts = texts + permute(x, recs, group, lambda r, g: (where(r, recs), g)).astype(F32)
    return loss[0, 0], grad_frames, texts.astype(BF16)


def body(frames, texts, pair_rec, pair_text, pair_label):
    recs, group = lax.axis_size("rec"), lax.axis_size("frame")
    here = lax.axis_index("rec")
    owned, held, width = texts.shape
    w = -(-held // 8) * 8
    tokens = held * group
    parts = Parts(group, group > 4)
    sent = jnp.pad(texts, ((0, 0), (0, w - held), (0, 0))) if w != held else texts
    near, far, cross = [
        permute(sent, recs, group, lambda r, g, to=to: (to(r, recs), g)) for to in (near_of, far_of, cross_of)
    ]
    far_rec = jnp.where(here % 2 == 0, here - 1 + recs, here + 1) % recs
    me = jnp.stack([here, far_rec, (here + recs // 2) % recs]).astype(jnp.int32)
    own = lax.axis_index("frame").astype(jnp.int32).reshape(1)
    n_cand = 3 * owned
    table = pl.pallas_call(
        functools.partial(table_kernel, recs=recs, owned=owned),
        name="table",
        out_shape=jax.ShapeDtypeStruct((4 * n_cand + 1,), jnp.int32),
        in_specs=[SMEM] * 4,
        out_specs=SMEM,
        scratch_shapes=[pltpu.SMEM((recs,), jnp.int32)],
    )(pair_rec, pair_text, pair_label, me)
    loss, grad_frames, grad_texts = slot_body(
        MOST, parts, w, tokens, recs, frames, near, far, cross, table, own
    )
    return loss, grad_frames, grad_texts[:, :held] if w != held else grad_texts


def solution(mesh):
    return jax.shard_map(
        body,
        mesh=mesh,
        in_specs=(P("rec", "frame", None), P("rec", "frame", None), P(), P(), P()),
        out_specs=(P(), P("rec", "frame", None), P("rec", "frame", None)),
        check_vma=False,
    )
```

```python
import functools

import jax
import jax.numpy as jnp
from jax import lax
from jax.experimental import pallas as pl
from jax.experimental.pallas import tpu as pltpu
from jax.sharding import PartitionSpec as P

MOST = 6
EPS = 1e-06
TEMP = 10.0
BIAS = -1.0
LOSS_SCALE = 2048.0

F32 = jnp.float32
BF16 = jnp.bfloat16
EXTRA = 16
LINES = 8
AXES = ("rec", "frame")
VMEM = pl.BlockSpec(memory_space=pltpu.VMEM)
SMEM = pl.BlockSpec(memory_space=pltpu.SMEM)


def nt(a, b):
    return lax.dot_general(a, b, (((1,), (1,)), ((), ())), preferred_element_type=F32)


def nn(a, b):
    return lax.dot_general(a, b, (((1,), (0,)), ((), ())), preferred_element_type=F32)


def slot_tables(pair_rec, pair_text, pair_label, here, most):
    record = pair_rec[:, 0]
    count = record.shape[0]
    order = jnp.arange(count, dtype=jnp.int32)
    same = (record[:, None] == record[None, :]).astype(jnp.int32)
    earlier = (order[None, :] < order[:, None]).astype(jnp.int32)
    rank = jnp.sum(same * earlier, axis=1)
    places = jnp.arange(most, dtype=jnp.int32)
    chosen = ((record[None, :] == here) & (rank[None, :] == places[:, None])).astype(jnp.int32)
    valid = jnp.sum(chosen, axis=1)
    slot_text = jnp.sum(chosen * pair_text[None, :], axis=1)
    sign = jnp.sum(chosen * (2 * pair_label[None, :] - 1), axis=1)
    return (valid, slot_text, sign)


def pair_terms(score, valid, sign, tokens):
    margin = -sign * (TEMP * score + BIAS)
    loss_part = valid * jax.nn.softplus(margin)
    grad_cos = -LOSS_SCALE * TEMP * valid * sign * jax.nn.sigmoid(margin) / tokens
    return (loss_part, grad_cos)


def general_body(frames, texts, pair_rec, pair_text, pair_label):
    here = lax.axis_index("rec")
    part = lax.axis_index("frame")
    owned, width_rows, width = texts.shape
    tokens = width_rows * lax.axis_size("frame")
    n_text = owned * lax.axis_size("rec")
    valid, slot_text, sign = slot_tables(pair_rec, pair_text, pair_label, here, MOST)
    valid_f = valid.astype(jnp.float32)
    sign_f = sign.astype(jnp.float32)
    picks = (
        (slot_text[:, None] == jnp.arange(n_text, dtype=jnp.int32)[None, :]) & (valid[:, None] > 0)
    ).astype(jnp.bfloat16)
    local = jnp.einsum(
        "jc,cgx->jgx",
        picks,
        lax.all_gather(texts, "rec", axis=0, tiled=True),
        preferred_element_type=jnp.float32,
    ).astype(jnp.bfloat16)
    query_vectors = lax.all_gather(local, "frame", axis=1, tiled=True)
    upstream_signal = frames[0]
    logit_scale = width ** (-0.5)
    pair_scores = (
        jnp.einsum(
            "ype,je->ypj", query_vectors, upstream_signal, preferred_element_type=jnp.float32
        )
        * logit_scale
    )
    local_max = jnp.max(pair_scores, axis=2)
    row_max = lax.pmax(local_max, "frame")
    expo = jnp.exp(pair_scores - row_max[..., None])
    batch_weights = expo.astype(jnp.bfloat16)
    value_partial = jnp.einsum(
        "pqx,xh->pqh", batch_weights, upstream_signal, preferred_element_type=jnp.float32
    )
    query_f = query_vectors.astype(jnp.float32)
    q_norm = lax.rsqrt(jnp.sum(query_f * query_f, axis=2) + EPS)
    q_unit = query_f * q_norm[..., None]
    context = lax.psum(value_partial, "frame")
    c_norm = lax.rsqrt(jnp.sum(context * context, axis=2) + EPS)
    c_unit = context * c_norm[..., None]
    cos = jnp.sum(q_unit * c_unit, axis=2)
    score = jnp.mean(cos, axis=1)
    loss_part, grad_cos = pair_terms(score, valid_f, sign_f, tokens)
    weight = grad_cos[:, None, None]
    d_context = weight * (q_unit - cos[..., None] * c_unit) * c_norm[..., None]
    direct = weight * (c_unit - cos[..., None] * q_unit) * q_norm[..., None]
    direct_own = lax.dynamic_slice_in_dim(direct, part * width_rows, width_rows, 1)
    context_batch_gradient = d_context.astype(jnp.bfloat16)
    weight_gradient = jnp.einsum(
        "ype,je->ypj", context_batch_gradient, upstream_signal, preferred_element_type=jnp.float32
    )
    score_gradient = (expo * weight_gradient * logit_scale).astype(jnp.bfloat16)
    d_query = lax.psum_scatter(
        jnp.einsum(
            "slf,fd->lsd", score_gradient, upstream_signal, preferred_element_type=jnp.float32
        ),
        "frame",
        scatter_dimension=0,
        tiled=True,
    )
    d_query = d_query + jnp.transpose(direct_own, (1, 0, 2))
    text_term = jnp.einsum(
        "st,lsd->tld", picks.astype(jnp.float32), d_query, precision=lax.Precision.HIGHEST
    )
    grad_texts = lax.psum_scatter(text_term, "rec", scatter_dimension=0, tiled=True).astype(
        jnp.bfloat16
    )
    frame_loss_piece = jnp.einsum(
        "cvm,cvz->mz", score_gradient, query_vectors, preferred_element_type=jnp.float32
    )
    frame_loss_piece = frame_loss_piece + jnp.einsum(
        "cvm,cvz->mz", batch_weights, context_batch_gradient, preferred_element_type=jnp.float32
    )
    grad_frames = frame_loss_piece.astype(jnp.bfloat16)[None]
    loss = lax.psum(jnp.sum(loss_part), "rec")
    return (loss, grad_frames, grad_texts)


def split(line):
    pieces = []
    for _ in range(3):
        piece = line.astype(BF16)
        pieces.append(piece)
        line = line - piece.astype(F32)
    return pieces


def stack(lines, count, width):
    n = lines[0].shape[1]
    place = lax.broadcasted_iota(jnp.int32, (count, n), 0)
    out = jnp.zeros((count, n), F32)
    for at, line in enumerate(lines):
        out = jnp.where(place == at, line, out)
    if n < width:
        out = jnp.concatenate([out, jnp.zeros((count, width - n), F32)], axis=1)
    return out


def unpack(extra, i, n):
    got = [extra[3 * i + j : 3 * i + j + 1, :n] for j in range(3)]
    return (got[0] + got[1]) + got[2]


def diagonal(n):
    r = lax.broadcasted_iota(jnp.int32, (n, n), 0)
    c = lax.broadcasted_iota(jnp.int32, (n, n), 1)
    return r == c


def eye(n):
    return jnp.where(diagonal(n), 1.0, 0.0).astype(BF16)


def to_column(line, one, lanes):
    n = line.shape[1]
    out = None
    for piece in split(line):
        term = nt(one, jnp.broadcast_to(piece, (lanes, n)))
        out = term if out is None else out + term
    return out


def turned(x, one):
    high = x.astype(BF16)
    low = (x - high.astype(F32)).astype(BF16)
    return nt(one, high) + nt(one, low)


def table_kernel(rec_ref, text_ref, label_ref, out_ref, count_ref, *, recs, owned):
    pairs = text_ref.shape[0]
    here = lax.axis_index("rec")
    odd = lax.rem(here, 2)
    near, far, cross = here ^ 1, lax.rem(here + 2 * odd + recs - 1, recs), lax.rem(here + recs // 2, recs)
    n_cand = 3 * owned
    for i in range(4 * n_cand + 1):
        out_ref[i] = 0
    for r in range(recs):
        count_ref[r] = 0

    def pair(p, carry):
        rec, text, label = rec_ref[p], text_ref[p], label_ref[p]
        repeats = lax.fori_loop(
            0, p, lambda q, n: n + jnp.where((rec_ref[q] == rec) & (text_ref[q] == text), 1, 0), 0
        )
        count_ref[rec] = count_ref[rec] + jnp.where(repeats == 0, 1, 0)
        out_ref[4 * n_cand] = jnp.maximum(out_ref[4 * n_cand], count_ref[rec])
        mine = jnp.where(rec == here, 1, 0)
        for w, owner in enumerate((near, far, cross)):
            for j in range(owned):
                hit = mine * jnp.where(text == owner * owned + j, 1, 0)
                c = w * owned + j
                out_ref[c] = out_ref[c] + hit * label
                out_ref[n_cand + c] = out_ref[n_cand + c] + hit * (1 - label)
        return carry

    lax.fori_loop(0, pairs, pair, 0)
    for s in range(n_cand):
        out_ref[3 * n_cand + s] = -1
    at = jnp.int32(0)
    for c in range(n_cand):
        used = (out_ref[c] + out_ref[n_cand + c]) > 0
        out_ref[2 * n_cand + c] = jnp.where(used, at, -1)

        @pl.when(used)
        def _(at=at, c=c):
            out_ref[3 * n_cand + at] = c

        at = at + jnp.where(used, 1, 0)


def select_kernel(table_ref, a_ref, b_ref, c_ref, out_ref, *, slots, n_cand):
    owned, w, _ = a_ref.shape
    for s in range(slots):
        c = table_ref[3 * n_cand + s]
        out_ref[s] = jnp.zeros(out_ref.shape[1:], out_ref.dtype)
        for i, ref in enumerate((a_ref, b_ref, c_ref)):

            @pl.when((c >= i * owned) & (c < (i + 1) * owned))
            def _(ref=ref, i=i, s=s, c=c):
                out_ref[s] = ref[c - i * owned]


def prepare_kernel(f_ref, out_ref):
    out_ref[...] = nt(eye(f_ref.shape[1]), f_ref[...]).astype(BF16)


def forward_kernel(f_ref, ft_ref, *refs, unit, first, group, scale):
    q_refs, (out_ref, weights_ref, top_ref, q_out_ref, q_ref) = refs[:group], refs[group:]
    me = lax.axis_index("frame")
    held, w, width = q_refs[0].shape
    slot = first + (me ^ unit)
    rows = group * w
    for j in range(group):
        q_ref[me ^ j] = q_refs[j][jnp.minimum(slot, held - 1)].astype(F32)
    q = q_ref[...].reshape(rows, width).astype(BF16)
    q_out_ref[...] = q
    s = nt(f_ref[...], q) * scale
    top = jnp.max(s, axis=0, keepdims=True)
    weights = jnp.exp(s - top)
    weights_ref[...] = weights
    top_ref[...] = top
    out_ref[:rows] = turned(nn(ft_ref[...], weights.astype(BF16)), eye(rows))
    out_ref[rows:] = stack([top], LINES, width)


def token_kernel(table_ref, q_ref, *refs, first, group, tokens, n_cand):
    in_refs, (out_ref, direct_ref) = refs[:group], refs[group:]
    rows, width = q_ref.shape
    one = eye(rows)
    tops = [ref[rows : rows + 1, :rows] for ref in in_refs]
    m = functools.reduce(jnp.maximum, tops)
    context = jnp.zeros((rows, width), F32)
    for top, ref in zip(tops, in_refs):
        share = to_column(jnp.exp(top - m), one, 128)
        context = context + jnp.concatenate([share] * (width // 128), axis=1) * ref[:rows]
    q = q_ref[...].astype(F32)
    q_norm = lax.rsqrt(jnp.sum(q * q, axis=1, keepdims=True) + EPS)
    c_norm = lax.rsqrt(jnp.sum(context * context, axis=1, keepdims=True) + EPS)
    q_unit, c_unit = q * q_norm, context * c_norm
    cos = jnp.sum(q_unit * c_unit, axis=1, keepdims=True)
    score = jnp.sum(cos, axis=0, keepdims=True) / tokens
    logit = TEMP * score + BIAS
    slot = first + lax.axis_index("frame")
    c = jnp.where(slot < n_cand, table_ref[3 * n_cand + jnp.minimum(slot, n_cand - 1)], -1)
    used = jnp.where(c >= 0, 1, 0)
    pos = (used * table_ref[jnp.maximum(c, 0)]).astype(F32)
    neg = (used * table_ref[n_cand + jnp.maximum(c, 0)]).astype(F32)
    tail = jnp.log1p(jnp.exp(-jnp.abs(logit)))
    loss = pos * (jnp.maximum(-logit, 0.0) + tail) + neg * (jnp.maximum(logit, 0.0) + tail)
    grad_pos = (-LOSS_SCALE * TEMP / tokens) * jax.nn.sigmoid(-logit)
    grad_neg = (LOSS_SCALE * TEMP / tokens) * jax.nn.sigmoid(logit)
    side = q_unit - cos * c_unit
    d_pos = (grad_pos * side * c_norm).astype(BF16).astype(F32)
    d_neg = (grad_neg * side * c_norm).astype(BF16).astype(F32)
    out_ref[:rows] = (pos * d_pos + neg * d_neg).astype(BF16)
    extra = split(m) + split(jnp.broadcast_to(loss, (1, rows)))
    out_ref[rows:] = stack([x.astype(F32) for x in extra], EXTRA, width).astype(BF16)
    direct_ref[...] = (pos * grad_pos + neg * grad_neg) * (c_unit - cos * q_unit) * q_norm


def backward_kernel(f_ref, ft_ref, weights_ref, top_ref, d_ref, *refs, unit, group, scale):
    if unit == 0:
        direct_ref, refs = refs[0], refs[1:]
    dq_ref, ds_ref, w_ref = refs
    width = f_ref.shape[1]
    rows = top_ref.shape[1]
    m = unpack(d_ref[rows:].astype(F32), 0, rows)
    weights = weights_ref[...] * jnp.exp(top_ref[...] - m)
    w_ref[...] = weights.astype(BF16)
    ds = (weights * nt(f_ref[...], d_ref[:rows]) * scale).astype(BF16)
    ds_ref[...] = ds
    dqt = nn(ft_ref[...], ds)
    dq = turned(dqt, eye(rows)) + direct_ref[...] if unit == 0 else nt(eye(rows), dqt.astype(BF16))
    dq_ref[...] = dq.reshape(group, rows // group, width)


def spread_kernel(*refs, units, group):
    in_refs, out_refs = refs[:units], refs[units:]
    me = lax.axis_index("frame")
    for i in range(units):
        slot = (i // group) * group + (me ^ (i % group))
        for j, ref in enumerate(out_refs):
            if units == group:
                ref[slot] = in_refs[i][me ^ j].astype(ref.dtype)
            else:

                @pl.when(slot < ref.shape[0])
                def _(ref=ref, i=i, j=j, slot=slot):
                    ref[slot] = in_refs[i][me ^ j].astype(ref.dtype)


def frames_kernel(*refs, units, last):
    ds_refs, q_refs, w_refs, d_refs = [refs[k * units : (k + 1) * units] for k in range(4)]
    rest = refs[4 * units :]
    out_ref = rest[-1]
    rows = q_refs[0].shape[0]
    total = None if len(rest) == 1 else rest[0][...]
    for i in range(units):
        term = nn(ds_refs[i][...], q_refs[i][...]) + nn(w_refs[i][...], d_refs[i][:rows])
        total = term if total is None else total + term
    if last:
        out_ref[0] = total.astype(BF16)
    else:
        out_ref[...] = total


def finish_kernel(table_ref, *refs, n_cand):
    in_refs, outs = refs[:-3], refs[-3:]
    owned = n_cand // 3
    for c in range(n_cand):
        s = table_ref[2 * n_cand + c]
        ref, j = outs[c // owned], c % owned
        at = jnp.maximum(s, 0)
        total = functools.reduce(jnp.add, [x[at].astype(F32) for x in in_refs])
        ref[j] = jnp.where(s >= 0, total, 0.0).astype(ref.dtype)


def call(kernel, name, out_shape, in_specs, *args, scratch=(), flops=0, nbytes=1 << 20, vmem=16):
    many = isinstance(out_shape, (list, tuple))
    return pl.pallas_call(
        kernel,
        name=name,
        out_shape=out_shape,
        in_specs=in_specs,
        out_specs=[VMEM] * len(out_shape) if many else VMEM,
        scratch_shapes=list(scratch),
        compiler_params=pltpu.CompilerParams(vmem_limit_bytes=vmem << 20),
        cost_estimate=pl.CostEstimate(flops=flops, bytes_accessed=nbytes, transcendentals=0),
    )(*args)


def permute(x, recs, group, move, sends=None):
    pairs = []
    for r in range(recs):
        for f in range(group):
            to_r, to_f = move(r, f)
            if sends is None or sends(f, to_f):
                pairs.append((r * group + f, to_r * group + to_f))
    return lax.ppermute(x, AXES, pairs)


def near_of(r, recs):
    return r ^ 1


def far_of(r, recs):
    return (r - 1) % recs if r % 2 == 0 else (r + 1) % recs


def cross_of(r, recs):
    return (r + recs // 2) % recs


def slot_body(slots, frames, ft, near, far, cross, table, *, tokens, recs, group):
    owned, w, width = near.shape
    n_cand = 3 * owned
    rows = group * w
    depth = frames.shape[1]
    f = frames[0]
    scale = width ** (-0.5)
    rounds = -(-slots // group)
    units = rounds * group
    cost = 2 * rows * depth * width
    shape = jax.ShapeDtypeStruct
    xor = [lambda r, g, j=j: (r, g ^ j) for j in range(group)]
    order = [3, 1, 2, 0]

    q = call(
        functools.partial(select_kernel, slots=slots, n_cand=n_cand),
        "select",
        shape((slots, w, width), BF16),
        [SMEM, VMEM, VMEM, VMEM],
        table, near, far, cross,
    )
    qs = [q] + [permute(q, recs, group, xor[j]) for j in range(1, group)]
    made, sent = {}, {}
    for r in range(rounds):
        for i in order:
            made[r, i] = call(
                functools.partial(forward_kernel, unit=i, first=r * group, group=group, scale=scale),
                f"forward{r}{i}",
                [
                    shape((rows + LINES, width), F32),
                    shape((depth, rows), F32),
                    shape((1, rows), F32),
                    shape((rows, width), BF16),
                ],
                [VMEM] * (2 + group),
                f, ft, *qs,
                scratch=[pltpu.VMEM((group, w, width), F32)],
                flops=2 * cost,
            )
            sent[r, i] = made[r, i][0]
            if i:
                sent[r, i] = permute(
                    sent[r, i], recs, group, xor[i], lambda a, b, r=r: r * group + b < slots
                )
    ds, directs = {}, {}
    for r in range(rounds):
        d, directs[r] = call(
            functools.partial(token_kernel, first=r * group, group=group, tokens=tokens, n_cand=n_cand),
            f"tokens{r}",
            [shape((rows + EXTRA, width), BF16), shape((rows, width), F32)],
            [SMEM] + [VMEM] * (1 + group),
            table, made[r, 0][3], *[sent[r, i] for i in range(group)],
        )
        for i in order:
            ds[r, i] = d
            if i:
                ds[r, i] = permute(d, recs, group, xor[i], lambda a, b, r=r: r * group + a < slots)
    back = {}
    for r in range(rounds):
        for i in order:
            back[r, i] = call(
                functools.partial(backward_kernel, unit=i, group=group, scale=scale),
                f"backward{r}{i}",
                [shape((group, w, width), F32), shape((depth, rows), BF16), shape((depth, rows), BF16)],
                [VMEM] * (6 if i == 0 else 5),
                f, ft, made[r, i][1], made[r, i][2], ds[r, i], *([directs[r]] if i == 0 else []),
                flops=2 * cost,
            )
    keys = [(r, i) for r in range(rounds) for i in range(group)]
    dqs = call(
        functools.partial(spread_kernel, units=units, group=group),
        "spread",
        [shape((slots, w, width), BF16)] * group,
        [VMEM] * units,
        *[back[k][0] for k in keys],
    )
    dqs = [dqs[0]] + [permute(dqs[j], recs, group, xor[j]) for j in range(1, group)]

    total, half = None, units // 2
    for n, some in enumerate((keys[:half], keys[half:])):
        args = [back[k][1] for k in some] + [made[k][3] for k in some]
        args += [back[k][2] for k in some] + [ds[k] for k in some]
        args += [] if total is None else [total]
        total = call(
            functools.partial(frames_kernel, units=half, last=n == 1),
            f"frames{n}",
            shape(frames.shape, BF16) if n else shape(frames.shape[1:], F32),
            [VMEM] * len(args),
            *args,
            flops=2 * half * cost,
        )
    loss = 0
    for k in keys:
        loss = loss + jnp.sum(ds[k][rows + 3 : rows + 6, :128].astype(F32), axis=0, keepdims=True)
    step = 1
    while step < recs:
        loss = loss + permute(loss, recs, group, lambda r, g, k=step: (r ^ k, g))
        step *= 2
    home = call(
        functools.partial(finish_kernel, n_cand=n_cand),
        "finish",
        [shape((owned, w, width), BF16)] * 3,
        [SMEM] + [VMEM] * group,
        table, *dqs,
    )
    texts = 0
    for x, where in zip(home, (near_of, far_of, cross_of)):
        texts = texts + permute(x, recs, group, lambda r, g: (where(r, recs), g)).astype(F32)
    return loss[0, 0], total, texts.astype(BF16)


def body(frames, texts, pair_rec, pair_text, pair_label):
    recs, group = lax.axis_size("rec"), lax.axis_size("frame")
    owned, w, width = texts.shape
    if group != 4 or w % 8 or recs < 4 or recs & (recs - 1) or 3 * owned > 2 * group:
        return general_body(frames, texts, pair_rec, pair_text, pair_label)
    near, far, cross = [
        permute(texts, recs, group, lambda r, g, to=to: (to(r, recs), g)) for to in (near_of, far_of, cross_of)
    ]
    n_cand = 3 * owned
    table = pl.pallas_call(
        functools.partial(table_kernel, recs=recs, owned=owned),
        name="table",
        out_shape=jax.ShapeDtypeStruct((4 * n_cand + 1,), jnp.int32),
        in_specs=[SMEM] * 3,
        out_specs=SMEM,
        scratch_shapes=[pltpu.SMEM((recs,), jnp.int32)],
    )(pair_rec[:, 0], pair_text, pair_label)
    ft = call(
        prepare_kernel, "prepare", jax.ShapeDtypeStruct((width, frames.shape[1]), BF16), [VMEM], frames[0]
    )
    run = functools.partial(slot_body, tokens=w * group, recs=recs, group=group)
    args = (frames, ft, near, far, cross, table)
    return lax.cond(
        table[4 * n_cand] <= group, functools.partial(run, group), functools.partial(run, n_cand), *args
    )


def solution(mesh):
    return jax.shard_map(
        body,
        mesh=mesh,
        in_specs=(P("rec", "frame", None), P("rec", "frame", None), P(), P(), P()),
        out_specs=(P(), P("rec", "frame", None), P("rec", "frame", None)),
        check_vma=False,
    )
```

```python
import functools

import jax
import jax.numpy as jnp
from jax import lax
from jax.experimental import pallas as pl
from jax.experimental.pallas import tpu as pltpu
from jax.sharding import PartitionSpec as P

MOST = 6
EPS = 1e-06
TEMP = 10.0
BIAS = -1.0
LOSS_SCALE = 2048.0

F32 = jnp.float32
BF16 = jnp.bfloat16
EXTRA = 16
LINES = 8
AXES = ("rec", "frame")
VMEM = pl.BlockSpec(memory_space=pltpu.VMEM)
SMEM = pl.BlockSpec(memory_space=pltpu.SMEM)


def nt(a, b):
    return lax.dot_general(a, b, (((1,), (1,)), ((), ())), preferred_element_type=F32)


def nn(a, b):
    return lax.dot_general(a, b, (((1,), (0,)), ((), ())), preferred_element_type=F32)


def slot_tables(pair_rec, pair_text, pair_label, here, most):
    record = pair_rec[:, 0]
    count = record.shape[0]
    order = jnp.arange(count, dtype=jnp.int32)
    same = (record[:, None] == record[None, :]).astype(jnp.int32)
    earlier = (order[None, :] < order[:, None]).astype(jnp.int32)
    rank = jnp.sum(same * earlier, axis=1)
    places = jnp.arange(most, dtype=jnp.int32)
    chosen = ((record[None, :] == here) & (rank[None, :] == places[:, None])).astype(jnp.int32)
    valid = jnp.sum(chosen, axis=1)
    slot_text = jnp.sum(chosen * pair_text[None, :], axis=1)
    sign = jnp.sum(chosen * (2 * pair_label[None, :] - 1), axis=1)
    return (valid, slot_text, sign)


def pair_terms(score, valid, sign, tokens):
    margin = -sign * (TEMP * score + BIAS)
    loss_part = valid * jax.nn.softplus(margin)
    grad_cos = -LOSS_SCALE * TEMP * valid * sign * jax.nn.sigmoid(margin) / tokens
    return (loss_part, grad_cos)


def general_body(frames, texts, pair_rec, pair_text, pair_label):
    here = lax.axis_index("rec")
    part = lax.axis_index("frame")
    owned, width_rows, width = texts.shape
    tokens = width_rows * lax.axis_size("frame")
    n_text = owned * lax.axis_size("rec")
    valid, slot_text, sign = slot_tables(pair_rec, pair_text, pair_label, here, MOST)
    valid_f = valid.astype(jnp.float32)
    sign_f = sign.astype(jnp.float32)
    picks = (
        (slot_text[:, None] == jnp.arange(n_text, dtype=jnp.int32)[None, :]) & (valid[:, None] > 0)
    ).astype(jnp.bfloat16)
    local = jnp.einsum(
        "jc,cgx->jgx",
        picks,
        lax.all_gather(texts, "rec", axis=0, tiled=True),
        preferred_element_type=jnp.float32,
    ).astype(jnp.bfloat16)
    query_vectors = lax.all_gather(local, "frame", axis=1, tiled=True)
    upstream_signal = frames[0]
    logit_scale = width ** (-0.5)
    pair_scores = (
        jnp.einsum(
            "ype,je->ypj", query_vectors, upstream_signal, preferred_element_type=jnp.float32
        )
        * logit_scale
    )
    local_max = jnp.max(pair_scores, axis=2)
    row_max = lax.pmax(local_max, "frame")
    expo = jnp.exp(pair_scores - row_max[..., None])
    batch_weights = expo.astype(jnp.bfloat16)
    value_partial = jnp.einsum(
        "pqx,xh->pqh", batch_weights, upstream_signal, preferred_element_type=jnp.float32
    )
    query_f = query_vectors.astype(jnp.float32)
    q_norm = lax.rsqrt(jnp.sum(query_f * query_f, axis=2) + EPS)
    q_unit = query_f * q_norm[..., None]
    context = lax.psum(value_partial, "frame")
    c_norm = lax.rsqrt(jnp.sum(context * context, axis=2) + EPS)
    c_unit = context * c_norm[..., None]
    cos = jnp.sum(q_unit * c_unit, axis=2)
    score = jnp.mean(cos, axis=1)
    loss_part, grad_cos = pair_terms(score, valid_f, sign_f, tokens)
    weight = grad_cos[:, None, None]
    d_context = weight * (q_unit - cos[..., None] * c_unit) * c_norm[..., None]
    direct = weight * (c_unit - cos[..., None] * q_unit) * q_norm[..., None]
    direct_own = lax.dynamic_slice_in_dim(direct, part * width_rows, width_rows, 1)
    context_batch_gradient = d_context.astype(jnp.bfloat16)
    weight_gradient = jnp.einsum(
        "ype,je->ypj", context_batch_gradient, upstream_signal, preferred_element_type=jnp.float32
    )
    score_gradient = (expo * weight_gradient * logit_scale).astype(jnp.bfloat16)
    d_query = lax.psum_scatter(
        jnp.einsum(
            "slf,fd->lsd", score_gradient, upstream_signal, preferred_element_type=jnp.float32
        ),
        "frame",
        scatter_dimension=0,
        tiled=True,
    )
    d_query = d_query + jnp.transpose(direct_own, (1, 0, 2))
    text_term = jnp.einsum(
        "st,lsd->tld", picks.astype(jnp.float32), d_query, precision=lax.Precision.HIGHEST
    )
    grad_texts = lax.psum_scatter(text_term, "rec", scatter_dimension=0, tiled=True).astype(
        jnp.bfloat16
    )
    frame_loss_piece = jnp.einsum(
        "cvm,cvz->mz", score_gradient, query_vectors, preferred_element_type=jnp.float32
    )
    frame_loss_piece = frame_loss_piece + jnp.einsum(
        "cvm,cvz->mz", batch_weights, context_batch_gradient, preferred_element_type=jnp.float32
    )
    grad_frames = frame_loss_piece.astype(jnp.bfloat16)[None]
    loss = lax.psum(jnp.sum(loss_part), "rec")
    return (loss, grad_frames, grad_texts)


def split(line):
    pieces = []
    for _ in range(3):
        piece = line.astype(BF16)
        pieces.append(piece)
        line = line - piece.astype(F32)
    return pieces


def stack(lines, count, width):
    n = lines[0].shape[1]
    place = lax.broadcasted_iota(jnp.int32, (count, n), 0)
    out = jnp.zeros((count, n), F32)
    for at, line in enumerate(lines):
        out = jnp.where(place == at, line, out)
    if n < width:
        out = jnp.concatenate([out, jnp.zeros((count, width - n), F32)], axis=1)
    return out


def unpack(extra, i, n):
    got = [extra[3 * i + j : 3 * i + j + 1, :n] for j in range(3)]
    return (got[0] + got[1]) + got[2]


def diagonal(n):
    r = lax.broadcasted_iota(jnp.int32, (n, n), 0)
    c = lax.broadcasted_iota(jnp.int32, (n, n), 1)
    return r == c


def eye(n):
    return jnp.where(diagonal(n), 1.0, 0.0).astype(BF16)


def to_column(line, one, lanes):
    n = line.shape[1]
    out = None
    for piece in split(line):
        term = nt(one, jnp.broadcast_to(piece, (lanes, n)))
        out = term if out is None else out + term
    return out


def turned(x, one):
    high = x.astype(BF16)
    low = (x - high.astype(F32)).astype(BF16)
    return nt(one, high) + nt(one, low)


def table_kernel(rec_ref, text_ref, label_ref, out_ref, seen_ref, count_ref, *, recs, owned):
    here = lax.axis_index("rec")
    odd = lax.rem(here, 2)
    far, cross = lax.rem(here + 2 * odd + recs - 1, recs), lax.rem(here + recs // 2, recs)
    n_cand = 3 * owned
    for i in range(2 * n_cand):
        out_ref[i] = 0
    for r in range(recs):
        seen_ref[r] = 0
        count_ref[r] = 0

    def pair(p, most):
        rec, text, label = rec_ref[p], text_ref[p], label_ref[p]
        seen, bit = seen_ref[rec], lax.shift_left(jnp.int32(1), text)
        n = count_ref[rec] + jnp.where((seen & bit) == 0, 1, 0)
        seen_ref[rec] = seen | bit
        count_ref[rec] = n
        owner = lax.div(text, owned)
        which = jnp.where(owner == far, 1, jnp.where(owner == cross, 2, 0))
        at = which * owned + text - owner * owned + (1 - label) * n_cand
        at = jnp.where(rec == here, at, 4 * n_cand + 1)
        out_ref[at] = out_ref[at] + 1
        return jnp.maximum(most, n)

    out_ref[4 * n_cand + 1] = 0
    out_ref[4 * n_cand] = lax.fori_loop(0, text_ref.shape[0], pair, jnp.int32(0))
    for s in range(n_cand):
        out_ref[3 * n_cand + s] = -1
    at = jnp.int32(0)
    for c in range(n_cand):
        used = (out_ref[c] + out_ref[n_cand + c]) > 0
        out_ref[2 * n_cand + c] = jnp.where(used, at, -1)

        @pl.when(used)
        def _(at=at, c=c):
            out_ref[3 * n_cand + at] = c

        at = at + jnp.where(used, 1, 0)


def select_kernel(table_ref, a_ref, b_ref, c_ref, out_ref, *, slots, n_cand):
    owned, w, _ = a_ref.shape
    for s in range(slots):
        c = table_ref[3 * n_cand + s]
        out_ref[s] = jnp.zeros(out_ref.shape[1:], out_ref.dtype)
        for i, ref in enumerate((a_ref, b_ref, c_ref)):

            @pl.when((c >= i * owned) & (c < (i + 1) * owned))
            def _(ref=ref, i=i, s=s, c=c):
                out_ref[s] = ref[c - i * owned]


def prepare_kernel(f_ref, out_ref):
    out_ref[...] = nt(eye(f_ref.shape[1]), f_ref[...]).astype(BF16)


def forward_kernel(f_ref, ft_ref, *refs, unit, first, group, scale):
    q_refs, (out_ref, weights_ref, top_ref, q_out_ref, q_ref) = refs[:group], refs[group:]
    me = lax.axis_index("frame")
    held, w, width = q_refs[0].shape
    slot = first + (me ^ unit)
    rows = group * w
    for j in range(group):
        q_ref[me ^ j] = q_refs[j][jnp.minimum(slot, held - 1)].astype(F32)
    q = q_ref[...].reshape(rows, width).astype(BF16)
    q_out_ref[...] = q
    s = nt(f_ref[...], q) * scale
    top = jnp.max(s, axis=0, keepdims=True)
    weights = jnp.exp(s - top)
    weights_ref[...] = weights
    top_ref[...] = top
    out_ref[:rows] = turned(nn(ft_ref[...], weights.astype(BF16)), eye(rows))
    out_ref[rows:] = stack([top], LINES, width)


def token_kernel(table_ref, q_ref, *refs, first, group, tokens, n_cand):
    in_refs, (out_ref, direct_ref) = refs[:group], refs[group:]
    rows, width = q_ref.shape
    one = eye(rows)
    tops = [ref[rows : rows + 1, :rows] for ref in in_refs]
    m = functools.reduce(jnp.maximum, tops)
    context = jnp.zeros((rows, width), F32)
    for top, ref in zip(tops, in_refs):
        share = to_column(jnp.exp(top - m), one, 128)
        context = context + jnp.concatenate([share] * (width // 128), axis=1) * ref[:rows]
    q = q_ref[...].astype(F32)
    q_norm = lax.rsqrt(jnp.sum(q * q, axis=1, keepdims=True) + EPS)
    c_norm = lax.rsqrt(jnp.sum(context * context, axis=1, keepdims=True) + EPS)
    q_unit, c_unit = q * q_norm, context * c_norm
    cos = jnp.sum(q_unit * c_unit, axis=1, keepdims=True)
    score = jnp.sum(cos, axis=0, keepdims=True) / tokens
    logit = TEMP * score + BIAS
    slot = first + lax.axis_index("frame")
    c = jnp.where(slot < n_cand, table_ref[3 * n_cand + jnp.minimum(slot, n_cand - 1)], -1)
    used = jnp.where(c >= 0, 1, 0)
    pos = (used * table_ref[jnp.maximum(c, 0)]).astype(F32)
    neg = (used * table_ref[n_cand + jnp.maximum(c, 0)]).astype(F32)
    tail = jnp.log1p(jnp.exp(-jnp.abs(logit)))
    loss = pos * (jnp.maximum(-logit, 0.0) + tail) + neg * (jnp.maximum(logit, 0.0) + tail)
    grad_pos = (-LOSS_SCALE * TEMP / tokens) * jax.nn.sigmoid(-logit)
    grad_neg = (LOSS_SCALE * TEMP / tokens) * jax.nn.sigmoid(logit)
    side = q_unit - cos * c_unit
    d_pos = (grad_pos * side * c_norm).astype(BF16).astype(F32)
    d_neg = (grad_neg * side * c_norm).astype(BF16).astype(F32)
    out_ref[:rows] = (pos * d_pos + neg * d_neg).astype(BF16)
    extra = split(m) + split(jnp.broadcast_to(loss, (1, rows)))
    out_ref[rows:] = stack([x.astype(F32) for x in extra], EXTRA, width).astype(BF16)
    direct_ref[...] = (pos * grad_pos + neg * grad_neg) * (c_unit - cos * q_unit) * q_norm


def backward_kernel(f_ref, ft_ref, weights_ref, top_ref, d_ref, *refs, unit, group, scale):
    if unit == 0:
        direct_ref, refs = refs[0], refs[1:]
    dq_ref, ds_ref, w_ref = refs
    width = f_ref.shape[1]
    rows = top_ref.shape[1]
    m = unpack(d_ref[rows:].astype(F32), 0, rows)
    weights = weights_ref[...] * jnp.exp(top_ref[...] - m)
    w_ref[...] = weights.astype(BF16)
    ds = (weights * nt(f_ref[...], d_ref[:rows]) * scale).astype(BF16)
    ds_ref[...] = ds
    dqt = nn(ft_ref[...], ds)
    dq = turned(dqt, eye(rows)) + direct_ref[...] if unit == 0 else nt(eye(rows), dqt.astype(BF16))
    dq_ref[...] = dq.reshape(group, rows // group, width)


def spread_kernel(*refs, units, group):
    in_refs, out_refs = refs[:units], refs[units:]
    me = lax.axis_index("frame")
    for i in range(units):
        slot = (i // group) * group + (me ^ (i % group))
        for j, ref in enumerate(out_refs):
            if units == group:
                ref[slot] = in_refs[i][me ^ j].astype(ref.dtype)
            else:

                @pl.when(slot < ref.shape[0])
                def _(ref=ref, i=i, j=j, slot=slot):
                    ref[slot] = in_refs[i][me ^ j].astype(ref.dtype)


def frames_kernel(*refs, units, last):
    ds_refs, q_refs, w_refs, d_refs = [refs[k * units : (k + 1) * units] for k in range(4)]
    rest = refs[4 * units :]
    out_ref = rest[-1]
    rows = q_refs[0].shape[0]
    total = None if len(rest) == 1 else rest[0][...]
    for i in range(units):
        term = nn(ds_refs[i][...], q_refs[i][...]) + nn(w_refs[i][...], d_refs[i][:rows])
        total = term if total is None else total + term
    if last:
        out_ref[0] = total.astype(BF16)
    else:
        out_ref[...] = total


def finish_kernel(table_ref, loss_ref, *refs, n_cand):
    in_refs, outs = refs[:-3], refs[-3:]
    owned = n_cand // 3
    w, width = in_refs[0].shape[1:]
    for c in range(n_cand):
        s = table_ref[2 * n_cand + c]
        k, j = c // owned, c % owned
        at = jnp.maximum(s, 0)
        total = functools.reduce(jnp.add, [x[at].astype(F32) for x in in_refs])
        total = jnp.where(s >= 0, total, 0.0).astype(BF16)
        if k < 2:
            outs[k][j] = total
        else:
            outs[k][j * w : (j + 1) * w] = total
    pieces = [x.astype(F32) for x in split(loss_ref[...])]
    outs[2][owned * w :] = stack(pieces, EXTRA, width).astype(BF16)


def close_kernel(loss_ref, near_ref, far_ref, cross_ref, out_ref, total_ref):
    owned, w, _ = near_ref.shape
    for j in range(owned):
        total = near_ref[j].astype(F32) + far_ref[j].astype(F32)
        out_ref[j] = (total + cross_ref[j * w : (j + 1) * w].astype(F32)).astype(BF16)
    total_ref[...] = loss_ref[...] + unpack(cross_ref[owned * w :].astype(F32), 0, total_ref.shape[1])


def call(kernel, name, out_shape, in_specs, *args, scratch=(), flops=0, nbytes=1 << 20, vmem=16):
    many = isinstance(out_shape, (list, tuple))
    return pl.pallas_call(
        kernel,
        name=name,
        out_shape=out_shape,
        in_specs=in_specs,
        out_specs=[VMEM] * len(out_shape) if many else VMEM,
        scratch_shapes=list(scratch),
        compiler_params=pltpu.CompilerParams(vmem_limit_bytes=vmem << 20),
        cost_estimate=pl.CostEstimate(flops=flops, bytes_accessed=nbytes, transcendentals=0),
    )(*args)


def permute(x, recs, group, move, sends=None):
    pairs = []
    for r in range(recs):
        for f in range(group):
            to_r, to_f = move(r, f)
            if sends is None or sends(f, to_f):
                pairs.append((r * group + f, to_r * group + to_f))
    return lax.ppermute(x, AXES, pairs)


def near_of(r, recs):
    return r ^ 1


def far_of(r, recs):
    return (r - 1) % recs if r % 2 == 0 else (r + 1) % recs


def cross_of(r, recs):
    return (r + recs // 2) % recs


def slot_body(slots, frames, near, far, cross, table, *, tokens, recs, group):
    owned, w, width = near.shape
    n_cand = 3 * owned
    rows = group * w
    depth = frames.shape[1]
    f = frames[0]
    scale = width ** (-0.5)
    rounds = -(-slots // group)
    units = rounds * group
    cost = 2 * rows * depth * width
    shape = jax.ShapeDtypeStruct
    xor = [lambda r, g, j=j: (r, g ^ j) for j in range(group)]
    order = [3, 1, 2, 0]

    q = call(
        functools.partial(select_kernel, slots=slots, n_cand=n_cand),
        "select",
        shape((slots, w, width), BF16),
        [SMEM, VMEM, VMEM, VMEM],
        table, near, far, cross,
    )
    qs = [q] + [permute(q, recs, group, xor[j]) for j in range(1, group)]
    ft = call(prepare_kernel, "prepare", shape((width, depth), BF16), [VMEM], f, flops=cost)
    made, sent = {}, {}
    for r in range(rounds):
        for i in order:
            made[r, i] = call(
                functools.partial(forward_kernel, unit=i, first=r * group, group=group, scale=scale),
                f"forward{r}{i}",
                [
                    shape((rows + LINES, width), F32),
                    shape((depth, rows), F32),
                    shape((1, rows), F32),
                    shape((rows, width), BF16),
                ],
                [VMEM] * (2 + group),
                f, ft, *qs,
                scratch=[pltpu.VMEM((group, w, width), F32)],
                flops=2 * cost,
            )
            sent[r, i] = made[r, i][0]
            if i:
                sent[r, i] = permute(
                    sent[r, i], recs, group, xor[i], lambda a, b, r=r: r * group + b < slots
                )
    ds, directs = {}, {}
    for r in range(rounds):
        d, directs[r] = call(
            functools.partial(token_kernel, first=r * group, group=group, tokens=tokens, n_cand=n_cand),
            f"tokens{r}",
            [shape((rows + EXTRA, width), BF16), shape((rows, width), F32)],
            [SMEM] + [VMEM] * (1 + group),
            table, made[r, 0][3], *[sent[r, i] for i in range(group)],
        )
        for i in order:
            ds[r, i] = d
            if i:
                ds[r, i] = permute(d, recs, group, xor[i], lambda a, b, r=r: r * group + a < slots)
    back = {}
    for r in range(rounds):
        for i in order:
            back[r, i] = call(
                functools.partial(backward_kernel, unit=i, group=group, scale=scale),
                f"backward{r}{i}",
                [shape((group, w, width), F32), shape((depth, rows), BF16), shape((depth, rows), BF16)],
                [VMEM] * (6 if i == 0 else 5),
                f, ft, made[r, i][1], made[r, i][2], ds[r, i], *([directs[r]] if i == 0 else []),
                flops=2 * cost,
            )
    keys = [(r, i) for r in range(rounds) for i in range(group)]
    dqs = call(
        functools.partial(spread_kernel, units=units, group=group),
        "spread",
        [shape((slots, w, width), BF16)] * group,
        [VMEM] * units,
        *[back[k][0] for k in keys],
    )

    loss = 0
    for k in keys:
        loss = loss + jnp.sum(ds[k][rows + 3 : rows + 6, :128].astype(F32), axis=0, keepdims=True)
    *dqs, loss = lax.optimization_barrier((*dqs, loss))
    dqs = [dqs[0]] + [permute(dqs[j], recs, group, xor[j]) for j in range(1, group)]
    step, total, half = 1, None, units // 2
    for n, some in enumerate((keys[:half], keys[half:])):
        if step < recs // 2:
            other = permute(loss, recs, group, lambda r, g, k=step: (r ^ k, g))
        args = [back[k][1] for k in some] + [made[k][3] for k in some]
        args += [back[k][2] for k in some] + [ds[k] for k in some]
        args += [] if total is None else [total]
        total = call(
            functools.partial(frames_kernel, units=half, last=n == 1),
            f"frames{n}",
            shape(frames.shape, BF16) if n else shape(frames.shape[1:], F32),
            [VMEM] * len(args),
            *args,
            flops=2 * half * cost,
        )
        if step < recs // 2:
            total, other = lax.optimization_barrier((total, other))
            loss = loss + other
            step *= 2
    while step < recs // 2:
        loss = loss + permute(loss, recs, group, lambda r, g, k=step: (r ^ k, g))
        step *= 2
    dqs = list(lax.optimization_barrier((total, *dqs)))
    total, dqs = dqs[0], dqs[1:]
    home = call(
        functools.partial(finish_kernel, n_cand=n_cand),
        "finish",
        [shape((owned, w, width), BF16)] * 2 + [shape((owned * w + EXTRA, width), BF16)],
        [SMEM] + [VMEM] * (1 + group),
        table, loss, *dqs,
    )
    got = []
    for x, where in zip(home, (near_of, far_of, cross_of)):
        got.append(permute(x, recs, group, lambda r, g: (where(r, recs), g)))
    texts, loss = call(
        close_kernel,
        "close",
        [shape((owned, w, width), BF16), shape((1, 128), F32)],
        [VMEM] * 4,
        loss, *got,
    )
    return loss[0, 0], total, texts


def body(frames, texts, pair_rec, pair_text, pair_label):
    recs, group = lax.axis_size("rec"), lax.axis_size("frame")
    owned, w, width = texts.shape
    if group != 4 or w % 8 or recs < 4 or recs & (recs - 1) or 3 * owned > 2 * group or owned * recs > 32:
        return general_body(frames, texts, pair_rec, pair_text, pair_label)
    near, far, cross = [
        permute(texts, recs, group, lambda r, g, to=to: (to(r, recs), g)) for to in (near_of, far_of, cross_of)
    ]
    n_cand = 3 * owned
    table = pl.pallas_call(
        functools.partial(table_kernel, recs=recs, owned=owned),
        name="table",
        out_shape=jax.ShapeDtypeStruct((4 * n_cand + 2,), jnp.int32),
        in_specs=[SMEM] * 3,
        out_specs=SMEM,
        scratch_shapes=[pltpu.SMEM((recs,), jnp.int32)] * 2,
    )(pair_rec[:, 0], pair_text, pair_label)
    run = functools.partial(slot_body, tokens=w * group, recs=recs, group=group)
    args = (frames, near, far, cross, table)
    return lax.cond(
        table[4 * n_cand] <= group, functools.partial(run, group), functools.partial(run, n_cand), *args
    )


def solution(mesh):
    return jax.shard_map(
        body,
        mesh=mesh,
        in_specs=(P("rec", "frame", None), P("rec", "frame", None), P(), P(), P()),
        out_specs=(P(), P("rec", "frame", None), P("rec", "frame", None)),
        check_vma=False,
    )
```

```python
import functools

import jax
import jax.numpy as jnp
from jax import lax
from jax.experimental import pallas as pl
from jax.experimental.pallas import tpu as pltpu
from jax.sharding import PartitionSpec as P

MOST = 6
EPS = 1e-06
TEMP = 10.0
BIAS = -1.0
LOSS_SCALE = 2048.0

F32 = jnp.float32
BF16 = jnp.bfloat16
EXTRA = 16
LINES = 8
AXES = ("rec", "frame")
VMEM = pl.BlockSpec(memory_space=pltpu.VMEM)
SMEM = pl.BlockSpec(memory_space=pltpu.SMEM)


def nt(a, b):
    return lax.dot_general(a, b, (((1,), (1,)), ((), ())), preferred_element_type=F32)


def nn(a, b):
    return lax.dot_general(a, b, (((1,), (0,)), ((), ())), preferred_element_type=F32)


def slot_tables(pair_rec, pair_text, pair_label, here, most):
    record = pair_rec[:, 0]
    count = record.shape[0]
    order = jnp.arange(count, dtype=jnp.int32)
    same = (record[:, None] == record[None, :]).astype(jnp.int32)
    earlier = (order[None, :] < order[:, None]).astype(jnp.int32)
    rank = jnp.sum(same * earlier, axis=1)
    places = jnp.arange(most, dtype=jnp.int32)
    chosen = ((record[None, :] == here) & (rank[None, :] == places[:, None])).astype(jnp.int32)
    valid = jnp.sum(chosen, axis=1)
    slot_text = jnp.sum(chosen * pair_text[None, :], axis=1)
    sign = jnp.sum(chosen * (2 * pair_label[None, :] - 1), axis=1)
    return (valid, slot_text, sign)


def pair_terms(score, valid, sign, tokens):
    margin = -sign * (TEMP * score + BIAS)
    loss_part = valid * jax.nn.softplus(margin)
    grad_cos = -LOSS_SCALE * TEMP * valid * sign * jax.nn.sigmoid(margin) / tokens
    return (loss_part, grad_cos)


def general_body(frames, texts, pair_rec, pair_text, pair_label):
    here = lax.axis_index("rec")
    part = lax.axis_index("frame")
    owned, width_rows, width = texts.shape
    tokens = width_rows * lax.axis_size("frame")
    n_text = owned * lax.axis_size("rec")
    valid, slot_text, sign = slot_tables(pair_rec, pair_text, pair_label, here, MOST)
    valid_f = valid.astype(jnp.float32)
    sign_f = sign.astype(jnp.float32)
    picks = (
        (slot_text[:, None] == jnp.arange(n_text, dtype=jnp.int32)[None, :]) & (valid[:, None] > 0)
    ).astype(jnp.bfloat16)
    local = jnp.einsum(
        "jc,cgx->jgx",
        picks,
        lax.all_gather(texts, "rec", axis=0, tiled=True),
        preferred_element_type=jnp.float32,
    ).astype(jnp.bfloat16)
    query_vectors = lax.all_gather(local, "frame", axis=1, tiled=True)
    upstream_signal = frames[0]
    logit_scale = width ** (-0.5)
    pair_scores = (
        jnp.einsum(
            "ype,je->ypj", query_vectors, upstream_signal, preferred_element_type=jnp.float32
        )
        * logit_scale
    )
    local_max = jnp.max(pair_scores, axis=2)
    row_max = lax.pmax(local_max, "frame")
    expo = jnp.exp(pair_scores - row_max[..., None])
    batch_weights = expo.astype(jnp.bfloat16)
    value_partial = jnp.einsum(
        "pqx,xh->pqh", batch_weights, upstream_signal, preferred_element_type=jnp.float32
    )
    query_f = query_vectors.astype(jnp.float32)
    q_norm = lax.rsqrt(jnp.sum(query_f * query_f, axis=2) + EPS)
    q_unit = query_f * q_norm[..., None]
    context = lax.psum(value_partial, "frame")
    c_norm = lax.rsqrt(jnp.sum(context * context, axis=2) + EPS)
    c_unit = context * c_norm[..., None]
    cos = jnp.sum(q_unit * c_unit, axis=2)
    score = jnp.mean(cos, axis=1)
    loss_part, grad_cos = pair_terms(score, valid_f, sign_f, tokens)
    weight = grad_cos[:, None, None]
    d_context = weight * (q_unit - cos[..., None] * c_unit) * c_norm[..., None]
    direct = weight * (c_unit - cos[..., None] * q_unit) * q_norm[..., None]
    direct_own = lax.dynamic_slice_in_dim(direct, part * width_rows, width_rows, 1)
    context_batch_gradient = d_context.astype(jnp.bfloat16)
    weight_gradient = jnp.einsum(
        "ype,je->ypj", context_batch_gradient, upstream_signal, preferred_element_type=jnp.float32
    )
    score_gradient = (expo * weight_gradient * logit_scale).astype(jnp.bfloat16)
    d_query = lax.psum_scatter(
        jnp.einsum(
            "slf,fd->lsd", score_gradient, upstream_signal, preferred_element_type=jnp.float32
        ),
        "frame",
        scatter_dimension=0,
        tiled=True,
    )
    d_query = d_query + jnp.transpose(direct_own, (1, 0, 2))
    text_term = jnp.einsum(
        "st,lsd->tld", picks.astype(jnp.float32), d_query, precision=lax.Precision.HIGHEST
    )
    grad_texts = lax.psum_scatter(text_term, "rec", scatter_dimension=0, tiled=True).astype(
        jnp.bfloat16
    )
    frame_loss_piece = jnp.einsum(
        "cvm,cvz->mz", score_gradient, query_vectors, preferred_element_type=jnp.float32
    )
    frame_loss_piece = frame_loss_piece + jnp.einsum(
        "cvm,cvz->mz", batch_weights, context_batch_gradient, preferred_element_type=jnp.float32
    )
    grad_frames = frame_loss_piece.astype(jnp.bfloat16)[None]
    loss = lax.psum(jnp.sum(loss_part), "rec")
    return (loss, grad_frames, grad_texts)


def split(line):
    pieces = []
    for _ in range(3):
        piece = line.astype(BF16)
        pieces.append(piece)
        line = line - piece.astype(F32)
    return pieces


def stack(lines, count, width):
    n = lines[0].shape[1]
    place = lax.broadcasted_iota(jnp.int32, (count, n), 0)
    out = jnp.zeros((count, n), F32)
    for at, line in enumerate(lines):
        out = jnp.where(place == at, line, out)
    if n < width:
        out = jnp.concatenate([out, jnp.zeros((count, width - n), F32)], axis=1)
    return out


def unpack(extra, i, n):
    got = [extra[3 * i + j : 3 * i + j + 1, :n] for j in range(3)]
    return (got[0] + got[1]) + got[2]


def diagonal(n):
    r = lax.broadcasted_iota(jnp.int32, (n, n), 0)
    c = lax.broadcasted_iota(jnp.int32, (n, n), 1)
    return r == c


def eye(n):
    return jnp.where(diagonal(n), 1.0, 0.0).astype(BF16)


def to_column(line, one, lanes):
    n = line.shape[1]
    out = None
    for piece in split(line):
        term = nt(one, jnp.broadcast_to(piece, (lanes, n)))
        out = term if out is None else out + term
    return out


def turned(x, one):
    high = x.astype(BF16)
    low = (x - high.astype(F32)).astype(BF16)
    return nt(one, high) + nt(one, low)


def table_kernel(rec_ref, text_ref, label_ref, out_ref, seen_ref, count_ref, *, recs, owned):
    here = lax.axis_index("rec")
    odd = lax.rem(here, 2)
    far, cross = lax.rem(here + 2 * odd + recs - 1, recs), lax.rem(here + recs // 2, recs)
    n_cand = 3 * owned
    for i in range(2 * n_cand):
        out_ref[i] = 0
    for r in range(recs):
        seen_ref[r] = 0
        count_ref[r] = 0

    def pair(p, most):
        rec, text, label = rec_ref[p], text_ref[p], label_ref[p]
        seen, bit = seen_ref[rec], lax.shift_left(jnp.int32(1), text)
        n = count_ref[rec] + jnp.where((seen & bit) == 0, 1, 0)
        seen_ref[rec] = seen | bit
        count_ref[rec] = n
        owner = lax.div(text, owned)
        which = jnp.where(owner == far, 1, jnp.where(owner == cross, 2, 0))
        at = which * owned + text - owner * owned + (1 - label) * n_cand
        at = jnp.where(rec == here, at, 4 * n_cand + 1)
        out_ref[at] = out_ref[at] + 1
        return jnp.maximum(most, n)

    out_ref[4 * n_cand + 1] = 0
    out_ref[4 * n_cand] = lax.fori_loop(0, text_ref.shape[0], pair, jnp.int32(0))
    for s in range(n_cand):
        out_ref[3 * n_cand + s] = -1
    at = jnp.int32(0)
    for c in range(n_cand):
        used = (out_ref[c] + out_ref[n_cand + c]) > 0
        out_ref[2 * n_cand + c] = jnp.where(used, at, -1)

        @pl.when(used)
        def _(at=at, c=c):
            out_ref[3 * n_cand + at] = c

        at = at + jnp.where(used, 1, 0)


def select_kernel(table_ref, a_ref, b_ref, c_ref, *out_refs, n_cand, order):
    owned = a_ref.shape[0]
    me = lax.axis_index("frame")
    half = out_refs[0].shape[0]
    for at, out_ref in enumerate(out_refs):
        for i in range(half):
            s = i if len(out_refs) == 1 else me ^ (at // 2) ^ order[at % 2 * half + i]
            c = table_ref[3 * n_cand + s]
            out_ref[i] = jnp.zeros(out_ref.shape[1:], out_ref.dtype)
            for k, ref in enumerate((a_ref, b_ref, c_ref)):

                @pl.when((c >= k * owned) & (c < (k + 1) * owned))
                def _(ref=ref, k=k, i=i, c=c, out_ref=out_ref):
                    out_ref[i] = ref[c - k * owned]


def prepare_kernel(f_ref, out_ref):
    out_ref[...] = nt(eye(f_ref.shape[1]), f_ref[...]).astype(BF16)


def forward_kernel(f_ref, ft_ref, *refs, unit, first, group, scale, place):
    q_refs, (out_ref, weights_ref, top_ref, q_out_ref, q_ref) = refs[:group], refs[group:]
    me = lax.axis_index("frame")
    held, w, width = q_refs[0].shape
    slot = first + (me ^ unit)
    rows = group * w
    for j in range(group):
        if place is None:
            block = q_refs[j][jnp.minimum(slot, held - 1)].astype(F32)
            q_ref[me ^ j] = jnp.where(slot < held, block, 0.0)
        else:
            q_ref[me ^ j] = q_refs[j][place].astype(F32)
    q = q_ref[...].reshape(rows, width).astype(BF16)
    q_out_ref[...] = q
    s = nt(f_ref[...], q) * scale
    top = jnp.max(s, axis=0, keepdims=True)
    weights = jnp.exp(s - top)
    weights_ref[...] = weights
    top_ref[...] = top
    out_ref[:rows] = turned(nn(ft_ref[...], weights.astype(BF16)), eye(rows))
    out_ref[rows:] = stack([top], LINES, width)


def token_kernel(table_ref, q_ref, *refs, first, group, tokens, n_cand):
    in_refs, (out_ref, direct_ref) = refs[:group], refs[group:]
    rows, width = q_ref.shape
    one = eye(rows)
    tops = [ref[rows : rows + 1, :rows] for ref in in_refs]
    m = functools.reduce(jnp.maximum, tops)
    context = jnp.zeros((rows, width), F32)
    for top, ref in zip(tops, in_refs):
        share = to_column(jnp.exp(top - m), one, 128)
        context = context + jnp.concatenate([share] * (width // 128), axis=1) * ref[:rows]
    q = q_ref[...].astype(F32)
    q_norm = lax.rsqrt(jnp.sum(q * q, axis=1, keepdims=True) + EPS)
    c_norm = lax.rsqrt(jnp.sum(context * context, axis=1, keepdims=True) + EPS)
    q_unit, c_unit = q * q_norm, context * c_norm
    cos = jnp.sum(q_unit * c_unit, axis=1, keepdims=True)
    score = jnp.sum(cos, axis=0, keepdims=True) / tokens
    logit = TEMP * score + BIAS
    slot = first + lax.axis_index("frame")
    c = jnp.where(slot < n_cand, table_ref[3 * n_cand + jnp.minimum(slot, n_cand - 1)], -1)
    used = jnp.where(c >= 0, 1, 0)
    pos = (used * table_ref[jnp.maximum(c, 0)]).astype(F32)
    neg = (used * table_ref[n_cand + jnp.maximum(c, 0)]).astype(F32)
    tail = jnp.log1p(jnp.exp(-jnp.abs(logit)))
    loss = pos * (jnp.maximum(-logit, 0.0) + tail) + neg * (jnp.maximum(logit, 0.0) + tail)
    grad_pos = (-LOSS_SCALE * TEMP / tokens) * jax.nn.sigmoid(-logit)
    grad_neg = (LOSS_SCALE * TEMP / tokens) * jax.nn.sigmoid(logit)
    side = q_unit - cos * c_unit
    d_pos = (grad_pos * side * c_norm).astype(BF16).astype(F32)
    d_neg = (grad_neg * side * c_norm).astype(BF16).astype(F32)
    out_ref[:rows] = (pos * d_pos + neg * d_neg).astype(BF16)
    extra = split(m) + split(jnp.broadcast_to(loss, (1, rows)))
    out_ref[rows:] = stack([x.astype(F32) for x in extra], EXTRA, width).astype(BF16)
    direct_ref[...] = (pos * grad_pos + neg * grad_neg) * (c_unit - cos * q_unit) * q_norm


def backward_kernel(f_ref, ft_ref, weights_ref, top_ref, d_ref, *refs, unit, group, scale):
    if unit == 0:
        direct_ref, refs = refs[0], refs[1:]
    dq_ref, ds_ref, w_ref = refs
    width = f_ref.shape[1]
    rows = top_ref.shape[1]
    m = unpack(d_ref[rows:].astype(F32), 0, rows)
    weights = weights_ref[...] * jnp.exp(top_ref[...] - m)
    w_ref[...] = weights.astype(BF16)
    ds = (weights * nt(f_ref[...], d_ref[:rows]) * scale).astype(BF16)
    ds_ref[...] = ds
    dqt = nn(ft_ref[...], ds)
    dq = turned(dqt, eye(rows)) + direct_ref[...] if unit == 0 else nt(eye(rows), dqt.astype(BF16))
    dq_ref[...] = dq.reshape(group, rows // group, width)


def spread_kernel(*refs, units, group):
    in_refs, out_refs = refs[:units], refs[units:]
    me = lax.axis_index("frame")
    for i in range(units):
        slot = (i // group) * group + (me ^ (i % group))
        for j, ref in enumerate(out_refs):
            if units == group:
                ref[slot] = in_refs[i][me ^ j].astype(ref.dtype)
            else:

                @pl.when(slot < ref.shape[0])
                def _(ref=ref, i=i, j=j, slot=slot):
                    ref[slot] = in_refs[i][me ^ j].astype(ref.dtype)


def frames_kernel(*refs, units):
    ds_refs, q_refs, w_refs, d_refs = [refs[k * units : (k + 1) * units] for k in range(4)]
    rows = q_refs[0].shape[0]
    total = None
    for i in range(units):
        term = nn(ds_refs[i][...], q_refs[i][...]) + nn(w_refs[i][...], d_refs[i][:rows])
        total = term if total is None else total + term
    refs[-1][...] = total


def last_frames_kernel(*refs, units):
    ds_refs, q_refs, w_refs, d_refs = [refs[k * units : (k + 1) * units] for k in range(4)]
    before_ref, out_ref, held_ref, sems = refs[4 * units :]
    rows, depth = q_refs[0].shape[0], before_ref.shape[0]
    blocks = sems.shape[0]
    size = depth // blocks
    copies = []
    for b in range(blocks):
        at = pl.ds(b * size, size)
        total = before_ref[at]
        for i in range(units):
            total = total + nn(ds_refs[i][at], q_refs[i][...]) + nn(w_refs[i][at], d_refs[i][:rows])
        held_ref[at] = total.astype(BF16)
        copies.append(pltpu.make_async_copy(held_ref.at[at], out_ref.at[0, at], sems.at[b]))
        copies[-1].start()
    for copy in copies:
        copy.wait()


def finish_kernel(table_ref, loss_ref, *refs, n_cand):
    in_refs, outs = refs[:-3], refs[-3:]
    owned = n_cand // 3
    w, width = in_refs[0].shape[1:]
    for c in range(n_cand):
        s = table_ref[2 * n_cand + c]
        k, j = c // owned, c % owned
        at = jnp.maximum(s, 0)
        total = functools.reduce(jnp.add, [x[at].astype(F32) for x in in_refs])
        total = jnp.where(s >= 0, total, 0.0).astype(BF16)
        if k < 2:
            outs[k][j] = total
        else:
            outs[k][j * w : (j + 1) * w] = total
    pieces = [x.astype(F32) for x in split(loss_ref[...])]
    outs[2][owned * w :] = stack(pieces, EXTRA, width).astype(BF16)


def close_kernel(loss_ref, near_ref, far_ref, cross_ref, out_ref, total_ref):
    owned, w, _ = near_ref.shape
    for j in range(owned):
        total = near_ref[j].astype(F32) + far_ref[j].astype(F32)
        out_ref[j] = (total + cross_ref[j * w : (j + 1) * w].astype(F32)).astype(BF16)
    total_ref[...] = loss_ref[...] + unpack(cross_ref[owned * w :].astype(F32), 0, total_ref.shape[1])


def call(kernel, out_shape, in_specs, *args, scratch=(), flops=0, nbytes=1 << 20, vmem=16, out_specs=None):
    many = isinstance(out_shape, (list, tuple))
    return pl.pallas_call(
        kernel,
        out_shape=out_shape,
        in_specs=in_specs,
        out_specs=out_specs or ([VMEM] * len(out_shape) if many else VMEM),
        scratch_shapes=list(scratch),
        compiler_params=pltpu.CompilerParams(vmem_limit_bytes=vmem << 20),
        cost_estimate=pl.CostEstimate(flops=flops, bytes_accessed=nbytes, transcendentals=0),
    )(*args)


def permute(x, recs, group, move, sends=None):
    pairs = []
    for r in range(recs):
        for f in range(group):
            to_r, to_f = move(r, f)
            if sends is None or sends(f, to_f):
                pairs.append((r * group + f, to_r * group + to_f))
    return lax.ppermute(x, AXES, pairs)


def near_of(r, recs):
    return r ^ 1


def far_of(r, recs):
    return (r - 1) % recs if r % 2 == 0 else (r + 1) % recs


def cross_of(r, recs):
    return (r + recs // 2) % recs


def slot_body(slots, frames, near, far, cross, table, *, tokens, recs, group):
    owned, w, width = near.shape
    n_cand = 3 * owned
    rows = group * w
    depth = frames.shape[1]
    f = frames[0]
    scale = width ** (-0.5)
    rounds = -(-slots // group)
    units = rounds * group
    cost = 2 * rows * depth * width
    shape = jax.ShapeDtypeStruct
    xor = [lambda r, g, j=j: (r, g ^ j) for j in range(group)]
    order = [3, 1, 2, 0]

    halves = 2 if slots == group else 1
    q = call(
        functools.partial(select_kernel, n_cand=n_cand, order=order),
        [shape((slots // halves, w, width), BF16)] * (2 * group if halves == 2 else 1),
        [SMEM, VMEM, VMEM, VMEM],
        table, near, far, cross,
    )
    qs = []
    for h in range(halves):
        part = [q[2 * j + h] if halves == 2 else q[0] for j in range(group)]
        qs.append(part[:1] + [permute(part[j], recs, group, xor[j]) for j in range(1, group)])
    ft = call(prepare_kernel, shape((width, depth), BF16), [VMEM], f, flops=cost)
    made, sent = {}, {}
    for r in range(rounds):
        for i in order:
            made[r, i] = call(
                functools.partial(
                    forward_kernel,
                    unit=i,
                    first=r * group,
                    group=group,
                    scale=scale,
                    place=order.index(i) % 2 if halves == 2 else None,
                ),
                [
                    shape((rows + LINES, width), F32),
                    shape((depth, rows), F32),
                    shape((1, rows), F32),
                    shape((rows, width), BF16),
                ],
                [VMEM] * (2 + group),
                f, ft, *qs[order.index(i) // 2 if halves == 2 else 0],
                scratch=[pltpu.VMEM((group, w, width), F32)],
                flops=2 * cost,
            )
            sent[r, i] = made[r, i][0]
            if i:
                sent[r, i] = permute(
                    sent[r, i], recs, group, xor[i], lambda a, b, r=r: r * group + b < slots
                )
    ds, directs = {}, {}
    for r in range(rounds):
        d, directs[r] = call(
            functools.partial(token_kernel, first=r * group, group=group, tokens=tokens, n_cand=n_cand),
            [shape((rows + EXTRA, width), BF16), shape((rows, width), F32)],
            [SMEM] + [VMEM] * (1 + group),
            table, made[r, 0][3], *[sent[r, i] for i in range(group)],
        )
        for i in order:
            ds[r, i] = d
            if i:
                ds[r, i] = permute(d, recs, group, xor[i], lambda a, b, r=r: r * group + a < slots)
    back = {}
    for r in range(rounds):
        for i in order:
            back[r, i] = call(
                functools.partial(backward_kernel, unit=i, group=group, scale=scale),
                [shape((group, w, width), F32), shape((depth, rows), BF16), shape((depth, rows), BF16)],
                [VMEM] * (6 if i == 0 else 5),
                f, ft, made[r, i][1], made[r, i][2], ds[r, i], *([directs[r]] if i == 0 else []),
                flops=2 * cost,
            )
    keys = [(r, i) for r in range(rounds) for i in range(group)]
    dqs = call(
        functools.partial(spread_kernel, units=units, group=group),
        [shape((slots, w, width), BF16)] * group,
        [VMEM] * units,
        *[back[k][0] for k in keys],
    )

    loss = 0
    for k in keys:
        loss = loss + jnp.sum(ds[k][rows + 3 : rows + 6, :128].astype(F32), axis=0, keepdims=True)
    *dqs, loss = lax.optimization_barrier((*dqs, loss))
    dqs = [dqs[0]] + [permute(dqs[j], recs, group, xor[j]) for j in range(1, group)]
    step, total, half = 1, None, units // 2
    for n, some in enumerate((keys[:half], keys[half:])):
        if step < recs // 2:
            other = permute(loss, recs, group, lambda r, g, k=step: (r ^ k, g))
        args = [back[k][1] for k in some] + [made[k][3] for k in some]
        args += [back[k][2] for k in some] + [ds[k] for k in some]
        if n == 0:
            total = call(
                functools.partial(frames_kernel, units=half),
                shape(frames.shape[1:], F32),
                [VMEM] * len(args),
                *args,
                flops=2 * half * cost,
            )
        else:
            blocks = 3 if depth % 384 == 0 else 1
            total = call(
                functools.partial(last_frames_kernel, units=half),
                shape(frames.shape, BF16),
                [VMEM] * (len(args) + 1),
                *args, total,
                out_specs=pl.BlockSpec(memory_space=pltpu.HBM),
                scratch=[pltpu.VMEM((depth, width), BF16), pltpu.SemaphoreType.DMA((blocks,))],
                flops=2 * half * cost,
            )
        if step < recs // 2:
            if n == 0:
                total, other = lax.optimization_barrier((total, other))
            loss = loss + other
            step *= 2
    while step < recs // 2:
        loss = loss + permute(loss, recs, group, lambda r, g, k=step: (r ^ k, g))
        step *= 2
    home = call(
        functools.partial(finish_kernel, n_cand=n_cand),
        [shape((owned, w, width), BF16)] * 2 + [shape((owned * w + EXTRA, width), BF16)],
        [SMEM] + [VMEM] * (1 + group),
        table, loss, *dqs,
    )
    got = []
    for x, where in zip(home, (near_of, far_of, cross_of)):
        got.append(permute(x, recs, group, lambda r, g: (where(r, recs), g)))
    texts, loss = call(
        close_kernel,
        [shape((owned, w, width), BF16), shape((1, 128), F32)],
        [VMEM] * 4,
        loss, *got,
    )
    return loss[0, 0], total, texts


def body(frames, texts, pair_rec, pair_text, pair_label):
    recs, group = lax.axis_size("rec"), lax.axis_size("frame")
    owned, w, _ = texts.shape
    if group != 4 or w % 8 or recs < 4 or recs & (recs - 1) or 3 * owned > 2 * group or owned * recs > 32:
        return general_body(frames, texts, pair_rec, pair_text, pair_label)
    near, far, cross = [
        permute(texts, recs, group, lambda r, g, to=to: (to(r, recs), g)) for to in (near_of, far_of, cross_of)
    ]
    n_cand = 3 * owned
    table = pl.pallas_call(
        functools.partial(table_kernel, recs=recs, owned=owned),
        name="table",
        out_shape=jax.ShapeDtypeStruct((4 * n_cand + 2,), jnp.int32),
        in_specs=[SMEM] * 3,
        out_specs=SMEM,
        scratch_shapes=[pltpu.SMEM((recs,), jnp.int32)] * 2,
    )(pair_rec[:, 0], pair_text, pair_label)

    def run(slots, *args):
        return slot_body(slots, *args, tokens=w * group, recs=recs, group=group)

    args = (frames, near, far, cross, table)
    return lax.cond(
        table[4 * n_cand] <= group, functools.partial(run, group), functools.partial(run, n_cand), *args
    )


def solution(mesh):
    return jax.shard_map(
        body,
        mesh=mesh,
        in_specs=(P("rec", "frame", None), P("rec", "frame", None), P(), P(), P()),
        out_specs=(P(), P("rec", "frame", None), P("rec", "frame", None)),
        check_vma=False,
    )
```

```python
import functools

import jax
import jax.numpy as jnp
from jax import lax
from jax.experimental import pallas as pl
from jax.experimental.pallas import tpu as pltpu
from jax.sharding import PartitionSpec as P

MOST = 6
EPS = 1e-06
TEMP = 10.0
BIAS = -1.0
LOSS_SCALE = 2048.0

F32 = jnp.float32
BF16 = jnp.bfloat16
EXTRA = 16
LINES = 8
AXES = ("rec", "frame")
VMEM = pl.BlockSpec(memory_space=pltpu.VMEM)
SMEM = pl.BlockSpec(memory_space=pltpu.SMEM)


def nt(a, b):
    return lax.dot_general(a, b, (((1,), (1,)), ((), ())), preferred_element_type=F32)


def nn(a, b):
    return lax.dot_general(a, b, (((1,), (0,)), ((), ())), preferred_element_type=F32)


def slot_tables(pair_rec, pair_text, pair_label, here, most):
    record = pair_rec[:, 0]
    count = record.shape[0]
    order = jnp.arange(count, dtype=jnp.int32)
    same = (record[:, None] == record[None, :]).astype(jnp.int32)
    earlier = (order[None, :] < order[:, None]).astype(jnp.int32)
    rank = jnp.sum(same * earlier, axis=1)
    places = jnp.arange(most, dtype=jnp.int32)
    chosen = ((record[None, :] == here) & (rank[None, :] == places[:, None])).astype(jnp.int32)
    valid = jnp.sum(chosen, axis=1)
    slot_text = jnp.sum(chosen * pair_text[None, :], axis=1)
    sign = jnp.sum(chosen * (2 * pair_label[None, :] - 1), axis=1)
    return (valid, slot_text, sign)


def pair_terms(score, valid, sign, tokens):
    margin = -sign * (TEMP * score + BIAS)
    loss_part = valid * jax.nn.softplus(margin)
    grad_cos = -LOSS_SCALE * TEMP * valid * sign * jax.nn.sigmoid(margin) / tokens
    return (loss_part, grad_cos)


def general_body(frames, texts, pair_rec, pair_text, pair_label):
    here = lax.axis_index("rec")
    part = lax.axis_index("frame")
    owned, width_rows, width = texts.shape
    tokens = width_rows * lax.axis_size("frame")
    n_text = owned * lax.axis_size("rec")
    valid, slot_text, sign = slot_tables(pair_rec, pair_text, pair_label, here, MOST)
    valid_f = valid.astype(jnp.float32)
    sign_f = sign.astype(jnp.float32)
    picks = (
        (slot_text[:, None] == jnp.arange(n_text, dtype=jnp.int32)[None, :]) & (valid[:, None] > 0)
    ).astype(jnp.bfloat16)
    local = jnp.einsum(
        "jc,cgx->jgx",
        picks,
        lax.all_gather(texts, "rec", axis=0, tiled=True),
        preferred_element_type=jnp.float32,
    ).astype(jnp.bfloat16)
    query_vectors = lax.all_gather(local, "frame", axis=1, tiled=True)
    upstream_signal = frames[0]
    logit_scale = width ** (-0.5)
    pair_scores = (
        jnp.einsum(
            "ype,je->ypj", query_vectors, upstream_signal, preferred_element_type=jnp.float32
        )
        * logit_scale
    )
    local_max = jnp.max(pair_scores, axis=2)
    row_max = lax.pmax(local_max, "frame")
    expo = jnp.exp(pair_scores - row_max[..., None])
    batch_weights = expo.astype(jnp.bfloat16)
    value_partial = jnp.einsum(
        "pqx,xh->pqh", batch_weights, upstream_signal, preferred_element_type=jnp.float32
    )
    query_f = query_vectors.astype(jnp.float32)
    q_norm = lax.rsqrt(jnp.sum(query_f * query_f, axis=2) + EPS)
    q_unit = query_f * q_norm[..., None]
    context = lax.psum(value_partial, "frame")
    c_norm = lax.rsqrt(jnp.sum(context * context, axis=2) + EPS)
    c_unit = context * c_norm[..., None]
    cos = jnp.sum(q_unit * c_unit, axis=2)
    score = jnp.mean(cos, axis=1)
    loss_part, grad_cos = pair_terms(score, valid_f, sign_f, tokens)
    weight = grad_cos[:, None, None]
    d_context = weight * (q_unit - cos[..., None] * c_unit) * c_norm[..., None]
    direct = weight * (c_unit - cos[..., None] * q_unit) * q_norm[..., None]
    direct_own = lax.dynamic_slice_in_dim(direct, part * width_rows, width_rows, 1)
    context_batch_gradient = d_context.astype(jnp.bfloat16)
    weight_gradient = jnp.einsum(
        "ype,je->ypj", context_batch_gradient, upstream_signal, preferred_element_type=jnp.float32
    )
    score_gradient = (expo * weight_gradient * logit_scale).astype(jnp.bfloat16)
    d_query = lax.psum_scatter(
        jnp.einsum(
            "slf,fd->lsd", score_gradient, upstream_signal, preferred_element_type=jnp.float32
        ),
        "frame",
        scatter_dimension=0,
        tiled=True,
    )
    d_query = d_query + jnp.transpose(direct_own, (1, 0, 2))
    text_term = jnp.einsum(
        "st,lsd->tld", picks.astype(jnp.float32), d_query, precision=lax.Precision.HIGHEST
    )
    grad_texts = lax.psum_scatter(text_term, "rec", scatter_dimension=0, tiled=True).astype(
        jnp.bfloat16
    )
    frame_loss_piece = jnp.einsum(
        "cvm,cvz->mz", score_gradient, query_vectors, preferred_element_type=jnp.float32
    )
    frame_loss_piece = frame_loss_piece + jnp.einsum(
        "cvm,cvz->mz", batch_weights, context_batch_gradient, preferred_element_type=jnp.float32
    )
    grad_frames = frame_loss_piece.astype(jnp.bfloat16)[None]
    loss = lax.psum(jnp.sum(loss_part), "rec")
    return (loss, grad_frames, grad_texts)


def split(line):
    pieces = []
    for _ in range(3):
        piece = line.astype(BF16)
        pieces.append(piece)
        line = line - piece.astype(F32)
    return pieces


def stack(lines, count, width):
    n = lines[0].shape[1]
    place = lax.broadcasted_iota(jnp.int32, (count, n), 0)
    out = jnp.zeros((count, n), F32)
    for at, line in enumerate(lines):
        out = jnp.where(place == at, line, out)
    if n < width:
        out = jnp.concatenate([out, jnp.zeros((count, width - n), F32)], axis=1)
    return out


def unpack(extra, i, n):
    got = [extra[3 * i + j : 3 * i + j + 1, :n] for j in range(3)]
    return (got[0] + got[1]) + got[2]


def diagonal(n):
    r = lax.broadcasted_iota(jnp.int32, (n, n), 0)
    c = lax.broadcasted_iota(jnp.int32, (n, n), 1)
    return r == c


def eye(n):
    return jnp.where(diagonal(n), 1.0, 0.0).astype(BF16)


def to_column(line, one, lanes):
    n = line.shape[1]
    out = None
    for piece in split(line):
        term = nt(one, jnp.broadcast_to(piece, (lanes, n)))
        out = term if out is None else out + term
    return out


def turned(x, one):
    high = x.astype(BF16)
    low = (x - high.astype(F32)).astype(BF16)
    return nt(one, high) + nt(one, low)


def table_kernel(rec_ref, text_ref, label_ref, out_ref, seen_ref, count_ref, *, recs, owned):
    here = lax.axis_index("rec")
    odd = lax.rem(here, 2)
    far, cross = lax.rem(here + 2 * odd + recs - 1, recs), lax.rem(here + recs // 2, recs)
    n_cand = 3 * owned
    for i in range(2 * n_cand):
        out_ref[i] = 0
    for r in range(recs):
        seen_ref[r] = 0
        count_ref[r] = 0

    def pair(p, most):
        rec, text, label = rec_ref[p], text_ref[p], label_ref[p]
        seen, bit = seen_ref[rec], lax.shift_left(jnp.int32(1), text)
        n = count_ref[rec] + jnp.where((seen & bit) == 0, 1, 0)
        seen_ref[rec] = seen | bit
        count_ref[rec] = n
        owner = lax.div(text, owned)
        which = jnp.where(owner == far, 1, jnp.where(owner == cross, 2, 0))
        at = which * owned + text - owner * owned + (1 - label) * n_cand
        at = jnp.where(rec == here, at, 4 * n_cand + 1)
        out_ref[at] = out_ref[at] + 1
        return jnp.maximum(most, n)

    out_ref[4 * n_cand + 1] = 0
    out_ref[4 * n_cand] = lax.fori_loop(0, text_ref.shape[0], pair, jnp.int32(0))
    for s in range(n_cand):
        out_ref[3 * n_cand + s] = -1
    at = jnp.int32(0)
    for c in range(n_cand):
        used = (out_ref[c] + out_ref[n_cand + c]) > 0
        out_ref[2 * n_cand + c] = jnp.where(used, at, -1)

        @pl.when(used)
        def _(at=at, c=c):
            out_ref[3 * n_cand + at] = c

        at = at + jnp.where(used, 1, 0)


def select_kernel(table_ref, a_ref, b_ref, c_ref, out_ref, *, slots, n_cand):
    owned, _, _ = a_ref.shape
    for s in range(slots):
        c = table_ref[3 * n_cand + s]
        out_ref[s] = jnp.zeros(out_ref.shape[1:], out_ref.dtype)
        for i, ref in enumerate((a_ref, b_ref, c_ref)):

            @pl.when((c >= i * owned) & (c < (i + 1) * owned))
            def _(ref=ref, i=i, s=s, c=c):
                out_ref[s] = ref[c - i * owned]


def prepare_kernel(f_ref, out_ref):
    out_ref[...] = nt(eye(f_ref.shape[1]), f_ref[...]).astype(BF16)


def forward_kernel(f_ref, ft_ref, *refs, unit, first, group, scale):
    q_refs, (out_ref, weights_ref, top_ref, q_out_ref, q_ref) = refs[:group], refs[group:]
    me = lax.axis_index("frame")
    held, w, width = q_refs[0].shape
    slot = first + (me ^ unit)
    rows = group * w
    for j in range(group):
        block = q_refs[j][jnp.minimum(slot, held - 1)].astype(F32)
        q_ref[me ^ j] = jnp.where(slot < held, block, 0.0)
    q = q_ref[...].reshape(rows, width).astype(BF16)
    q_out_ref[...] = q
    s = nt(f_ref[...], q) * scale
    top = jnp.max(s, axis=0, keepdims=True)
    weights = jnp.exp(s - top)
    weights_ref[...] = weights
    top_ref[...] = top
    out_ref[:rows] = turned(nn(ft_ref[...], weights.astype(BF16)), eye(rows))
    out_ref[rows:] = stack([top], LINES, width)


def token_kernel(table_ref, q_ref, *refs, first, group, tokens, n_cand):
    in_refs, (out_ref, direct_ref) = refs[:group], refs[group:]
    rows, width = q_ref.shape
    one = eye(rows)
    tops = [ref[rows : rows + 1, :rows] for ref in in_refs]
    m = functools.reduce(jnp.maximum, tops)
    context = jnp.zeros((rows, width), F32)
    for top, ref in zip(tops, in_refs):
        share = to_column(jnp.exp(top - m), one, 128)
        context = context + jnp.concatenate([share] * (width // 128), axis=1) * ref[:rows]
    q = q_ref[...].astype(F32)
    q_norm = lax.rsqrt(jnp.sum(q * q, axis=1, keepdims=True) + EPS)
    c_norm = lax.rsqrt(jnp.sum(context * context, axis=1, keepdims=True) + EPS)
    q_unit, c_unit = q * q_norm, context * c_norm
    cos = jnp.sum(q_unit * c_unit, axis=1, keepdims=True)
    score = jnp.sum(cos, axis=0, keepdims=True) / tokens
    logit = TEMP * score + BIAS
    slot = first + lax.axis_index("frame")
    c = jnp.where(slot < n_cand, table_ref[3 * n_cand + jnp.minimum(slot, n_cand - 1)], -1)
    used = jnp.where(c >= 0, 1, 0)
    pos = (used * table_ref[jnp.maximum(c, 0)]).astype(F32)
    neg = (used * table_ref[n_cand + jnp.maximum(c, 0)]).astype(F32)
    tail = jnp.log1p(jnp.exp(-jnp.abs(logit)))
    loss = pos * (jnp.maximum(-logit, 0.0) + tail) + neg * (jnp.maximum(logit, 0.0) + tail)
    grad_pos = (-LOSS_SCALE * TEMP / tokens) * jax.nn.sigmoid(-logit)
    grad_neg = (LOSS_SCALE * TEMP / tokens) * jax.nn.sigmoid(logit)
    side = q_unit - cos * c_unit
    d_pos = (grad_pos * side * c_norm).astype(BF16).astype(F32)
    d_neg = (grad_neg * side * c_norm).astype(BF16).astype(F32)
    out_ref[:rows] = (pos * d_pos + neg * d_neg).astype(BF16)
    extra = split(m) + split(jnp.broadcast_to(loss, (1, rows)))
    out_ref[rows:] = stack([x.astype(F32) for x in extra], EXTRA, width).astype(BF16)
    direct_ref[...] = (pos * grad_pos + neg * grad_neg) * (c_unit - cos * q_unit) * q_norm


def backward_kernel(f_ref, ft_ref, weights_ref, top_ref, d_ref, *refs, unit, group, scale):
    if unit == 0:
        direct_ref, refs = refs[0], refs[1:]
    dq_ref, ds_ref, w_ref = refs
    width = f_ref.shape[1]
    rows = top_ref.shape[1]
    m = unpack(d_ref[rows:].astype(F32), 0, rows)
    weights = weights_ref[...] * jnp.exp(top_ref[...] - m)
    w_ref[...] = weights.astype(BF16)
    ds = (weights * nt(f_ref[...], d_ref[:rows]) * scale).astype(BF16)
    ds_ref[...] = ds
    dqt = nn(ft_ref[...], ds)
    dq = turned(dqt, eye(rows)) + direct_ref[...] if unit == 0 else nt(eye(rows), dqt.astype(BF16))
    dq_ref[...] = dq.reshape(group, rows // group, width)


def spread_kernel(*refs, units, group):
    in_refs, d_refs, out_refs, loss_ref = refs[:units], refs[units : 2 * units], refs[2 * units : -1], refs[-1]
    me = lax.axis_index("frame")
    rows = d_refs[0].shape[0] - EXTRA
    loss = jnp.zeros(loss_ref.shape, F32)
    for i in range(units):
        loss = loss + unpack(d_refs[i][rows:].astype(F32), 1, loss_ref.shape[1])
        slot = (i // group) * group + (me ^ (i % group))
        for j, ref in enumerate(out_refs):
            if ref.shape[0] == units:
                ref[slot] = in_refs[i][me ^ j].astype(ref.dtype)
            else:

                @pl.when(slot < ref.shape[0])
                def _(ref=ref, i=i, j=j, slot=slot):
                    ref[slot] = in_refs[i][me ^ j].astype(ref.dtype)

    loss_ref[...] = loss


def frames_kernel(*refs, units):
    ds_refs, q_refs, w_refs, d_refs = [refs[k * units : (k + 1) * units] for k in range(4)]
    rows = q_refs[0].shape[0]
    total = None
    for i in range(units):
        term = nn(ds_refs[i][...], q_refs[i][...]) + nn(w_refs[i][...], d_refs[i][:rows])
        total = term if total is None else total + term
    refs[-1][...] = total


def last_frames_kernel(*refs, units):
    ds_refs, q_refs, w_refs, d_refs = [refs[k * units : (k + 1) * units] for k in range(4)]
    before_ref, out_ref, held_ref, sems = refs[4 * units :]
    rows, depth = q_refs[0].shape[0], before_ref.shape[0]
    blocks = sems.shape[0]
    size = depth // blocks
    copies = []
    for b in range(blocks):
        at = pl.ds(b * size, size)
        total = before_ref[at]
        for i in range(units):
            total = total + nn(ds_refs[i][at], q_refs[i][...]) + nn(w_refs[i][at], d_refs[i][:rows])
        held_ref[at] = total.astype(BF16)
        copies.append(pltpu.make_async_copy(held_ref.at[at], out_ref.at[0, at], sems.at[b]))
        copies[-1].start()
    for copy in copies:
        copy.wait()


def finish_kernel(table_ref, pair_ref, across_ref, *refs, n_cand):
    in_refs, outs = refs[:-3], refs[-3:]
    owned = n_cand // 3
    w, width = in_refs[0].shape[1:]
    for c in range(n_cand):
        s = table_ref[2 * n_cand + c]
        j = c % owned
        at = jnp.maximum(s, 0)
        total = functools.reduce(jnp.add, [x[at].astype(F32) for x in in_refs])
        outs[c // owned][j * w : (j + 1) * w] = jnp.where(s >= 0, total, 0.0).astype(BF16)
    for ref, loss_ref in zip(outs, (across_ref, across_ref, pair_ref)):
        pieces = [x.astype(F32) for x in split(loss_ref[...])]
        ref[owned * w :] = stack(pieces, EXTRA, width).astype(BF16)


def close_kernel(pair_ref, near_ref, far_ref, cross_ref, out_ref, total_ref):
    owned, w, _ = out_ref.shape
    loss = pair_ref[...]
    for ref in (near_ref, far_ref, cross_ref):
        loss = loss + unpack(ref[owned * w :].astype(F32), 0, total_ref.shape[1])
    total_ref[...] = loss
    for j in range(owned):
        at = slice(j * w, (j + 1) * w)
        total = near_ref[at].astype(F32) + far_ref[at].astype(F32)
        out_ref[j] = (total + cross_ref[at].astype(F32)).astype(BF16)


def call(kernel, out_shape, in_specs, *args, scratch=(), flops=0, nbytes=1 << 20, vmem=16, out_specs=None):
    many = isinstance(out_shape, (list, tuple))
    return pl.pallas_call(
        kernel,
        out_shape=out_shape,
        in_specs=in_specs,
        out_specs=out_specs or ([VMEM] * len(out_shape) if many else VMEM),
        scratch_shapes=list(scratch),
        compiler_params=pltpu.CompilerParams(vmem_limit_bytes=vmem << 20),
        cost_estimate=pl.CostEstimate(flops=flops, bytes_accessed=nbytes, transcendentals=0),
    )(*args)


def permute(x, recs, group, move, sends=None):
    pairs = []
    for r in range(recs):
        for f in range(group):
            to_r, to_f = move(r, f)
            if sends is None or sends(f, to_f):
                pairs.append((r * group + f, to_r * group + to_f))
    return lax.ppermute(x, AXES, pairs)


def near_of(r, recs):
    return r ^ 1


def far_of(r, recs):
    return (r - 1) % recs if r % 2 == 0 else (r + 1) % recs


def cross_of(r, recs):
    return (r + recs // 2) % recs


def slot_body(slots, frames, near, far, cross, table, *, tokens, recs, group):
    owned, w, width = near.shape
    n_cand = 3 * owned
    rows = group * w
    depth = frames.shape[1]
    f = frames[0]
    scale = width ** (-0.5)
    rounds = -(-slots // group)
    units = rounds * group
    cost = 2 * rows * depth * width
    shape = jax.ShapeDtypeStruct
    xor = [lambda r, g, j=j: (r, g ^ j) for j in range(group)]
    order = [3, 1, 2, 0]

    q = call(
        functools.partial(select_kernel, slots=slots, n_cand=n_cand),
        shape((slots, w, width), BF16),
        [SMEM, VMEM, VMEM, VMEM],
        table, near, far, cross,
    )
    qs = [q] + [permute(q, recs, group, xor[j]) for j in range(1, group)]
    ft = call(prepare_kernel, shape((width, depth), BF16), [VMEM], f, flops=cost)
    made, sent = {}, {}
    for r in range(rounds):
        for i in order:
            made[r, i] = call(
functools.partial(forward_kernel, unit=i, first=r * group, group=group, scale=scale),
                [
                    shape((rows + LINES, width), F32),
                    shape((depth, rows), F32),
                    shape((1, rows), F32),
                    shape((rows, width), BF16),
                ],
                [VMEM] * (2 + group),
                f, ft, *qs,
                scratch=[pltpu.VMEM((group, w, width), F32)],
                flops=2 * cost,
            )
            sent[r, i] = made[r, i][0]
            if i:
                sent[r, i] = permute(
                    sent[r, i], recs, group, xor[i], lambda a, b, r=r: r * group + b < slots
                )
    ds, directs = {}, {}
    for r in range(rounds):
        d, directs[r] = call(
            functools.partial(token_kernel, first=r * group, group=group, tokens=tokens, n_cand=n_cand),
            [shape((rows + EXTRA, width), BF16), shape((rows, width), F32)],
            [SMEM] + [VMEM] * (1 + group),
            table, made[r, 0][3], *[sent[r, i] for i in range(group)],
        )
        for i in order:
            ds[r, i] = d
            if i:
                ds[r, i] = permute(d, recs, group, xor[i], lambda a, b, r=r: r * group + a < slots)
    back = {}
    for r in range(rounds):
        for i in order:
            back[r, i] = call(
                functools.partial(backward_kernel, unit=i, group=group, scale=scale),
                [shape((group, w, width), F32), shape((depth, rows), BF16), shape((depth, rows), BF16)],
                [VMEM] * (6 if i == 0 else 5),
                f, ft, made[r, i][1], made[r, i][2], ds[r, i], *([directs[r]] if i == 0 else []),
                flops=2 * cost,
            )
    keys = [(r, i) for r in range(rounds) for i in range(group)]
    *dqs, loss = call(
        functools.partial(spread_kernel, units=units, group=group),
        [shape((slots, w, width), BF16)] * group + [shape((1, 128), F32)],
        [VMEM] * (2 * units),
        *[back[k][0] for k in keys], *[ds[k] for k in keys],
    )
    dqs = [dqs[0]] + [permute(dqs[j], recs, group, xor[j]) for j in range(1, group)]
    pair = loss + permute(loss, recs, group, lambda r, g: (r ^ 2, g))
    across = loss + permute(loss, recs, group, lambda r, g: (cross_of(r, recs), g))
    total, half = None, units // 2
    for n, some in enumerate((keys[:half], keys[half:])):
        args = [back[k][1] for k in some] + [made[k][3] for k in some]
        args += [back[k][2] for k in some] + [ds[k] for k in some]
        if n == 0:
            total = call(
                functools.partial(frames_kernel, units=half),
                shape(frames.shape[1:], F32),
                [VMEM] * len(args),
                *args,
                flops=2 * half * cost,
            )
        else:
            blocks = 3 if depth % 384 == 0 else 1
            total = call(
                functools.partial(last_frames_kernel, units=half),
                pltpu.HBM(frames.shape, BF16),
                [VMEM] * (len(args) + 1),
                *args, total,
                out_specs=pl.BlockSpec(memory_space=pltpu.HBM),
                scratch=[pltpu.VMEM((depth, width), BF16), pltpu.SemaphoreType.DMA((blocks,))],
                flops=2 * half * cost,
            )
    pair, across, *dqs = lax.optimization_barrier((pair, across, *dqs))
    home = call(
        functools.partial(finish_kernel, n_cand=n_cand),
        [shape((owned * w + EXTRA, width), BF16)] * 3,
        [SMEM] + [VMEM] * (2 + group),
        table, pair, across, *dqs,
    )
    got = []
    for x, where in zip(home, (near_of, far_of, cross_of)):
        got.append(permute(x, recs, group, lambda r, g: (where(r, recs), g)))
    texts, loss = call(
        close_kernel,
        [shape((owned, w, width), BF16), shape((1, 128), F32)],
        [VMEM] * 4,
        pair, *got,
    )
    return loss[0, 0], total, texts


def body(frames, texts, pair_rec, pair_text, pair_label):
    recs, group = lax.axis_size("rec"), lax.axis_size("frame")
    owned, w, _ = texts.shape
    if group != 4 or w % 8 or recs != 8 or 3 * owned > 2 * group or owned * recs > 32:
        return general_body(frames, texts, pair_rec, pair_text, pair_label)
    fetched = []
    for to in (near_of, far_of, cross_of):
        fetched.append(permute(texts, recs, group, lambda r, g: (to(r, recs), g)))
    near, far, cross = fetched
    n_cand = 3 * owned
    table = pl.pallas_call(
        functools.partial(table_kernel, recs=recs, owned=owned),
        name="table",
        out_shape=jax.ShapeDtypeStruct((4 * n_cand + 2,), jnp.int32),
        in_specs=[SMEM] * 3,
        out_specs=SMEM,
        scratch_shapes=[pltpu.SMEM((recs,), jnp.int32)] * 2,
    )(pair_rec[:, 0], pair_text, pair_label)

    def run(slots, *args):
        return slot_body(slots, *args, tokens=w * group, recs=recs, group=group)

    args = (frames, near, far, cross, table)
    return lax.cond(
        table[4 * n_cand] <= group, functools.partial(run, group), functools.partial(run, n_cand), *args
    )


def solution(mesh):
    return jax.shard_map(
        body,
        mesh=mesh,
        in_specs=(P("rec", "frame", None), P("rec", "frame", None), P(), P(), P()),
        out_specs=(P(), P("rec", "frame", None), P("rec", "frame", None)),
        check_vma=False,
    )
```

```python
import functools

import jax
import jax.numpy as jnp
from jax import lax
from jax.experimental import pallas as pl
from jax.experimental.pallas import tpu as pltpu
from jax.sharding import PartitionSpec as P

MOST = 6
EPS = 1e-06
TEMP = 10.0
BIAS = -1.0
LOSS_SCALE = 2048.0

F32 = jnp.float32
BF16 = jnp.bfloat16
EXTRA = 16
LINES = 8
AXES = ("rec", "frame")
VMEM = pl.BlockSpec(memory_space=pltpu.VMEM)
SMEM = pl.BlockSpec(memory_space=pltpu.SMEM)


def nt(a, b):
    return lax.dot_general(a, b, (((1,), (1,)), ((), ())), preferred_element_type=F32)


def nn(a, b):
    return lax.dot_general(a, b, (((1,), (0,)), ((), ())), preferred_element_type=F32)


def slot_tables(pair_rec, pair_text, pair_label, here, most):
    record = pair_rec[:, 0]
    count = record.shape[0]
    order = jnp.arange(count, dtype=jnp.int32)
    same = (record[:, None] == record[None, :]).astype(jnp.int32)
    earlier = (order[None, :] < order[:, None]).astype(jnp.int32)
    rank = jnp.sum(same * earlier, axis=1)
    places = jnp.arange(most, dtype=jnp.int32)
    chosen = ((record[None, :] == here) & (rank[None, :] == places[:, None])).astype(jnp.int32)
    valid = jnp.sum(chosen, axis=1)
    slot_text = jnp.sum(chosen * pair_text[None, :], axis=1)
    sign = jnp.sum(chosen * (2 * pair_label[None, :] - 1), axis=1)
    return (valid, slot_text, sign)


def pair_terms(score, valid, sign, tokens):
    margin = -sign * (TEMP * score + BIAS)
    loss_part = valid * jax.nn.softplus(margin)
    grad_cos = -LOSS_SCALE * TEMP * valid * sign * jax.nn.sigmoid(margin) / tokens
    return (loss_part, grad_cos)


def general_body(frames, texts, pair_rec, pair_text, pair_label):
    here = lax.axis_index("rec")
    part = lax.axis_index("frame")
    owned, width_rows, width = texts.shape
    tokens = width_rows * lax.axis_size("frame")
    n_text = owned * lax.axis_size("rec")
    valid, slot_text, sign = slot_tables(pair_rec, pair_text, pair_label, here, MOST)
    valid_f = valid.astype(jnp.float32)
    sign_f = sign.astype(jnp.float32)
    picks = (
        (slot_text[:, None] == jnp.arange(n_text, dtype=jnp.int32)[None, :]) & (valid[:, None] > 0)
    ).astype(jnp.bfloat16)
    local = jnp.einsum(
        "jc,cgx->jgx",
        picks,
        lax.all_gather(texts, "rec", axis=0, tiled=True),
        preferred_element_type=jnp.float32,
    ).astype(jnp.bfloat16)
    query_vectors = lax.all_gather(local, "frame", axis=1, tiled=True)
    upstream_signal = frames[0]
    logit_scale = width ** (-0.5)
    pair_scores = (
        jnp.einsum(
            "ype,je->ypj", query_vectors, upstream_signal, preferred_element_type=jnp.float32
        )
        * logit_scale
    )
    local_max = jnp.max(pair_scores, axis=2)
    row_max = lax.pmax(local_max, "frame")
    expo = jnp.exp(pair_scores - row_max[..., None])
    batch_weights = expo.astype(jnp.bfloat16)
    value_partial = jnp.einsum(
        "pqx,xh->pqh", batch_weights, upstream_signal, preferred_element_type=jnp.float32
    )
    query_f = query_vectors.astype(jnp.float32)
    q_norm = lax.rsqrt(jnp.sum(query_f * query_f, axis=2) + EPS)
    q_unit = query_f * q_norm[..., None]
    context = lax.psum(value_partial, "frame")
    c_norm = lax.rsqrt(jnp.sum(context * context, axis=2) + EPS)
    c_unit = context * c_norm[..., None]
    cos = jnp.sum(q_unit * c_unit, axis=2)
    score = jnp.mean(cos, axis=1)
    loss_part, grad_cos = pair_terms(score, valid_f, sign_f, tokens)
    weight = grad_cos[:, None, None]
    d_context = weight * (q_unit - cos[..., None] * c_unit) * c_norm[..., None]
    direct = weight * (c_unit - cos[..., None] * q_unit) * q_norm[..., None]
    direct_own = lax.dynamic_slice_in_dim(direct, part * width_rows, width_rows, 1)
    context_batch_gradient = d_context.astype(jnp.bfloat16)
    weight_gradient = jnp.einsum(
        "ype,je->ypj", context_batch_gradient, upstream_signal, preferred_element_type=jnp.float32
    )
    score_gradient = (expo * weight_gradient * logit_scale).astype(jnp.bfloat16)
    d_query = lax.psum_scatter(
        jnp.einsum(
            "slf,fd->lsd", score_gradient, upstream_signal, preferred_element_type=jnp.float32
        ),
        "frame",
        scatter_dimension=0,
        tiled=True,
    )
    d_query = d_query + jnp.transpose(direct_own, (1, 0, 2))
    text_term = jnp.einsum(
        "st,lsd->tld", picks.astype(jnp.float32), d_query, precision=lax.Precision.HIGHEST
    )
    grad_texts = lax.psum_scatter(text_term, "rec", scatter_dimension=0, tiled=True).astype(
        jnp.bfloat16
    )
    frame_loss_piece = jnp.einsum(
        "cvm,cvz->mz", score_gradient, query_vectors, preferred_element_type=jnp.float32
    )
    frame_loss_piece = frame_loss_piece + jnp.einsum(
        "cvm,cvz->mz", batch_weights, context_batch_gradient, preferred_element_type=jnp.float32
    )
    grad_frames = frame_loss_piece.astype(jnp.bfloat16)[None]
    loss = lax.psum(jnp.sum(loss_part), "rec")
    return (loss, grad_frames, grad_texts)


def split(line):
    pieces = []
    for _ in range(3):
        piece = line.astype(BF16)
        pieces.append(piece)
        line = line - piece.astype(F32)
    return pieces


def stack(lines, count, width):
    n = lines[0].shape[1]
    place = lax.broadcasted_iota(jnp.int32, (count, n), 0)
    out = jnp.zeros((count, n), F32)
    for at, line in enumerate(lines):
        out = jnp.where(place == at, line, out)
    if n < width:
        out = jnp.concatenate([out, jnp.zeros((count, width - n), F32)], axis=1)
    return out


def unpack(extra, i, n):
    got = [extra[3 * i + j : 3 * i + j + 1, :n] for j in range(3)]
    return (got[0] + got[1]) + got[2]


def diagonal(n):
    r = lax.broadcasted_iota(jnp.int32, (n, n), 0)
    c = lax.broadcasted_iota(jnp.int32, (n, n), 1)
    return r == c


def eye(n):
    return jnp.where(diagonal(n), 1.0, 0.0).astype(BF16)


def to_column(line, one, lanes):
    n = line.shape[1]
    out = None
    for piece in split(line):
        term = nt(one, jnp.broadcast_to(piece, (lanes, n)))
        out = term if out is None else out + term
    return out


def turned(x, one):
    high = x.astype(BF16)
    low = (x - high.astype(F32)).astype(BF16)
    return nt(one, high) + nt(one, low)


def table_kernel(rec_ref, text_ref, label_ref, out_ref, seen_ref, count_ref, *, recs, owned):
    here = lax.axis_index("rec")
    odd = lax.rem(here, 2)
    far, cross = lax.rem(here + 2 * odd + recs - 1, recs), lax.rem(here + recs // 2, recs)
    n_cand = 3 * owned
    for i in range(2 * n_cand):
        out_ref[i] = 0
    for r in range(recs):
        seen_ref[r] = 0
        count_ref[r] = 0

    def pair(p, most):
        rec, text, label = rec_ref[p], text_ref[p], label_ref[p]
        seen, bit = seen_ref[rec], lax.shift_left(jnp.int32(1), text)
        n = count_ref[rec] + jnp.where((seen & bit) == 0, 1, 0)
        seen_ref[rec] = seen | bit
        count_ref[rec] = n
        owner = lax.div(text, owned)
        which = jnp.where(owner == far, 1, jnp.where(owner == cross, 2, 0))
        at = which * owned + text - owner * owned + (1 - label) * n_cand
        at = jnp.where(rec == here, at, 4 * n_cand + 1)
        out_ref[at] = out_ref[at] + 1
        return jnp.maximum(most, n)

    out_ref[4 * n_cand + 1] = 0
    out_ref[4 * n_cand] = lax.fori_loop(0, text_ref.shape[0], pair, jnp.int32(0))
    for s in range(n_cand):
        out_ref[3 * n_cand + s] = -1
    at = jnp.int32(0)
    for c in range(n_cand):
        used = (out_ref[c] + out_ref[n_cand + c]) > 0
        out_ref[2 * n_cand + c] = jnp.where(used, at, -1)

        @pl.when(used)
        def _(at=at, c=c):
            out_ref[3 * n_cand + at] = c

        at = at + jnp.where(used, 1, 0)


def select_kernel(table_ref, a_ref, b_ref, c_ref, out_ref, *, slots, n_cand):
    owned, _, _ = a_ref.shape
    for s in range(slots):
        c = table_ref[3 * n_cand + s]
        out_ref[s] = jnp.zeros(out_ref.shape[1:], out_ref.dtype)
        for i, ref in enumerate((a_ref, b_ref, c_ref)):

            @pl.when((c >= i * owned) & (c < (i + 1) * owned))
            def _(ref=ref, i=i, s=s, c=c):
                out_ref[s] = ref[c - i * owned]


def prepare_kernel(f_ref, out_ref):
    out_ref[...] = nt(eye(f_ref.shape[1]), f_ref[...]).astype(BF16)


def forward_kernel(f_ref, ft_ref, *refs, unit, first, group, scale):
    q_refs, (out_ref, weights_ref, top_ref, q_out_ref, q_ref) = refs[:group], refs[group:]
    me = lax.axis_index("frame")
    held, w, width = q_refs[0].shape
    slot = first + (me ^ unit)
    rows = group * w
    for j in range(group):
        block = q_refs[j][jnp.minimum(slot, held - 1)].astype(F32)
        q_ref[me ^ j] = jnp.where(slot < held, block, 0.0)
    q = q_ref[...].reshape(rows, width).astype(BF16)
    q_out_ref[...] = q
    s = nt(f_ref[...], q) * scale
    top = jnp.max(s, axis=0, keepdims=True)
    weights = jnp.exp(s - top)
    weights_ref[...] = weights
    top_ref[...] = top
    out_ref[:rows] = turned(nn(ft_ref[...], weights.astype(BF16)), eye(rows))
    out_ref[rows:] = stack([top], LINES, width)


def token_kernel(table_ref, q_ref, *refs, first, group, tokens, n_cand):
    in_refs, (out_ref, direct_ref) = refs[:group], refs[group:]
    rows, width = q_ref.shape
    one = eye(rows)
    tops = [ref[rows : rows + 1, :rows] for ref in in_refs]
    m = functools.reduce(jnp.maximum, tops)
    context = jnp.zeros((rows, width), F32)
    for top, ref in zip(tops, in_refs):
        share = to_column(jnp.exp(top - m), one, 128)
        context = context + jnp.concatenate([share] * (width // 128), axis=1) * ref[:rows]
    q = q_ref[...].astype(F32)
    q_norm = lax.rsqrt(jnp.sum(q * q, axis=1, keepdims=True) + EPS)
    c_norm = lax.rsqrt(jnp.sum(context * context, axis=1, keepdims=True) + EPS)
    q_unit, c_unit = q * q_norm, context * c_norm
    cos = jnp.sum(q_unit * c_unit, axis=1, keepdims=True)
    score = jnp.sum(cos, axis=0, keepdims=True) / tokens
    logit = TEMP * score + BIAS
    slot = first + lax.axis_index("frame")
    c = jnp.where(slot < n_cand, table_ref[3 * n_cand + jnp.minimum(slot, n_cand - 1)], -1)
    used = jnp.where(c >= 0, 1, 0)
    pos = (used * table_ref[jnp.maximum(c, 0)]).astype(F32)
    neg = (used * table_ref[n_cand + jnp.maximum(c, 0)]).astype(F32)
    tail = jnp.log1p(jnp.exp(-jnp.abs(logit)))
    loss = pos * (jnp.maximum(-logit, 0.0) + tail) + neg * (jnp.maximum(logit, 0.0) + tail)
    grad_pos = (-LOSS_SCALE * TEMP / tokens) * jax.nn.sigmoid(-logit)
    grad_neg = (LOSS_SCALE * TEMP / tokens) * jax.nn.sigmoid(logit)
    side = q_unit - cos * c_unit
    d_pos = (grad_pos * side * c_norm).astype(BF16).astype(F32)
    d_neg = (grad_neg * side * c_norm).astype(BF16).astype(F32)
    out_ref[:rows] = (pos * d_pos + neg * d_neg).astype(BF16)
    extra = split(m) + split(jnp.broadcast_to(loss, (1, rows)))
    out_ref[rows:] = stack([x.astype(F32) for x in extra], EXTRA, width).astype(BF16)
    direct_ref[...] = (pos * grad_pos + neg * grad_neg) * (c_unit - cos * q_unit) * q_norm


def backward_kernel(f_ref, ft_ref, weights_ref, top_ref, d_ref, *refs, unit, group, scale):
    if unit == 0:
        direct_ref, refs = refs[0], refs[1:]
    dq_ref, ds_ref, w_ref = refs
    width = f_ref.shape[1]
    rows = top_ref.shape[1]
    m = unpack(d_ref[rows:].astype(F32), 0, rows)
    weights = weights_ref[...] * jnp.exp(top_ref[...] - m)
    w_ref[...] = weights.astype(BF16)
    ds = (weights * nt(f_ref[...], d_ref[:rows]) * scale).astype(BF16)
    ds_ref[...] = ds
    dqt = nn(ft_ref[...], ds)
    dq = turned(dqt, eye(rows)) + direct_ref[...] if unit == 0 else nt(eye(rows), dqt.astype(BF16))
    dq_ref[...] = dq.reshape(group, rows // group, width)


def spread_kernel(*refs, units, group):
    in_refs, d_refs, out_refs, loss_ref = refs[:units], refs[units : 2 * units], refs[2 * units : -1], refs[-1]
    me = lax.axis_index("frame")
    rows = d_refs[0].shape[0] - EXTRA
    loss = jnp.zeros(loss_ref.shape, F32)
    for i in range(units):
        loss = loss + unpack(d_refs[i][rows:].astype(F32), 1, loss_ref.shape[1])
        slot = (i // group) * group + (me ^ (i % group))
        for j, ref in enumerate(out_refs):
            if ref.shape[0] == units:
                ref[slot] = in_refs[i][me ^ j].astype(ref.dtype)
            else:

                @pl.when(slot < ref.shape[0])
                def _(ref=ref, i=i, j=j, slot=slot):
                    ref[slot] = in_refs[i][me ^ j].astype(ref.dtype)

    loss_ref[...] = loss


def frames_kernel(*refs, units):
    ds_refs, q_refs, w_refs, d_refs = [refs[k * units : (k + 1) * units] for k in range(4)]
    out_ref, held_ref, sems = refs[4 * units :]
    rows, depth = q_refs[0].shape[0], held_ref.shape[0]
    blocks = sems.shape[0]
    size = depth // blocks
    copies = []
    for b in range(blocks):
        at = pl.ds(b * size, size)
        total = None
        for i in range(units):
            term = nn(ds_refs[i][at], q_refs[i][...]) + nn(w_refs[i][at], d_refs[i][:rows])
            total = term if total is None else total + term
        held_ref[at] = total.astype(BF16)
        copies.append(pltpu.make_async_copy(held_ref.at[at], out_ref.at[0, at], sems.at[b]))
        copies[-1].start()
    for copy in copies:
        copy.wait()


def finish_kernel(table_ref, pair_ref, across_ref, *refs, n_cand):
    in_refs, outs = refs[:-3], refs[-3:]
    owned = n_cand // 3
    w, width = in_refs[0].shape[1:]
    for c in range(n_cand):
        s = table_ref[2 * n_cand + c]
        j = c % owned
        at = jnp.maximum(s, 0)
        total = functools.reduce(jnp.add, [x[at].astype(F32) for x in in_refs])
        outs[c // owned][j * w : (j + 1) * w] = jnp.where(s >= 0, total, 0.0).astype(BF16)
    for ref, loss_ref in zip(outs, (across_ref, across_ref, pair_ref)):
        pieces = [x.astype(F32) for x in split(loss_ref[...])]
        ref[owned * w :] = stack(pieces, EXTRA, width).astype(BF16)


def close_kernel(pair_ref, near_ref, far_ref, cross_ref, out_ref, total_ref):
    owned, w, _ = out_ref.shape
    loss = pair_ref[...]
    for ref in (near_ref, far_ref, cross_ref):
        loss = loss + unpack(ref[owned * w :].astype(F32), 0, total_ref.shape[1])
    total_ref[...] = loss
    for j in range(owned):
        at = slice(j * w, (j + 1) * w)
        total = near_ref[at].astype(F32) + far_ref[at].astype(F32)
        out_ref[j] = (total + cross_ref[at].astype(F32)).astype(BF16)


def call(kernel, out_shape, in_specs, *args, scratch=(), flops=0, nbytes=1 << 20, vmem=16, out_specs=None):
    many = isinstance(out_shape, (list, tuple))
    return pl.pallas_call(
        kernel,
        out_shape=out_shape,
        in_specs=in_specs,
        out_specs=out_specs or ([VMEM] * len(out_shape) if many else VMEM),
        scratch_shapes=list(scratch),
        compiler_params=pltpu.CompilerParams(vmem_limit_bytes=vmem << 20),
        cost_estimate=pl.CostEstimate(flops=flops, bytes_accessed=nbytes, transcendentals=0),
    )(*args)


def permute(x, recs, group, move, sends=None):
    pairs = []
    for r in range(recs):
        for f in range(group):
            to_r, to_f = move(r, f)
            if sends is None or sends(f, to_f):
                pairs.append((r * group + f, to_r * group + to_f))
    return lax.ppermute(x, AXES, pairs)


def near_of(r, recs):
    return r ^ 1


def far_of(r, recs):
    return (r - 1) % recs if r % 2 == 0 else (r + 1) % recs


def cross_of(r, recs):
    return (r + recs // 2) % recs


def slot_body(slots, frames, near, far, cross, table, *, tokens, recs, group):
    owned, w, width = near.shape
    n_cand = 3 * owned
    rows = group * w
    depth = frames.shape[1]
    f = frames[0]
    scale = width ** (-0.5)
    rounds = -(-slots // group)
    units = rounds * group
    cost = 2 * rows * depth * width
    shape = jax.ShapeDtypeStruct
    xor = [lambda r, g, j=j: (r, g ^ j) for j in range(group)]
    order = [3, 1, 2, 0]

    q = call(
        functools.partial(select_kernel, slots=slots, n_cand=n_cand),
        shape((slots, w, width), BF16),
        [SMEM, VMEM, VMEM, VMEM],
        table, near, far, cross,
    )
    qs = [q] + [permute(q, recs, group, xor[j]) for j in range(1, group)]
    ft = call(prepare_kernel, shape((width, depth), BF16), [VMEM], f, flops=cost)
    made, sent = {}, {}
    for r in range(rounds):
        for i in order:
            made[r, i] = call(
functools.partial(forward_kernel, unit=i, first=r * group, group=group, scale=scale),
                [
                    shape((rows + LINES, width), F32),
                    shape((depth, rows), F32),
                    shape((1, rows), F32),
                    shape((rows, width), BF16),
                ],
                [VMEM] * (2 + group),
                f, ft, *qs,
                scratch=[pltpu.VMEM((group, w, width), F32)],
                flops=2 * cost,
            )
            sent[r, i] = made[r, i][0]
            if i:
                sent[r, i] = permute(
                    sent[r, i], recs, group, xor[i], lambda a, b, r=r: r * group + b < slots
                )
    ds, directs = {}, {}
    for r in range(rounds):
        d, directs[r] = call(
            functools.partial(token_kernel, first=r * group, group=group, tokens=tokens, n_cand=n_cand),
            [shape((rows + EXTRA, width), BF16), shape((rows, width), F32)],
            [SMEM] + [VMEM] * (1 + group),
            table, made[r, 0][3], *[sent[r, i] for i in range(group)],
        )
        for i in order:
            ds[r, i] = d
            if i:
                ds[r, i] = permute(d, recs, group, xor[i], lambda a, b, r=r: r * group + a < slots)
    back = {}
    for r in range(rounds):
        for i in order:
            back[r, i] = call(
                functools.partial(backward_kernel, unit=i, group=group, scale=scale),
                [shape((group, w, width), F32), shape((depth, rows), BF16), shape((depth, rows), BF16)],
                [VMEM] * (6 if i == 0 else 5),
                f, ft, made[r, i][1], made[r, i][2], ds[r, i], *([directs[r]] if i == 0 else []),
                flops=2 * cost,
            )
    keys = [(r, i) for r in range(rounds) for i in range(group)]
    *dqs, loss = call(
        functools.partial(spread_kernel, units=units, group=group),
        [shape((slots, w, width), BF16)] * group + [shape((1, 128), F32)],
        [VMEM] * (2 * units),
        *[back[k][0] for k in keys], *[ds[k] for k in keys],
    )
    dqs = [dqs[0]] + [permute(dqs[j], recs, group, xor[j]) for j in range(1, group)]
    pair = loss + permute(loss, recs, group, lambda r, g: (r ^ 2, g))
    across = loss + permute(loss, recs, group, lambda r, g: (cross_of(r, recs), g))
    home = call(
        functools.partial(finish_kernel, n_cand=n_cand),
        [shape((owned * w + EXTRA, width), BF16)] * 3,
        [SMEM] + [VMEM] * (2 + group),
        table, pair, across, *dqs,
    )
    got = []
    for x, where in zip(home, (near_of, far_of, cross_of)):
        got.append(permute(x, recs, group, lambda r, g: (where(r, recs), g)))
    args = [back[k][1] for k in keys]
    args[0], _ = lax.optimization_barrier((args[0], home[0]))
    args += [made[k][3] for k in keys] + [back[k][2] for k in keys] + [ds[k] for k in keys]
    blocks = 6 if depth % 768 == 0 else 1
    total = call(
        functools.partial(frames_kernel, units=units),
        pltpu.HBM(frames.shape, BF16),
        [VMEM] * len(args),
        *args,
        out_specs=pl.BlockSpec(memory_space=pltpu.HBM),
        scratch=[pltpu.VMEM((depth, width), BF16), pltpu.SemaphoreType.DMA((blocks,))],
        flops=2 * units * cost,
    )
    texts, loss = call(
        close_kernel,
        [shape((owned, w, width), BF16), shape((1, 128), F32)],
        [VMEM] * 4,
        pair, *got,
    )
    return loss[0, 0], total, texts


def body(frames, texts, pair_rec, pair_text, pair_label):
    recs, group = lax.axis_size("rec"), lax.axis_size("frame")
    owned, w, _ = texts.shape
    if group != 4 or w % 8 or recs != 8 or 3 * owned > 2 * group or owned * recs > 32:
        return general_body(frames, texts, pair_rec, pair_text, pair_label)
    fetched = []
    for to in (near_of, far_of, cross_of):
        fetched.append(permute(texts, recs, group, lambda r, g: (to(r, recs), g)))
    near, far, cross = fetched
    n_cand = 3 * owned
    table = pl.pallas_call(
        functools.partial(table_kernel, recs=recs, owned=owned),
        name="table",
        out_shape=jax.ShapeDtypeStruct((4 * n_cand + 2,), jnp.int32),
        in_specs=[SMEM] * 3,
        out_specs=SMEM,
        scratch_shapes=[pltpu.SMEM((recs,), jnp.int32)] * 2,
    )(pair_rec[:, 0], pair_text, pair_label)

    def run(slots, *args):
        return slot_body(slots, *args, tokens=w * group, recs=recs, group=group)

    args = (frames, near, far, cross, table)
    return lax.cond(
        table[4 * n_cand] <= group, functools.partial(run, group), functools.partial(run, n_cand), *args
    )


def solution(mesh):
    return jax.shard_map(
        body,
        mesh=mesh,
        in_specs=(P("rec", "frame", None), P("rec", "frame", None), P(), P(), P()),
        out_specs=(P(), P("rec", "frame", None), P("rec", "frame", None)),
        check_vma=False,
    )
```

```python
import functools

import jax
import jax.numpy as jnp
from jax import lax
from jax.experimental import pallas as pl
from jax.experimental.pallas import tpu as pltpu
from jax.sharding import PartitionSpec as P

MOST = 6
EPS = 1e-06
TEMP = 10.0
BIAS = -1.0
LOSS_SCALE = 2048.0

F32 = jnp.float32
BF16 = jnp.bfloat16
EXTRA = 16
LINES = 8
AXES = ("rec", "frame")
VMEM = pl.BlockSpec(memory_space=pltpu.VMEM)
SMEM = pl.BlockSpec(memory_space=pltpu.SMEM)


def nt(a, b):
    return lax.dot_general(a, b, (((1,), (1,)), ((), ())), preferred_element_type=F32)


def nn(a, b):
    return lax.dot_general(a, b, (((1,), (0,)), ((), ())), preferred_element_type=F32)


def slot_tables(pair_rec, pair_text, pair_label, here, most):
    record = pair_rec[:, 0]
    count = record.shape[0]
    order = jnp.arange(count, dtype=jnp.int32)
    same = (record[:, None] == record[None, :]).astype(jnp.int32)
    earlier = (order[None, :] < order[:, None]).astype(jnp.int32)
    rank = jnp.sum(same * earlier, axis=1)
    places = jnp.arange(most, dtype=jnp.int32)
    chosen = ((record[None, :] == here) & (rank[None, :] == places[:, None])).astype(jnp.int32)
    valid = jnp.sum(chosen, axis=1)
    slot_text = jnp.sum(chosen * pair_text[None, :], axis=1)
    sign = jnp.sum(chosen * (2 * pair_label[None, :] - 1), axis=1)
    return (valid, slot_text, sign)


def pair_terms(score, valid, sign, tokens):
    margin = -sign * (TEMP * score + BIAS)
    loss_part = valid * jax.nn.softplus(margin)
    grad_cos = -LOSS_SCALE * TEMP * valid * sign * jax.nn.sigmoid(margin) / tokens
    return (loss_part, grad_cos)


def general_body(frames, texts, pair_rec, pair_text, pair_label):
    here = lax.axis_index("rec")
    part = lax.axis_index("frame")
    owned, width_rows, width = texts.shape
    tokens = width_rows * lax.axis_size("frame")
    n_text = owned * lax.axis_size("rec")
    valid, slot_text, sign = slot_tables(pair_rec, pair_text, pair_label, here, MOST)
    valid_f = valid.astype(jnp.float32)
    sign_f = sign.astype(jnp.float32)
    picks = (
        (slot_text[:, None] == jnp.arange(n_text, dtype=jnp.int32)[None, :]) & (valid[:, None] > 0)
    ).astype(jnp.bfloat16)
    local = jnp.einsum(
        "jc,cgx->jgx",
        picks,
        lax.all_gather(texts, "rec", axis=0, tiled=True),
        preferred_element_type=jnp.float32,
    ).astype(jnp.bfloat16)
    query_vectors = lax.all_gather(local, "frame", axis=1, tiled=True)
    upstream_signal = frames[0]
    logit_scale = width ** (-0.5)
    pair_scores = (
        jnp.einsum(
            "ype,je->ypj", query_vectors, upstream_signal, preferred_element_type=jnp.float32
        )
        * logit_scale
    )
    local_max = jnp.max(pair_scores, axis=2)
    row_max = lax.pmax(local_max, "frame")
    expo = jnp.exp(pair_scores - row_max[..., None])
    batch_weights = expo.astype(jnp.bfloat16)
    value_partial = jnp.einsum(
        "pqx,xh->pqh", batch_weights, upstream_signal, preferred_element_type=jnp.float32
    )
    query_f = query_vectors.astype(jnp.float32)
    q_norm = lax.rsqrt(jnp.sum(query_f * query_f, axis=2) + EPS)
    q_unit = query_f * q_norm[..., None]
    context = lax.psum(value_partial, "frame")
    c_norm = lax.rsqrt(jnp.sum(context * context, axis=2) + EPS)
    c_unit = context * c_norm[..., None]
    cos = jnp.sum(q_unit * c_unit, axis=2)
    score = jnp.mean(cos, axis=1)
    loss_part, grad_cos = pair_terms(score, valid_f, sign_f, tokens)
    weight = grad_cos[:, None, None]
    d_context = weight * (q_unit - cos[..., None] * c_unit) * c_norm[..., None]
    direct = weight * (c_unit - cos[..., None] * q_unit) * q_norm[..., None]
    direct_own = lax.dynamic_slice_in_dim(direct, part * width_rows, width_rows, 1)
    context_batch_gradient = d_context.astype(jnp.bfloat16)
    weight_gradient = jnp.einsum(
        "ype,je->ypj", context_batch_gradient, upstream_signal, preferred_element_type=jnp.float32
    )
    score_gradient = (expo * weight_gradient * logit_scale).astype(jnp.bfloat16)
    d_query = lax.psum_scatter(
        jnp.einsum(
            "slf,fd->lsd", score_gradient, upstream_signal, preferred_element_type=jnp.float32
        ),
        "frame",
        scatter_dimension=0,
        tiled=True,
    )
    d_query = d_query + jnp.transpose(direct_own, (1, 0, 2))
    text_term = jnp.einsum(
        "st,lsd->tld", picks.astype(jnp.float32), d_query, precision=lax.Precision.HIGHEST
    )
    grad_texts = lax.psum_scatter(text_term, "rec", scatter_dimension=0, tiled=True).astype(
        jnp.bfloat16
    )
    frame_loss_piece = jnp.einsum(
        "cvm,cvz->mz", score_gradient, query_vectors, preferred_element_type=jnp.float32
    )
    frame_loss_piece = frame_loss_piece + jnp.einsum(
        "cvm,cvz->mz", batch_weights, context_batch_gradient, preferred_element_type=jnp.float32
    )
    grad_frames = frame_loss_piece.astype(jnp.bfloat16)[None]
    loss = lax.psum(jnp.sum(loss_part), "rec")
    return (loss, grad_frames, grad_texts)


def split(line):
    pieces = []
    for _ in range(3):
        piece = line.astype(BF16)
        pieces.append(piece)
        line = line - piece.astype(F32)
    return pieces


def stack(lines, count, width):
    n = lines[0].shape[1]
    place = lax.broadcasted_iota(jnp.int32, (count, n), 0)
    out = jnp.zeros((count, n), F32)
    for at, line in enumerate(lines):
        out = jnp.where(place == at, line, out)
    if n < width:
        out = jnp.concatenate([out, jnp.zeros((count, width - n), F32)], axis=1)
    return out


def unpack(extra, i, n):
    got = [extra[3 * i + j : 3 * i + j + 1, :n] for j in range(3)]
    return (got[0] + got[1]) + got[2]


def diagonal(n):
    r = lax.broadcasted_iota(jnp.int32, (n, n), 0)
    c = lax.broadcasted_iota(jnp.int32, (n, n), 1)
    return r == c


def eye(n):
    return jnp.where(diagonal(n), 1.0, 0.0).astype(BF16)


def to_column(line, one, lanes):
    n = line.shape[1]
    out = None
    for piece in split(line):
        term = nt(one, jnp.broadcast_to(piece, (lanes, n)))
        out = term if out is None else out + term
    return out


def turned(x, one):
    high = x.astype(BF16)
    low = (x - high.astype(F32)).astype(BF16)
    return nt(one, high) + nt(one, low)


def table_kernel(rec_ref, text_ref, label_ref, table_ref, most_ref, out_ref, seen_ref, count_ref, *, recs, owned):
    here = lax.axis_index("rec")
    odd = lax.rem(here, 2)
    far, cross = lax.rem(here + 2 * odd + recs - 1, recs), lax.rem(here + recs // 2, recs)
    n_cand = 3 * owned
    for i in range(2 * n_cand):
        out_ref[i] = 0
    for r in range(recs):
        seen_ref[r] = 0
        count_ref[r] = 0

    def pair(p, most):
        rec, text, label = rec_ref[p], text_ref[p], label_ref[p]
        seen, bit = seen_ref[rec], lax.shift_left(jnp.int32(1), text)
        n = count_ref[rec] + jnp.where((seen & bit) == 0, 1, 0)
        seen_ref[rec] = seen | bit
        count_ref[rec] = n
        owner = lax.div(text, owned)
        which = jnp.where(owner == far, 1, jnp.where(owner == cross, 2, 0))
        at = which * owned + text - owner * owned + (1 - label) * n_cand
        at = jnp.where(rec == here, at, 2 * n_cand)
        out_ref[at] = out_ref[at] + 1
        return jnp.maximum(most, n)

    out_ref[2 * n_cand] = 0
    most_ref[0] = lax.fori_loop(0, text_ref.shape[0], pair, jnp.int32(0))
    row = lax.broadcasted_iota(jnp.int32, table_ref.shape, 0)
    lane = lax.broadcasted_iota(jnp.int32, table_ref.shape, 1)
    table = jnp.zeros(table_ref.shape, F32)
    at = jnp.int32(0)
    for c in range(n_cand):
        pos, neg = out_ref[c], out_ref[n_cand + c]
        used = (pos + neg) > 0
        here = row == jnp.where(used, at, -1)
        for k, value in ((c, 1.0), (n_cand, pos.astype(F32)), (n_cand + 1, neg.astype(F32))):
            table = jnp.where(here & (lane == k), value, table)
        at = at + jnp.where(used, 1, 0)
    table_ref[...] = table


def select_kernel(table_ref, *refs, slots):
    cand_refs, out_ref = refs[:-1], refs[-1]
    owned = cand_refs[0].shape[0]
    cands = [ref[j].astype(F32) for ref in cand_refs for j in range(owned)]
    for s in range(slots):
        picked = [table_ref[s : s + 1, c : c + 1] * cand for c, cand in enumerate(cands)]
        out_ref[s] = functools.reduce(jnp.add, picked).astype(out_ref.dtype)


def prepare_kernel(f_ref, out_ref):
    out_ref[...] = nt(eye(f_ref.shape[1]), f_ref[...]).astype(BF16)


def if_slot(slot, slots, group, work, idle):
    if slots % group == 0:
        work()
    else:
        pl.when(slot < slots)(work)
        pl.when(slot >= slots)(idle)


def clear(*refs):
    for ref in refs:
        ref[...] = jnp.zeros(ref.shape, ref.dtype)


def forward_kernel(f_ref, ft_ref, *refs, unit, first, group, scale):
    q_refs, (out_ref, weights_ref, top_ref, q_out_ref, q_ref) = refs[:group], refs[group:]
    me = lax.axis_index("frame")
    held, w, width = q_refs[0].shape
    slot = first + (me ^ unit)
    rows = group * w

    def work():
        for j in range(group):
            q_ref[me ^ j] = q_refs[j][jnp.minimum(slot, held - 1)].astype(F32)
        q = q_ref[...].reshape(rows, width).astype(BF16)
        q_out_ref[...] = q
        s = nt(f_ref[...], q) * scale
        top = jnp.max(s, axis=0, keepdims=True)
        weights = jnp.exp(s - top)
        weights_ref[...] = weights
        top_ref[...] = top
        out_ref[:rows] = turned(nn(ft_ref[...], weights.astype(BF16)), eye(rows))
        out_ref[rows:] = stack([top], LINES, width)

    if_slot(slot, held if first else group, group, work, lambda: clear(q_out_ref, out_ref))


def token_kernel(table_ref, q_ref, *refs, first, slots, group, tokens, n_cand):
    in_refs, (out_ref, direct_ref) = refs[:group], refs[group:]
    rows, width = q_ref.shape
    one = eye(rows)
    tops = [ref[rows : rows + 1, :rows] for ref in in_refs]
    m = functools.reduce(jnp.maximum, tops)
    context = jnp.zeros((rows, width), F32)
    for top, ref in zip(tops, in_refs):
        share = to_column(jnp.exp(top - m), one, 128)
        context = context + jnp.concatenate([share] * (width // 128), axis=1) * ref[:rows]
    q = q_ref[...].astype(F32)
    q_norm = lax.rsqrt(jnp.sum(q * q, axis=1, keepdims=True) + EPS)
    c_norm = lax.rsqrt(jnp.sum(context * context, axis=1, keepdims=True) + EPS)
    q_unit, c_unit = q * q_norm, context * c_norm
    cos = jnp.sum(q_unit * c_unit, axis=1, keepdims=True)
    score = jnp.sum(cos, axis=0, keepdims=True) / tokens
    logit = TEMP * score + BIAS
    table = table_ref[...]
    mine = lax.broadcasted_iota(jnp.int32, table.shape, 0) == first + lax.axis_index("frame")
    counts = jnp.sum(jnp.where(mine, table, 0.0), axis=0, keepdims=True)
    pos, neg = counts[:, n_cand : n_cand + 1], counts[:, n_cand + 1 : n_cand + 2]
    tail = jnp.log1p(jnp.exp(-jnp.abs(logit)))
    loss = pos * (jnp.maximum(-logit, 0.0) + tail) + neg * (jnp.maximum(logit, 0.0) + tail)
    grad_pos = (-LOSS_SCALE * TEMP / tokens) * jax.nn.sigmoid(-logit)
    grad_neg = (LOSS_SCALE * TEMP / tokens) * jax.nn.sigmoid(logit)
    side = q_unit - cos * c_unit
    d_pos = (grad_pos * side * c_norm).astype(BF16).astype(F32)
    d_neg = (grad_neg * side * c_norm).astype(BF16).astype(F32)
    out_ref[:rows] = (pos * d_pos + neg * d_neg).astype(BF16)
    extra = split(m) + split(jnp.broadcast_to(loss, (1, rows)))
    out_ref[rows:] = stack([x.astype(F32) for x in extra], EXTRA, width).astype(BF16)
    direct_ref[...] = (pos * grad_pos + neg * grad_neg) * (c_unit - cos * q_unit) * q_norm


def backward_kernel(f_ref, ft_ref, weights_ref, top_ref, d_ref, *refs, unit, first, slots, group, scale):
    if unit == 0:
        direct_ref, refs = refs[0], refs[1:]
    dq_ref, ds_ref, w_ref = refs
    width = f_ref.shape[1]
    rows = top_ref.shape[1]
    slot = first + (lax.axis_index("frame") ^ unit)

    def work():
        m = unpack(d_ref[rows:].astype(F32), 0, rows)
        weights = weights_ref[...] * jnp.exp(top_ref[...] - m)
        w_ref[...] = weights.astype(BF16)
        ds = (weights * nt(f_ref[...], d_ref[:rows]) * scale).astype(BF16)
        ds_ref[...] = ds
        dqt = nn(ft_ref[...], ds)
        dq = turned(dqt, eye(rows)) + direct_ref[...] if unit == 0 else nt(eye(rows), dqt.astype(BF16))
        dq_ref[...] = dq.reshape(group, rows // group, width)

    if_slot(slot, slots if first else group, group, work, lambda: clear(dq_ref, ds_ref, w_ref))


def spread_kernel(*refs, units, group):
    in_refs, d_refs, out_refs, loss_ref = refs[:units], refs[units : 2 * units], refs[2 * units : -1], refs[-1]
    me = lax.axis_index("frame")
    rows = d_refs[0].shape[0] - EXTRA
    loss = jnp.zeros(loss_ref.shape, F32)
    for i in range(units):
        loss = loss + unpack(d_refs[i][rows:].astype(F32), 1, loss_ref.shape[1])
        slot = (i // group) * group + (me ^ (i % group))
        for j, ref in enumerate(out_refs):
            if ref.shape[0] == units:
                ref[slot] = in_refs[i][me ^ j].astype(ref.dtype)
            else:

                @pl.when(slot < ref.shape[0])
                def _(ref=ref, i=i, j=j, slot=slot):
                    ref[slot] = in_refs[i][me ^ j].astype(ref.dtype)

    loss_ref[...] = loss


def frames_kernel(*refs, units):
    ds_refs, q_refs, w_refs, d_refs = [refs[k * units : (k + 1) * units] for k in range(4)]
    out_ref, held_ref, sems = refs[4 * units :]
    rows, depth = q_refs[0].shape[0], held_ref.shape[0]
    blocks = sems.shape[0]
    size = depth // blocks
    copies = []
    for b in range(blocks):
        at = pl.ds(b * size, size)
        total = None
        for i in range(units):
            term = nn(ds_refs[i][at], q_refs[i][...]) + nn(w_refs[i][at], d_refs[i][:rows])
            total = term if total is None else total + term
        held_ref[at] = total.astype(BF16)
        copies.append(pltpu.make_async_copy(held_ref.at[at], out_ref.at[0, at], sems.at[b]))
        copies[-1].start()
    for copy in copies:
        copy.wait()


def finish_kernel(table_ref, pair_ref, across_ref, *refs):
    in_refs, outs = refs[:-3], refs[-3:]
    slots, w, width = in_refs[0].shape
    owned = (outs[0].shape[0] - EXTRA) // w
    totals = [functools.reduce(jnp.add, [x[s].astype(F32) for x in in_refs]) for s in range(slots)]
    for c in range(3 * owned):
        picked = [table_ref[s : s + 1, c : c + 1] * total for s, total in enumerate(totals)]
        j = c % owned
        outs[c // owned][j * w : (j + 1) * w] = functools.reduce(jnp.add, picked).astype(BF16)
    for ref, loss_ref in zip(outs, (across_ref, across_ref, pair_ref)):
        pieces = [x.astype(F32) for x in split(loss_ref[...])]
        ref[owned * w :] = stack(pieces, EXTRA, width).astype(BF16)


def close_kernel(pair_ref, near_ref, far_ref, cross_ref, out_ref, total_ref):
    owned, w, _ = out_ref.shape
    loss = pair_ref[...]
    for ref in (near_ref, far_ref, cross_ref):
        loss = loss + unpack(ref[owned * w :].astype(F32), 0, total_ref.shape[1])
    total_ref[...] = loss
    for j in range(owned):
        at = slice(j * w, (j + 1) * w)
        total = near_ref[at].astype(F32) + far_ref[at].astype(F32)
        out_ref[j] = (total + cross_ref[at].astype(F32)).astype(BF16)


def call(kernel, out_shape, in_specs, *args, scratch=(), flops=0, nbytes=1 << 20, vmem=16, out_specs=None):
    many = isinstance(out_shape, (list, tuple))
    return pl.pallas_call(
        kernel,
        out_shape=out_shape,
        in_specs=in_specs,
        out_specs=out_specs or ([VMEM] * len(out_shape) if many else VMEM),
        scratch_shapes=list(scratch),
        compiler_params=pltpu.CompilerParams(vmem_limit_bytes=vmem << 20),
        cost_estimate=pl.CostEstimate(flops=flops, bytes_accessed=nbytes, transcendentals=0),
    )(*args)


def permute(x, recs, group, move, sends=None):
    pairs = []
    for r in range(recs):
        for f in range(group):
            to_r, to_f = move(r, f)
            if sends is None or sends(f, to_f):
                pairs.append((r * group + f, to_r * group + to_f))
    return lax.ppermute(x, AXES, pairs)


def near_of(r, recs):
    return r ^ 1


def far_of(r, recs):
    return (r - 1) % recs if r % 2 == 0 else (r + 1) % recs


def cross_of(r, recs):
    return (r + recs // 2) % recs


def slot_body(slots, frames, near, far, cross, table, *, tokens, recs, group):
    owned, w, width = near.shape
    n_cand = 3 * owned
    rows = group * w
    depth = frames.shape[1]
    f = frames[0]
    scale = width ** (-0.5)
    rounds = -(-slots // group)
    units = rounds * group
    cost = 2 * rows * depth * width
    shape = jax.ShapeDtypeStruct
    xor = [lambda r, g, j=j: (r, g ^ j) for j in range(group)]
    order = [3, 1, 2, 0]

    q = call(
        functools.partial(select_kernel, slots=slots),
        shape((slots, w, width), BF16),
        [VMEM] * 4,
        table, near, far, cross,
    )
    qs = [q] + [permute(q, recs, group, xor[j]) for j in range(1, group)]
    ft = call(prepare_kernel, shape((width, depth), BF16), [VMEM], f, flops=cost)
    made, sent = {}, {}
    for r in range(rounds):
        for i in order:
            made[r, i] = call(
functools.partial(forward_kernel, unit=i, first=r * group, group=group, scale=scale),
                [
                    shape((rows + LINES, width), F32),
                    shape((depth, rows), F32),
                    shape((1, rows), F32),
                    shape((rows, width), BF16),
                ],
                [VMEM] * (2 + group),
                f, ft, *qs,
                scratch=[pltpu.VMEM((group, w, width), F32)],
                flops=2 * cost,
            )
            sent[r, i] = made[r, i][0]
            if i:
                sent[r, i] = permute(
                    sent[r, i], recs, group, xor[i], lambda a, b, r=r: r * group + b < slots
                )
    ds, directs = {}, {}
    for r in range(rounds):
        d, directs[r] = call(
            functools.partial(
                token_kernel, first=r * group, slots=slots, group=group, tokens=tokens, n_cand=n_cand
            ),
            [shape((rows + EXTRA, width), BF16), shape((rows, width), F32)],
            [VMEM] * (2 + group),
            table, made[r, 0][3], *[sent[r, i] for i in range(group)],
        )
        for i in order:
            ds[r, i] = d
            if i:
                ds[r, i] = permute(d, recs, group, xor[i], lambda a, b, r=r: r * group + a < slots)
    back = {}
    for r in range(rounds):
        for i in order:
            back[r, i] = call(
                functools.partial(
                    backward_kernel, unit=i, first=r * group, slots=slots, group=group, scale=scale
                ),
                [shape((group, w, width), F32), shape((depth, rows), BF16), shape((depth, rows), BF16)],
                [VMEM] * (6 if i == 0 else 5),
                f, ft, made[r, i][1], made[r, i][2], ds[r, i], *([directs[r]] if i == 0 else []),
                flops=2 * cost,
            )
    keys = [(r, i) for r in range(rounds) for i in range(group)]
    *dqs, loss = call(
        functools.partial(spread_kernel, units=units, group=group),
        [shape((slots, w, width), BF16)] * group + [shape((1, 128), F32)],
        [VMEM] * (2 * units),
        *[back[k][0] for k in keys], *[ds[k] for k in keys],
    )
    dqs = [dqs[0]] + [permute(dqs[j], recs, group, xor[j]) for j in range(1, group)]
    pair = loss + permute(loss, recs, group, lambda r, g: (r ^ 2, g))
    across = loss + permute(loss, recs, group, lambda r, g: (cross_of(r, recs), g))
    home = call(
        finish_kernel,
        [shape((owned * w + EXTRA, width), BF16)] * 3,
        [VMEM] * (3 + group),
        table, pair, across, *dqs,
    )
    got = []
    for x, where in zip(home, (near_of, far_of, cross_of)):
        got.append(permute(x, recs, group, lambda r, g: (where(r, recs), g)))
    args = [back[k][1] for k in keys]
    args[0], _ = lax.optimization_barrier((args[0], home[0]))
    args += [made[k][3] for k in keys] + [back[k][2] for k in keys] + [ds[k] for k in keys]
    blocks = 6 if depth % 768 == 0 else 1
    total = call(
        functools.partial(frames_kernel, units=units),
        pltpu.HBM(frames.shape, BF16),
        [VMEM] * len(args),
        *args,
        out_specs=pl.BlockSpec(memory_space=pltpu.HBM),
        scratch=[pltpu.VMEM((depth, width), BF16), pltpu.SemaphoreType.DMA((blocks,))],
        flops=2 * units * cost,
    )
    texts, loss = call(
        close_kernel,
        [shape((owned, w, width), BF16), shape((1, 128), F32)],
        [VMEM] * 4,
        pair, *got,
    )
    return loss[0, 0], total, texts


def body(frames, texts, pair_rec, pair_text, pair_label):
    recs, group = lax.axis_size("rec"), lax.axis_size("frame")
    owned, w, _ = texts.shape
    if group != 4 or w % 8 or recs != 8 or 3 * owned > 2 * group or owned * recs > 32:
        return general_body(frames, texts, pair_rec, pair_text, pair_label)
    fetched = []
    for to in (near_of, far_of, cross_of):
        fetched.append(permute(texts, recs, group, lambda r, g: (to(r, recs), g)))
    near, far, cross = fetched
    n_cand = 3 * owned
    table, most = pl.pallas_call(
        functools.partial(table_kernel, recs=recs, owned=owned),
        name="table",
        out_shape=[jax.ShapeDtypeStruct((8, 128), F32), jax.ShapeDtypeStruct((1,), jnp.int32)],
        in_specs=[SMEM] * 3,
        out_specs=[VMEM, SMEM],
        scratch_shapes=[pltpu.SMEM((n,), jnp.int32) for n in (2 * n_cand + 1, recs, recs)],
    )(pair_rec[:, 0], pair_text, pair_label)

    def run(slots, *args):
        return slot_body(slots, *args, tokens=w * group, recs=recs, group=group)

    args = (frames, near, far, cross, table)
    return lax.cond(
        most[0] <= group, functools.partial(run, group), functools.partial(run, n_cand), *args
    )


def solution(mesh):
    return jax.shard_map(
        body,
        mesh=mesh,
        in_specs=(P("rec", "frame", None), P("rec", "frame", None), P(), P(), P()),
        out_specs=(P(), P("rec", "frame", None), P("rec", "frame", None)),
        check_vma=False,
    )
```

```python
import functools

import jax
import jax.numpy as jnp
from jax import lax
from jax.experimental import pallas as pl
from jax.experimental.pallas import tpu as pltpu
from jax.sharding import PartitionSpec as P

MOST = 6
EPS = 1e-06
TEMP = 10.0
BIAS = -1.0
LOSS_SCALE = 2048.0

F32 = jnp.float32
BF16 = jnp.bfloat16
EXTRA = 16
LINES = 8
AXES = ("rec", "frame")
VMEM = pl.BlockSpec(memory_space=pltpu.VMEM)
SMEM = pl.BlockSpec(memory_space=pltpu.SMEM)


def nt(a, b):
    return lax.dot_general(a, b, (((1,), (1,)), ((), ())), preferred_element_type=F32)


def nn(a, b):
    return lax.dot_general(a, b, (((1,), (0,)), ((), ())), preferred_element_type=F32)


def slot_tables(pair_rec, pair_text, pair_label, here, most):
    record = pair_rec[:, 0]
    count = record.shape[0]
    order = jnp.arange(count, dtype=jnp.int32)
    same = (record[:, None] == record[None, :]).astype(jnp.int32)
    earlier = (order[None, :] < order[:, None]).astype(jnp.int32)
    rank = jnp.sum(same * earlier, axis=1)
    places = jnp.arange(most, dtype=jnp.int32)
    chosen = ((record[None, :] == here) & (rank[None, :] == places[:, None])).astype(jnp.int32)
    valid = jnp.sum(chosen, axis=1)
    slot_text = jnp.sum(chosen * pair_text[None, :], axis=1)
    sign = jnp.sum(chosen * (2 * pair_label[None, :] - 1), axis=1)
    return (valid, slot_text, sign)


def pair_terms(score, valid, sign, tokens):
    margin = -sign * (TEMP * score + BIAS)
    loss_part = valid * jax.nn.softplus(margin)
    grad_cos = -LOSS_SCALE * TEMP * valid * sign * jax.nn.sigmoid(margin) / tokens
    return (loss_part, grad_cos)


def general_body(frames, texts, pair_rec, pair_text, pair_label):
    here = lax.axis_index("rec")
    part = lax.axis_index("frame")
    owned, width_rows, width = texts.shape
    tokens = width_rows * lax.axis_size("frame")
    n_text = owned * lax.axis_size("rec")
    valid, slot_text, sign = slot_tables(pair_rec, pair_text, pair_label, here, MOST)
    valid_f = valid.astype(jnp.float32)
    sign_f = sign.astype(jnp.float32)
    picks = (
        (slot_text[:, None] == jnp.arange(n_text, dtype=jnp.int32)[None, :]) & (valid[:, None] > 0)
    ).astype(jnp.bfloat16)
    local = jnp.einsum(
        "jc,cgx->jgx",
        picks,
        lax.all_gather(texts, "rec", axis=0, tiled=True),
        preferred_element_type=jnp.float32,
    ).astype(jnp.bfloat16)
    query_vectors = lax.all_gather(local, "frame", axis=1, tiled=True)
    upstream_signal = frames[0]
    logit_scale = width ** (-0.5)
    pair_scores = (
        jnp.einsum(
            "ype,je->ypj", query_vectors, upstream_signal, preferred_element_type=jnp.float32
        )
        * logit_scale
    )
    local_max = jnp.max(pair_scores, axis=2)
    row_max = lax.pmax(local_max, "frame")
    expo = jnp.exp(pair_scores - row_max[..., None])
    batch_weights = expo.astype(jnp.bfloat16)
    value_partial = jnp.einsum(
        "pqx,xh->pqh", batch_weights, upstream_signal, preferred_element_type=jnp.float32
    )
    query_f = query_vectors.astype(jnp.float32)
    q_norm = lax.rsqrt(jnp.sum(query_f * query_f, axis=2) + EPS)
    q_unit = query_f * q_norm[..., None]
    context = lax.psum(value_partial, "frame")
    c_norm = lax.rsqrt(jnp.sum(context * context, axis=2) + EPS)
    c_unit = context * c_norm[..., None]
    cos = jnp.sum(q_unit * c_unit, axis=2)
    score = jnp.mean(cos, axis=1)
    loss_part, grad_cos = pair_terms(score, valid_f, sign_f, tokens)
    weight = grad_cos[:, None, None]
    d_context = weight * (q_unit - cos[..., None] * c_unit) * c_norm[..., None]
    direct = weight * (c_unit - cos[..., None] * q_unit) * q_norm[..., None]
    direct_own = lax.dynamic_slice_in_dim(direct, part * width_rows, width_rows, 1)
    context_batch_gradient = d_context.astype(jnp.bfloat16)
    weight_gradient = jnp.einsum(
        "ype,je->ypj", context_batch_gradient, upstream_signal, preferred_element_type=jnp.float32
    )
    score_gradient = (expo * weight_gradient * logit_scale).astype(jnp.bfloat16)
    d_query = lax.psum_scatter(
        jnp.einsum(
            "slf,fd->lsd", score_gradient, upstream_signal, preferred_element_type=jnp.float32
        ),
        "frame",
        scatter_dimension=0,
        tiled=True,
    )
    d_query = d_query + jnp.transpose(direct_own, (1, 0, 2))
    text_term = jnp.einsum(
        "st,lsd->tld", picks.astype(jnp.float32), d_query, precision=lax.Precision.HIGHEST
    )
    grad_texts = lax.psum_scatter(text_term, "rec", scatter_dimension=0, tiled=True).astype(
        jnp.bfloat16
    )
    frame_loss_piece = jnp.einsum(
        "cvm,cvz->mz", score_gradient, query_vectors, preferred_element_type=jnp.float32
    )
    frame_loss_piece = frame_loss_piece + jnp.einsum(
        "cvm,cvz->mz", batch_weights, context_batch_gradient, preferred_element_type=jnp.float32
    )
    grad_frames = frame_loss_piece.astype(jnp.bfloat16)[None]
    loss = lax.psum(jnp.sum(loss_part), "rec")
    return (loss, grad_frames, grad_texts)


def split(line):
    pieces = []
    for _ in range(3):
        piece = line.astype(BF16)
        pieces.append(piece)
        line = line - piece.astype(F32)
    return pieces


def stack(lines, count, width):
    n = lines[0].shape[1]
    place = lax.broadcasted_iota(jnp.int32, (count, n), 0)
    out = jnp.zeros((count, n), F32)
    for at, line in enumerate(lines):
        out = jnp.where(place == at, line, out)
    if n < width:
        out = jnp.concatenate([out, jnp.zeros((count, width - n), F32)], axis=1)
    return out


def unpack(extra, i, n):
    got = [extra[3 * i + j : 3 * i + j + 1, :n] for j in range(3)]
    return (got[0] + got[1]) + got[2]


def diagonal(n):
    r = lax.broadcasted_iota(jnp.int32, (n, n), 0)
    c = lax.broadcasted_iota(jnp.int32, (n, n), 1)
    return r == c


def eye(n):
    return jnp.where(diagonal(n), 1.0, 0.0).astype(BF16)


def to_column(line, one, lanes):
    n = line.shape[1]
    out = None
    for piece in split(line):
        term = nt(one, jnp.broadcast_to(piece, (lanes, n)))
        out = term if out is None else out + term
    return out


def turned(x, one):
    high = x.astype(BF16)
    low = (x - high.astype(F32)).astype(BF16)
    return nt(one, high) + nt(one, low)


def table_kernel(rec_ref, text_ref, label_ref, table_ref, most_ref, out_ref, seen_ref, count_ref, *, recs, owned):
    here = lax.axis_index("rec")
    odd = lax.rem(here, 2)
    far, cross = lax.rem(here + 2 * odd + recs - 1, recs), lax.rem(here + recs // 2, recs)
    n_cand = 3 * owned
    for i in range(2 * n_cand):
        out_ref[i] = 0
    for r in range(recs):
        seen_ref[r] = 0
        count_ref[r] = 0

    def pair(p, most):
        rec, text, label = rec_ref[p], text_ref[p], label_ref[p]
        seen, bit = seen_ref[rec], lax.shift_left(jnp.int32(1), text)
        n = count_ref[rec] + jnp.where((seen & bit) == 0, 1, 0)
        seen_ref[rec] = seen | bit
        count_ref[rec] = n
        owner = lax.div(text, owned)
        which = jnp.where(owner == far, 1, jnp.where(owner == cross, 2, 0))
        at = which * owned + text - owner * owned + (1 - label) * n_cand
        at = jnp.where(rec == here, at, 2 * n_cand)
        out_ref[at] = out_ref[at] + 1
        return jnp.maximum(most, n)

    out_ref[2 * n_cand] = 0
    most_ref[0] = lax.fori_loop(0, text_ref.shape[0], pair, jnp.int32(0))
    row = lax.broadcasted_iota(jnp.int32, table_ref.shape, 0)
    lane = lax.broadcasted_iota(jnp.int32, table_ref.shape, 1)
    table = jnp.zeros(table_ref.shape, F32)
    at = jnp.int32(0)
    for c in range(n_cand):
        pos, neg = out_ref[c], out_ref[n_cand + c]
        used = (pos + neg) > 0
        here = row == jnp.where(used, at, -1)
        for k, value in ((c, 1.0), (n_cand, pos.astype(F32)), (n_cand + 1, neg.astype(F32))):
            table = jnp.where(here & (lane == k), value, table)
        at = at + jnp.where(used, 1, 0)
    table_ref[...] = table


def select_kernel(table_ref, *refs, slots):
    cand_refs, out_ref = refs[:-1], refs[-1]
    owned = cand_refs[0].shape[0]
    cands = [ref[j].astype(F32) for ref in cand_refs for j in range(owned)]
    for s in range(slots):
        picked = [table_ref[s : s + 1, c : c + 1] * cand for c, cand in enumerate(cands)]
        out_ref[s] = functools.reduce(jnp.add, picked).astype(out_ref.dtype)


def prepare_kernel(f_ref, out_ref):
    out_ref[...] = nt(eye(f_ref.shape[1]), f_ref[...]).astype(BF16)


def if_slot(slot, slots, group, work, idle):
    if slots % group == 0:
        work()
    else:
        pl.when(slot < slots)(work)
        pl.when(slot >= slots)(idle)


def clear(*refs):
    for ref in refs:
        ref[...] = jnp.zeros(ref.shape, ref.dtype)


def forward_kernel(f_ref, ft_ref, *refs, unit, first, group, scale):
    q_refs, (out_ref, weights_ref, top_ref, q_out_ref, q_ref) = refs[:group], refs[group:]
    me = lax.axis_index("frame")
    held, w, width = q_refs[0].shape
    slot = first + (me ^ unit)
    rows = group * w

    def work():
        for j in range(group):
            q_ref[me ^ j] = q_refs[j][jnp.minimum(slot, held - 1)].astype(F32)
        q = q_ref[...].reshape(rows, width).astype(BF16)
        q_out_ref[...] = q
        s = nt(f_ref[...], q) * scale
        top = jnp.max(s, axis=0, keepdims=True)
        weights = jnp.exp(s - top)
        weights_ref[...] = weights
        top_ref[...] = top
        out_ref[:rows] = turned(nn(ft_ref[...], weights.astype(BF16)), eye(rows))
        out_ref[rows:] = stack([top], LINES, width)

    if_slot(slot, held if first else group, group, work, lambda: clear(q_out_ref, out_ref))


def token_kernel(table_ref, q_ref, *refs, first, slots, group, tokens, n_cand):
    in_refs, (out_ref, direct_ref) = refs[:group], refs[group:]
    rows, width = q_ref.shape
    one = eye(rows)
    tops = [ref[rows : rows + 1, :rows] for ref in in_refs]
    m = functools.reduce(jnp.maximum, tops)
    context = jnp.zeros((rows, width), F32)
    for top, ref in zip(tops, in_refs):
        share = to_column(jnp.exp(top - m), one, 128)
        context = context + jnp.concatenate([share] * (width // 128), axis=1) * ref[:rows]
    q = q_ref[...].astype(F32)
    q_norm = lax.rsqrt(jnp.sum(q * q, axis=1, keepdims=True) + EPS)
    c_norm = lax.rsqrt(jnp.sum(context * context, axis=1, keepdims=True) + EPS)
    q_unit, c_unit = q * q_norm, context * c_norm
    cos = jnp.sum(q_unit * c_unit, axis=1, keepdims=True)
    score = jnp.sum(cos, axis=0, keepdims=True) / tokens
    logit = TEMP * score + BIAS
    table = table_ref[...]
    mine = lax.broadcasted_iota(jnp.int32, table.shape, 0) == first + lax.axis_index("frame")
    counts = jnp.sum(jnp.where(mine, table, 0.0), axis=0, keepdims=True)
    pos, neg = counts[:, n_cand : n_cand + 1], counts[:, n_cand + 1 : n_cand + 2]
    tail = jnp.log1p(jnp.exp(-jnp.abs(logit)))
    loss = pos * (jnp.maximum(-logit, 0.0) + tail) + neg * (jnp.maximum(logit, 0.0) + tail)
    grad_pos = (-LOSS_SCALE * TEMP / tokens) * jax.nn.sigmoid(-logit)
    grad_neg = (LOSS_SCALE * TEMP / tokens) * jax.nn.sigmoid(logit)
    side = q_unit - cos * c_unit
    d_pos = (grad_pos * side * c_norm).astype(BF16).astype(F32)
    d_neg = (grad_neg * side * c_norm).astype(BF16).astype(F32)
    out_ref[:rows] = (pos * d_pos + neg * d_neg).astype(BF16)
    extra = split(m) + split(jnp.broadcast_to(loss, (1, rows)))
    out_ref[rows:] = stack([x.astype(F32) for x in extra], EXTRA, width).astype(BF16)
    direct_ref[...] = (pos * grad_pos + neg * grad_neg) * (c_unit - cos * q_unit) * q_norm


def backward_kernel(f_ref, ft_ref, weights_ref, top_ref, d_ref, *refs, unit, first, slots, group, scale):
    if unit == 0:
        direct_ref, refs = refs[0], refs[1:]
    dq_ref, ds_ref, w_ref = refs
    width = f_ref.shape[1]
    rows = top_ref.shape[1]
    slot = first + (lax.axis_index("frame") ^ unit)

    def work():
        m = unpack(d_ref[rows:].astype(F32), 0, rows)
        weights = weights_ref[...] * jnp.exp(top_ref[...] - m)
        w_ref[...] = weights.astype(BF16)
        ds = (weights * nt(f_ref[...], d_ref[:rows]) * scale).astype(BF16)
        ds_ref[...] = ds
        dqt = nn(ft_ref[...], ds)
        dq = turned(dqt, eye(rows)) + direct_ref[...] if unit == 0 else nt(eye(rows), dqt.astype(BF16))
        dq_ref[...] = dq.reshape(group, rows // group, width)

    if_slot(slot, slots if first else group, group, work, lambda: clear(dq_ref, ds_ref, w_ref))


def spread_kernel(*refs, units, group):
    in_refs, d_refs, out_refs, loss_ref = refs[:units], refs[units : 2 * units], refs[2 * units : -1], refs[-1]
    me = lax.axis_index("frame")
    rows = d_refs[0].shape[0] - EXTRA
    loss = jnp.zeros(loss_ref.shape, F32)
    for i in range(units):
        loss = loss + unpack(d_refs[i][rows:].astype(F32), 1, loss_ref.shape[1])
        slot = (i // group) * group + (me ^ (i % group))
        for j, ref in enumerate(out_refs):
            if ref.shape[0] == units:
                ref[slot] = in_refs[i][me ^ j].astype(ref.dtype)
            else:

                @pl.when(slot < ref.shape[0])
                def _(ref=ref, i=i, j=j, slot=slot):
                    ref[slot] = in_refs[i][me ^ j].astype(ref.dtype)

    loss_ref[...] = loss


def first_frames_kernel(*refs, units, blocks):
    ds_refs, q_refs, w_refs, d_refs = [refs[k * units : (k + 1) * units] for k in range(4)]
    out_ref = refs[-1]
    rows = q_refs[0].shape[0]
    size = out_ref.shape[0] // blocks

    def block(b, carry):
        at = pl.ds(pl.multiple_of(b * size, size), size)
        total = None
        for i in range(units):
            term = nn(ds_refs[i][at], q_refs[i][...]) + nn(w_refs[i][at], d_refs[i][:rows])
            total = term if total is None else total + term
        out_ref[at] = total
        return carry

    lax.fori_loop(0, blocks, block, 0)


def frames_kernel(*refs, units, spare):
    ds_refs, q_refs, w_refs, d_refs = [refs[k * units : (k + 1) * units] for k in range(4)]
    out_ref, held_ref, sum_ref, sems = refs[-4:]
    before = refs[4 * units : -4]
    rows, depth = q_refs[0].shape[0], held_ref.shape[0]
    blocks = sems.shape[0]
    size = depth // blocks
    me = lax.axis_index("frame")
    copies = []
    for b in range(blocks):
        at = pl.ds(b * size, size)
        total = before[0][at] if before else None
        if spare is not None:
            sum_ref[...] = total
        for i in range(units):

            def term(i=i, at=at):
                return nn(ds_refs[i][at], q_refs[i][...]) + nn(w_refs[i][at], d_refs[i][:rows])

            if spare is not None:

                @pl.when((me ^ i) < spare)
                def _(term=term):
                    sum_ref[...] = sum_ref[...] + term()

            else:
                total = term() if total is None else total + term()
        if spare is not None:
            total = sum_ref[...]
        held_ref[at] = total.astype(BF16)
        copies.append(pltpu.make_async_copy(held_ref.at[at], out_ref.at[0, at], sems.at[b]))
        copies[-1].start()
    for copy in copies:
        copy.wait()


def finish_kernel(table_ref, pair_ref, across_ref, *refs):
    in_refs, outs = refs[:-3], refs[-3:]
    slots, w, width = in_refs[0].shape
    owned = (outs[0].shape[0] - EXTRA) // w
    totals = [functools.reduce(jnp.add, [x[s].astype(F32) for x in in_refs]) for s in range(slots)]
    for c in range(3 * owned):
        picked = [table_ref[s : s + 1, c : c + 1] * total for s, total in enumerate(totals)]
        j = c % owned
        outs[c // owned][j * w : (j + 1) * w] = functools.reduce(jnp.add, picked).astype(BF16)
    for ref, loss_ref in zip(outs, (across_ref, across_ref, pair_ref)):
        pieces = [x.astype(F32) for x in split(loss_ref[...])]
        ref[owned * w :] = stack(pieces, EXTRA, width).astype(BF16)


def close_kernel(pair_ref, near_ref, far_ref, cross_ref, out_ref, total_ref):
    owned, w, _ = out_ref.shape
    loss = pair_ref[...]
    for ref in (near_ref, far_ref, cross_ref):
        loss = loss + unpack(ref[owned * w :].astype(F32), 0, total_ref.shape[1])
    total_ref[...] = loss
    for j in range(owned):
        at = slice(j * w, (j + 1) * w)
        total = near_ref[at].astype(F32) + far_ref[at].astype(F32)
        out_ref[j] = (total + cross_ref[at].astype(F32)).astype(BF16)


def call(kernel, out_shape, in_specs, *args, scratch=(), flops=0, nbytes=1 << 20, vmem=16, out_specs=None):
    many = isinstance(out_shape, (list, tuple))
    return pl.pallas_call(
        kernel,
        out_shape=out_shape,
        in_specs=in_specs,
        out_specs=out_specs or ([VMEM] * len(out_shape) if many else VMEM),
        scratch_shapes=list(scratch),
        compiler_params=pltpu.CompilerParams(vmem_limit_bytes=vmem << 20),
        cost_estimate=pl.CostEstimate(flops=flops, bytes_accessed=nbytes, transcendentals=0),
    )(*args)


def permute(x, recs, group, move, sends=None):
    pairs = []
    for r in range(recs):
        for f in range(group):
            to_r, to_f = move(r, f)
            if sends is None or sends(f, to_f):
                pairs.append((r * group + f, to_r * group + to_f))
    return lax.ppermute(x, AXES, pairs)


def near_of(r, recs):
    return r ^ 1


def far_of(r, recs):
    return (r - 1) % recs if r % 2 == 0 else (r + 1) % recs


def cross_of(r, recs):
    return (r + recs // 2) % recs


def slot_body(slots, frames, near, far, cross, table, *, tokens, recs, group):
    owned, w, width = near.shape
    n_cand = 3 * owned
    rows = group * w
    depth = frames.shape[1]
    f = frames[0]
    scale = width ** (-0.5)
    rounds = -(-slots // group)
    units = rounds * group
    cost = 2 * rows * depth * width
    shape = jax.ShapeDtypeStruct
    xor = [lambda r, g, j=j: (r, g ^ j) for j in range(group)]
    order = [3, 1, 2, 0]

    q = call(
        functools.partial(select_kernel, slots=slots),
        shape((slots, w, width), BF16),
        [VMEM] * 4,
        table, near, far, cross,
    )
    qs = [q] + [permute(q, recs, group, xor[j]) for j in range(1, group)]
    ft = call(prepare_kernel, shape((width, depth), BF16), [VMEM], f, flops=cost)
    made, sent = {}, {}
    for r in range(rounds):
        for i in order:
            made[r, i] = call(
functools.partial(forward_kernel, unit=i, first=r * group, group=group, scale=scale),
                [
                    shape((rows + LINES, width), F32),
                    shape((depth, rows), F32),
                    shape((1, rows), F32),
                    shape((rows, width), BF16),
                ],
                [VMEM] * (2 + group),
                f, ft, *qs,
                scratch=[pltpu.VMEM((group, w, width), F32)],
                flops=2 * cost,
            )
            sent[r, i] = made[r, i][0]
            if i:
                sent[r, i] = permute(
                    sent[r, i], recs, group, xor[i], lambda a, b, r=r: r * group + b < slots
                )
    ds, directs = {}, {}
    for r in range(rounds):
        d, directs[r] = call(
            functools.partial(
                token_kernel, first=r * group, slots=slots, group=group, tokens=tokens, n_cand=n_cand
            ),
            [shape((rows + EXTRA, width), BF16), shape((rows, width), F32)],
            [VMEM] * (2 + group),
            table, made[r, 0][3], *[sent[r, i] for i in range(group)],
        )
        for i in order:
            ds[r, i] = d
            if i:
                ds[r, i] = permute(d, recs, group, xor[i], lambda a, b, r=r: r * group + a < slots)
    back = {}
    for r in range(rounds):
        for i in order:
            back[r, i] = call(
                functools.partial(
                    backward_kernel, unit=i, first=r * group, slots=slots, group=group, scale=scale
                ),
                [shape((group, w, width), F32), shape((depth, rows), BF16), shape((depth, rows), BF16)],
                [VMEM] * (6 if i == 0 else 5),
                f, ft, made[r, i][1], made[r, i][2], ds[r, i], *([directs[r]] if i == 0 else []),
                flops=2 * cost,
            )
    keys = [(r, i) for r in range(rounds) for i in range(group)]
    *dqs, loss = call(
        functools.partial(spread_kernel, units=units, group=group),
        [shape((slots, w, width), BF16)] * group + [shape((1, 128), F32)],
        [VMEM] * (2 * units),
        *[back[k][0] for k in keys], *[ds[k] for k in keys],
    )
    dqs = [dqs[0]] + [permute(dqs[j], recs, group, xor[j]) for j in range(1, group)]
    pair = loss + permute(loss, recs, group, lambda r, g: (r ^ 2, g))
    across = loss + permute(loss, recs, group, lambda r, g: (cross_of(r, recs), g))
    home = call(
        finish_kernel,
        [shape((owned * w + EXTRA, width), BF16)] * 3,
        [VMEM] * (3 + group),
        table, pair, across, *dqs,
    )

    def frame_args(n, some):
        return [(back[k][1], made[k][3], back[k][2], ds[k])[n] for k in some]

    got = []
    for x, where in zip(home, (near_of, far_of, cross_of)):
        got.append(permute(x, recs, group, lambda r, g: (where(r, recs), g)))
    total = []
    blocks = 6 if depth % 768 == 0 else 1
    if rounds > 1:
        args = [x for n in range(4) for x in frame_args(n, keys[:group])]
        total = [
            call(
                functools.partial(first_frames_kernel, units=group, blocks=blocks // 2 or 1),
                shape(frames.shape[1:], F32),
                [VMEM] * len(args),
                *args,
                flops=2 * group * cost,
            )
        ]
    args = [x for n in range(4) for x in frame_args(n, keys[-group:])]
    args[0], _ = lax.optimization_barrier((args[0], home[0]))
    args += total
    total = call(
        functools.partial(frames_kernel, units=group, spare=slots % group or None),
        pltpu.HBM(frames.shape, BF16),
        [VMEM] * len(args),
        *args,
        out_specs=pl.BlockSpec(memory_space=pltpu.HBM),
        scratch=[
            pltpu.VMEM((depth, width), BF16),
            pltpu.VMEM((depth // blocks, width), F32),
            pltpu.SemaphoreType.DMA((blocks,)),
        ],
        flops=2 * group * cost,
    )
    texts, loss = call(
        close_kernel,
        [shape((owned, w, width), BF16), shape((1, 128), F32)],
        [VMEM] * 4,
        pair, *got,
    )
    return loss[0, 0], total, texts


def body(frames, texts, pair_rec, pair_text, pair_label):
    recs, group = lax.axis_size("rec"), lax.axis_size("frame")
    owned, w, _ = texts.shape
    if group != 4 or w % 8 or recs != 8 or 3 * owned > 2 * group or owned * recs > 32:
        return general_body(frames, texts, pair_rec, pair_text, pair_label)
    fetched = []
    for to in (near_of, far_of, cross_of):
        fetched.append(permute(texts, recs, group, lambda r, g: (to(r, recs), g)))
    near, far, cross = fetched
    n_cand = 3 * owned
    table, most = pl.pallas_call(
        functools.partial(table_kernel, recs=recs, owned=owned),
        name="table",
        out_shape=[jax.ShapeDtypeStruct((8, 128), F32), jax.ShapeDtypeStruct((1,), jnp.int32)],
        in_specs=[SMEM] * 3,
        out_specs=[VMEM, SMEM],
        scratch_shapes=[pltpu.SMEM((n,), jnp.int32) for n in (2 * n_cand + 1, recs, recs)],
    )(pair_rec[:, 0], pair_text, pair_label)

    def run(slots, *args):
        return slot_body(slots, *args, tokens=w * group, recs=recs, group=group)

    args = (frames, near, far, cross, table)
    return lax.cond(
        most[0] <= group, functools.partial(run, group), functools.partial(run, n_cand), *args
    )


def solution(mesh):
    return jax.shard_map(
        body,
        mesh=mesh,
        in_specs=(P("rec", "frame", None), P("rec", "frame", None), P(), P(), P()),
        out_specs=(P(), P("rec", "frame", None), P("rec", "frame", None)),
        check_vma=False,
    )
```

```python
import functools

import jax
import jax.numpy as jnp
from jax import lax
from jax.experimental import pallas as pl
from jax.experimental.pallas import tpu as pltpu
from jax.sharding import PartitionSpec as P

MOST = 6
EPS = 1e-06
TEMP = 10.0
BIAS = -1.0
LOSS_SCALE = 2048.0

F32 = jnp.float32
BF16 = jnp.bfloat16
EXTRA = 16
LINES = 8
AXES = ("rec", "frame")
VMEM = pl.BlockSpec(memory_space=pltpu.VMEM)
SMEM = pl.BlockSpec(memory_space=pltpu.SMEM)


def nt(a, b):
    return lax.dot_general(a, b, (((1,), (1,)), ((), ())), preferred_element_type=F32)


def nn(a, b):
    return lax.dot_general(a, b, (((1,), (0,)), ((), ())), preferred_element_type=F32)


def slot_tables(pair_rec, pair_text, pair_label, here, most):
    record = pair_rec[:, 0]
    count = record.shape[0]
    order = jnp.arange(count, dtype=jnp.int32)
    same = (record[:, None] == record[None, :]).astype(jnp.int32)
    earlier = (order[None, :] < order[:, None]).astype(jnp.int32)
    rank = jnp.sum(same * earlier, axis=1)
    places = jnp.arange(most, dtype=jnp.int32)
    chosen = ((record[None, :] == here) & (rank[None, :] == places[:, None])).astype(jnp.int32)
    valid = jnp.sum(chosen, axis=1)
    slot_text = jnp.sum(chosen * pair_text[None, :], axis=1)
    sign = jnp.sum(chosen * (2 * pair_label[None, :] - 1), axis=1)
    return (valid, slot_text, sign)


def pair_terms(score, valid, sign, tokens):
    margin = -sign * (TEMP * score + BIAS)
    loss_part = valid * jax.nn.softplus(margin)
    grad_cos = -LOSS_SCALE * TEMP * valid * sign * jax.nn.sigmoid(margin) / tokens
    return (loss_part, grad_cos)


def general_body(frames, texts, pair_rec, pair_text, pair_label):
    here = lax.axis_index("rec")
    part = lax.axis_index("frame")
    owned, width_rows, width = texts.shape
    tokens = width_rows * lax.axis_size("frame")
    n_text = owned * lax.axis_size("rec")
    valid, slot_text, sign = slot_tables(pair_rec, pair_text, pair_label, here, MOST)
    valid_f = valid.astype(jnp.float32)
    sign_f = sign.astype(jnp.float32)
    picks = (
        (slot_text[:, None] == jnp.arange(n_text, dtype=jnp.int32)[None, :]) & (valid[:, None] > 0)
    ).astype(jnp.bfloat16)
    local = jnp.einsum(
        "jc,cgx->jgx",
        picks,
        lax.all_gather(texts, "rec", axis=0, tiled=True),
        preferred_element_type=jnp.float32,
    ).astype(jnp.bfloat16)
    query_vectors = lax.all_gather(local, "frame", axis=1, tiled=True)
    upstream_signal = frames[0]
    logit_scale = width ** (-0.5)
    pair_scores = (
        jnp.einsum(
            "ype,je->ypj", query_vectors, upstream_signal, preferred_element_type=jnp.float32
        )
        * logit_scale
    )
    local_max = jnp.max(pair_scores, axis=2)
    row_max = lax.pmax(local_max, "frame")
    expo = jnp.exp(pair_scores - row_max[..., None])
    batch_weights = expo.astype(jnp.bfloat16)
    value_partial = jnp.einsum(
        "pqx,xh->pqh", batch_weights, upstream_signal, preferred_element_type=jnp.float32
    )
    query_f = query_vectors.astype(jnp.float32)
    q_norm = lax.rsqrt(jnp.sum(query_f * query_f, axis=2) + EPS)
    q_unit = query_f * q_norm[..., None]
    context = lax.psum(value_partial, "frame")
    c_norm = lax.rsqrt(jnp.sum(context * context, axis=2) + EPS)
    c_unit = context * c_norm[..., None]
    cos = jnp.sum(q_unit * c_unit, axis=2)
    score = jnp.mean(cos, axis=1)
    loss_part, grad_cos = pair_terms(score, valid_f, sign_f, tokens)
    weight = grad_cos[:, None, None]
    d_context = weight * (q_unit - cos[..., None] * c_unit) * c_norm[..., None]
    direct = weight * (c_unit - cos[..., None] * q_unit) * q_norm[..., None]
    direct_own = lax.dynamic_slice_in_dim(direct, part * width_rows, width_rows, 1)
    context_batch_gradient = d_context.astype(jnp.bfloat16)
    weight_gradient = jnp.einsum(
        "ype,je->ypj", context_batch_gradient, upstream_signal, preferred_element_type=jnp.float32
    )
    score_gradient = (expo * weight_gradient * logit_scale).astype(jnp.bfloat16)
    d_query = lax.psum_scatter(
        jnp.einsum(
            "slf,fd->lsd", score_gradient, upstream_signal, preferred_element_type=jnp.float32
        ),
        "frame",
        scatter_dimension=0,
        tiled=True,
    )
    d_query = d_query + jnp.transpose(direct_own, (1, 0, 2))
    text_term = jnp.einsum(
        "st,lsd->tld", picks.astype(jnp.float32), d_query, precision=lax.Precision.HIGHEST
    )
    grad_texts = lax.psum_scatter(text_term, "rec", scatter_dimension=0, tiled=True).astype(
        jnp.bfloat16
    )
    frame_loss_piece = jnp.einsum(
        "cvm,cvz->mz", score_gradient, query_vectors, preferred_element_type=jnp.float32
    )
    frame_loss_piece = frame_loss_piece + jnp.einsum(
        "cvm,cvz->mz", batch_weights, context_batch_gradient, preferred_element_type=jnp.float32
    )
    grad_frames = frame_loss_piece.astype(jnp.bfloat16)[None]
    loss = lax.psum(jnp.sum(loss_part), "rec")
    return (loss, grad_frames, grad_texts)


def split(line):
    pieces = []
    for _ in range(3):
        piece = line.astype(BF16)
        pieces.append(piece)
        line = line - piece.astype(F32)
    return pieces


def stack(lines, count, width):
    n = lines[0].shape[1]
    place = lax.broadcasted_iota(jnp.int32, (count, n), 0)
    out = jnp.zeros((count, n), F32)
    for at, line in enumerate(lines):
        out = jnp.where(place == at, line, out)
    if n < width:
        out = jnp.concatenate([out, jnp.zeros((count, width - n), F32)], axis=1)
    return out


def unpack(extra, i, n):
    got = [extra[3 * i + j : 3 * i + j + 1, :n] for j in range(3)]
    return (got[0] + got[1]) + got[2]


def diagonal(n):
    r = lax.broadcasted_iota(jnp.int32, (n, n), 0)
    c = lax.broadcasted_iota(jnp.int32, (n, n), 1)
    return r == c


def eye(n):
    return jnp.where(diagonal(n), 1.0, 0.0).astype(BF16)


def to_column(line, one, lanes):
    n = line.shape[1]
    out = None
    for piece in split(line):
        term = nt(one, jnp.broadcast_to(piece, (lanes, n)))
        out = term if out is None else out + term
    return out


def turned(x, one):
    high = x.astype(BF16)
    low = (x - high.astype(F32)).astype(BF16)
    return nt(one, high) + nt(one, low)


def table_kernel(rec_ref, text_ref, label_ref, table_ref, most_ref, out_ref, seen_ref, count_ref, *, recs, owned):
    here = lax.axis_index("rec")
    odd = lax.rem(here, 2)
    far, cross = lax.rem(here + 2 * odd + recs - 1, recs), lax.rem(here + recs // 2, recs)
    n_cand = 3 * owned
    for i in range(2 * n_cand):
        out_ref[i] = 0
    for r in range(recs):
        seen_ref[r] = 0
        count_ref[r] = 0

    def pair(p, most):
        rec, text, label = rec_ref[p], text_ref[p], label_ref[p]
        seen, bit = seen_ref[rec], lax.shift_left(jnp.int32(1), text)
        n = count_ref[rec] + jnp.where((seen & bit) == 0, 1, 0)
        seen_ref[rec] = seen | bit
        count_ref[rec] = n
        owner = lax.div(text, owned)
        which = jnp.where(owner == far, 1, jnp.where(owner == cross, 2, 0))
        at = which * owned + text - owner * owned + (1 - label) * n_cand
        at = jnp.where(rec == here, at, 2 * n_cand)
        out_ref[at] = out_ref[at] + 1
        return jnp.maximum(most, n)

    out_ref[2 * n_cand] = 0
    most_ref[0] = lax.fori_loop(0, text_ref.shape[0], pair, jnp.int32(0))
    row = lax.broadcasted_iota(jnp.int32, table_ref.shape, 0)
    lane = lax.broadcasted_iota(jnp.int32, table_ref.shape, 1)
    table = jnp.zeros(table_ref.shape, F32)
    at = jnp.int32(0)
    for c in range(n_cand):
        pos, neg = out_ref[c], out_ref[n_cand + c]
        used = (pos + neg) > 0
        here = row == jnp.where(used, at, -1)
        for k, value in ((c, 1.0), (n_cand, pos.astype(F32)), (n_cand + 1, neg.astype(F32))):
            table = jnp.where(here & (lane == k), value, table)
        at = at + jnp.where(used, 1, 0)
    table_ref[...] = table


def select_kernel(table_ref, *refs, slots):
    cand_refs, out_ref = refs[:-1], refs[-1]
    owned = cand_refs[0].shape[0]
    cands = [ref[j].astype(F32) for ref in cand_refs for j in range(owned)]
    for s in range(slots):
        picked = [table_ref[s : s + 1, c : c + 1] * cand for c, cand in enumerate(cands)]
        out_ref[s] = functools.reduce(jnp.add, picked).astype(out_ref.dtype)


def prepare_kernel(f_ref, out_ref):
    out_ref[...] = nt(eye(f_ref.shape[1]), f_ref[...]).astype(BF16)


def if_slot(slot, slots, group, work, idle):
    if slots % group == 0:
        work()
    else:
        pl.when(slot < slots)(work)
        pl.when(slot >= slots)(idle)


def clear(*refs):
    for ref in refs:
        ref[...] = jnp.zeros(ref.shape, ref.dtype)


def forward_kernel(f_ref, ft_ref, *refs, unit, first, group, scale):
    q_refs, (out_ref, weights_ref, top_ref, q_out_ref, q_ref) = refs[:group], refs[group:]
    me = lax.axis_index("frame")
    held, w, width = q_refs[0].shape
    slot = first + (me ^ unit)
    rows = group * w

    def work():
        for j in range(group):
            q_ref[me ^ j] = q_refs[j][jnp.minimum(slot, held - 1)].astype(F32)
        q = q_ref[...].reshape(rows, width).astype(BF16)
        q_out_ref[...] = q
        s = nt(f_ref[...], q) * scale
        top = jnp.max(s, axis=0, keepdims=True)
        weights = jnp.exp(s - top)
        weights_ref[...] = weights
        top_ref[...] = top
        out_ref[:rows] = turned(nn(ft_ref[...], weights.astype(BF16)), eye(rows))
        out_ref[rows:] = stack([top], LINES, width)

    if_slot(slot, held if first else group, group, work, lambda: clear(q_out_ref, out_ref))


def token_kernel(table_ref, q_ref, *refs, first, slots, group, tokens, n_cand):
    in_refs, (out_ref, direct_ref) = refs[:group], refs[group:]
    rows, width = q_ref.shape
    one = eye(rows)
    tops = [ref[rows : rows + 1, :rows] for ref in in_refs]
    m = functools.reduce(jnp.maximum, tops)
    context = jnp.zeros((rows, width), F32)
    for top, ref in zip(tops, in_refs):
        share = to_column(jnp.exp(top - m), one, 128)
        context = context + jnp.concatenate([share] * (width // 128), axis=1) * ref[:rows]
    q = q_ref[...].astype(F32)
    q_norm = lax.rsqrt(jnp.sum(q * q, axis=1, keepdims=True) + EPS)
    c_norm = lax.rsqrt(jnp.sum(context * context, axis=1, keepdims=True) + EPS)
    q_unit, c_unit = q * q_norm, context * c_norm
    cos = jnp.sum(q_unit * c_unit, axis=1, keepdims=True)
    score = jnp.sum(cos, axis=0, keepdims=True) / tokens
    logit = TEMP * score + BIAS
    table = table_ref[...]
    mine = lax.broadcasted_iota(jnp.int32, table.shape, 0) == first + lax.axis_index("frame")
    counts = jnp.sum(jnp.where(mine, table, 0.0), axis=0, keepdims=True)
    pos, neg = counts[:, n_cand : n_cand + 1], counts[:, n_cand + 1 : n_cand + 2]
    tail = jnp.log1p(jnp.exp(-jnp.abs(logit)))
    loss = pos * (jnp.maximum(-logit, 0.0) + tail) + neg * (jnp.maximum(logit, 0.0) + tail)
    grad_pos = (-LOSS_SCALE * TEMP / tokens) * jax.nn.sigmoid(-logit)
    grad_neg = (LOSS_SCALE * TEMP / tokens) * jax.nn.sigmoid(logit)
    side = q_unit - cos * c_unit
    d_pos = (grad_pos * side * c_norm).astype(BF16).astype(F32)
    d_neg = (grad_neg * side * c_norm).astype(BF16).astype(F32)
    out_ref[:rows] = (pos * d_pos + neg * d_neg).astype(BF16)
    extra = split(m) + split(jnp.broadcast_to(loss, (1, rows)))
    out_ref[rows:] = stack([x.astype(F32) for x in extra], EXTRA, width).astype(BF16)
    direct_ref[...] = (pos * grad_pos + neg * grad_neg) * (c_unit - cos * q_unit) * q_norm


def backward_kernel(f_ref, ft_ref, weights_ref, top_ref, d_ref, *refs, unit, first, slots, group, scale):
    if unit == 0:
        direct_ref, refs = refs[0], refs[1:]
    dq_ref, ds_ref, w_ref = refs
    width = f_ref.shape[1]
    rows = top_ref.shape[1]
    slot = first + (lax.axis_index("frame") ^ unit)

    def work():
        m = unpack(d_ref[rows:].astype(F32), 0, rows)
        weights = weights_ref[...] * jnp.exp(top_ref[...] - m)
        w_ref[...] = weights.astype(BF16)
        ds = (weights * nt(f_ref[...], d_ref[:rows]) * scale).astype(BF16)
        ds_ref[...] = ds
        dqt = nn(ft_ref[...], ds)
        dq = turned(dqt, eye(rows)) + direct_ref[...] if unit == 0 else nt(eye(rows), dqt.astype(BF16))
        dq_ref[...] = dq.reshape(group, rows // group, width)

    if_slot(slot, slots if first else group, group, work, lambda: clear(dq_ref, ds_ref, w_ref))


def spread_kernel(*refs, units, group):
    in_refs, d_refs, out_refs, loss_ref = refs[:units], refs[units : 2 * units], refs[2 * units : -1], refs[-1]
    me = lax.axis_index("frame")
    rows = d_refs[0].shape[0] - EXTRA
    loss = jnp.zeros(loss_ref.shape, F32)
    for i in range(units):
        loss = loss + unpack(d_refs[i][rows:].astype(F32), 1, loss_ref.shape[1])
        slot = (i // group) * group + (me ^ (i % group))
        for j, ref in enumerate(out_refs):
            if ref.shape[0] == units:
                ref[slot] = in_refs[i][me ^ j].astype(ref.dtype)
            else:

                @pl.when(slot < ref.shape[0])
                def _(ref=ref, i=i, j=j, slot=slot):
                    ref[slot] = in_refs[i][me ^ j].astype(ref.dtype)

    loss_ref[...] = loss


def first_frames_kernel(*refs, units, blocks):
    ds_refs, q_refs, w_refs, d_refs = [refs[k * units : (k + 1) * units] for k in range(4)]
    out_ref = refs[-1]
    rows = q_refs[0].shape[0]
    size = out_ref.shape[0] // blocks

    def block(b, carry):
        at = pl.ds(pl.multiple_of(b * size, size), size)
        total = None
        for i in range(units):
            term = nn(ds_refs[i][at], q_refs[i][...]) + nn(w_refs[i][at], d_refs[i][:rows])
            total = term if total is None else total + term
        out_ref[at] = total
        return carry

    lax.fori_loop(0, blocks, block, 0)


def frames_kernel(*refs, units, spare):
    ds_refs, q_refs, w_refs, d_refs = [refs[k * units : (k + 1) * units] for k in range(4)]
    out_ref, held_ref, sum_ref, sems = refs[-4:]
    before = refs[4 * units : -4]
    rows, depth = q_refs[0].shape[0], held_ref.shape[0]
    blocks = sems.shape[0]
    size = depth // blocks
    me = lax.axis_index("frame")
    copies = []
    for b in range(blocks):
        at = pl.ds(b * size, size)
        total = before[0][at] if before else None
        if spare is not None:
            sum_ref[...] = total
        for i in range(units):

            def term(i=i, at=at):
                return nn(ds_refs[i][at], q_refs[i][...]) + nn(w_refs[i][at], d_refs[i][:rows])

            if spare is not None:

                @pl.when((me ^ i) < spare)
                def _(term=term):
                    sum_ref[...] = sum_ref[...] + term()

            else:
                total = term() if total is None else total + term()
        if spare is not None:
            total = sum_ref[...]
        held_ref[at] = total.astype(BF16)
        copies.append(pltpu.make_async_copy(held_ref.at[at], out_ref.at[0, at], sems.at[b]))
        copies[-1].start()
    for copy in copies:
        copy.wait()


def finish_kernel(table_ref, pair_ref, across_ref, *refs):
    in_refs, outs = refs[:-3], refs[-3:]
    slots, w, width = in_refs[0].shape
    owned = (outs[0].shape[0] - EXTRA) // w
    totals = [functools.reduce(jnp.add, [x[s].astype(F32) for x in in_refs]) for s in range(slots)]
    for c in range(3 * owned):
        picked = [table_ref[s : s + 1, c : c + 1] * total for s, total in enumerate(totals)]
        j = c % owned
        outs[c // owned][j * w : (j + 1) * w] = functools.reduce(jnp.add, picked).astype(BF16)
    for ref, loss_ref in zip(outs, (across_ref, across_ref, pair_ref)):
        pieces = [x.astype(F32) for x in split(loss_ref[...])]
        ref[owned * w :] = stack(pieces, EXTRA, width).astype(BF16)


def close_kernel(pair_ref, near_ref, far_ref, cross_ref, out_ref, total_ref):
    owned, w, _ = out_ref.shape
    loss = pair_ref[...]
    for ref in (near_ref, far_ref, cross_ref):
        loss = loss + unpack(ref[owned * w :].astype(F32), 0, total_ref.shape[1])
    total_ref[...] = loss
    for j in range(owned):
        at = slice(j * w, (j + 1) * w)
        total = near_ref[at].astype(F32) + far_ref[at].astype(F32)
        out_ref[j] = (total + cross_ref[at].astype(F32)).astype(BF16)


def call(kernel, out_shape, in_specs, *args, scratch=(), flops=0, nbytes=1 << 20, vmem=16, out_specs=None):
    many = isinstance(out_shape, (list, tuple))
    return pl.pallas_call(
        kernel,
        out_shape=out_shape,
        in_specs=in_specs,
        out_specs=out_specs or ([VMEM] * len(out_shape) if many else VMEM),
        scratch_shapes=list(scratch),
        compiler_params=pltpu.CompilerParams(vmem_limit_bytes=vmem << 20),
        cost_estimate=pl.CostEstimate(flops=flops, bytes_accessed=nbytes, transcendentals=0),
    )(*args)


def permute(x, recs, group, move, sends=None):
    pairs = []
    for r in range(recs):
        for f in range(group):
            to_r, to_f = move(r, f)
            if sends is None or sends(f, to_f):
                pairs.append((r * group + f, to_r * group + to_f))
    return lax.ppermute(x, AXES, pairs)


def near_of(r, recs):
    return r ^ 1


def far_of(r, recs):
    return (r - 1) % recs if r % 2 == 0 else (r + 1) % recs


def cross_of(r, recs):
    return (r + recs // 2) % recs


def slot_body(slots, frames, near, far, cross, table, *, tokens, recs, group):
    owned, w, width = near.shape
    n_cand = 3 * owned
    rows = group * w
    depth = frames.shape[1]
    f = frames[0]
    scale = width ** (-0.5)
    rounds = -(-slots // group)
    units = rounds * group
    cost = 2 * rows * depth * width
    shape = jax.ShapeDtypeStruct
    xor = [lambda r, g, j=j: (r, g ^ j) for j in range(group)]
    order = [3, 1, 2, 0]

    q = call(
        functools.partial(select_kernel, slots=slots),
        shape((slots, w, width), BF16),
        [VMEM] * 4,
        table, near, far, cross,
    )
    qs = [q]
    for j in range(1, group):
        qs.append(permute(q, recs, group, xor[j]))
    ft = call(prepare_kernel, shape((width, depth), BF16), [VMEM], f, flops=cost)
    made, sent = {}, {}
    for r in range(rounds):
        for i in order:
            made[r, i] = call(
functools.partial(forward_kernel, unit=i, first=r * group, group=group, scale=scale),
                [
                    shape((rows + LINES, width), F32),
                    shape((depth, rows), F32),
                    shape((1, rows), F32),
                    shape((rows, width), BF16),
                ],
                [VMEM] * (2 + group),
                f, ft, *qs,
                scratch=[pltpu.VMEM((group, w, width), F32)],
                flops=2 * cost,
            )
            sent[r, i] = made[r, i][0]
            if i:
                sent[r, i] = permute(
                    sent[r, i], recs, group, xor[i], lambda a, b, r=r: r * group + b < slots
                )
    ds, directs = {}, {}
    for r in range(rounds):
        d, directs[r] = call(
            functools.partial(
                token_kernel, first=r * group, slots=slots, group=group, tokens=tokens, n_cand=n_cand
            ),
            [shape((rows + EXTRA, width), BF16), shape((rows, width), F32)],
            [VMEM] * (2 + group),
            table, made[r, 0][3], *[sent[r, i] for i in range(group)],
        )
        for i in order:
            ds[r, i] = d
            if i:
                ds[r, i] = permute(d, recs, group, xor[i], lambda a, b, r=r: r * group + a < slots)
    back = {}
    for r in range(rounds):
        for i in order:
            back[r, i] = call(
                functools.partial(
                    backward_kernel, unit=i, first=r * group, slots=slots, group=group, scale=scale
                ),
                [shape((group, w, width), F32), shape((depth, rows), BF16), shape((depth, rows), BF16)],
                [VMEM] * (6 if i == 0 else 5),
                f, ft, made[r, i][1], made[r, i][2], ds[r, i], *([directs[r]] if i == 0 else []),
                flops=2 * cost,
            )
    keys = [(r, i) for r in range(rounds) for i in range(group)]
    *dqs, loss = call(
        functools.partial(spread_kernel, units=units, group=group),
        [shape((slots, w, width), BF16)] * group + [shape((1, 128), F32)],
        [VMEM] * (2 * units),
        *[back[k][0] for k in keys], *[ds[k] for k in keys],
    )
    for j in range(1, group):
        dqs[j] = permute(dqs[j], recs, group, xor[j])
    pair = loss + permute(loss, recs, group, lambda r, g: (r ^ 2, g))
    across = loss + permute(loss, recs, group, lambda r, g: (cross_of(r, recs), g))
    home = call(
        finish_kernel,
        [shape((owned * w + EXTRA, width), BF16)] * 3,
        [VMEM] * (3 + group),
        table, pair, across, *dqs,
    )

    def frame_args(n, some):
        return [(back[k][1], made[k][3], back[k][2], ds[k])[n] for k in some]

    got = []
    for x, where in zip(home, (near_of, far_of, cross_of)):
        got.append(permute(x, recs, group, lambda r, g: (where(r, recs), g)))
    total = []
    blocks = 6 if depth % 768 == 0 else 1
    if rounds > 1:
        args = [x for n in range(4) for x in frame_args(n, keys[:group])]
        total = [
            call(
                functools.partial(first_frames_kernel, units=group, blocks=blocks // 2 or 1),
                shape(frames.shape[1:], F32),
                [VMEM] * len(args),
                *args,
                flops=2 * group * cost,
            )
        ]
    args = [x for n in range(4) for x in frame_args(n, keys[-group:])]
    args[0], _ = lax.optimization_barrier((args[0], home[0]))
    args += total
    total = call(
        functools.partial(frames_kernel, units=group, spare=slots % group or None),
        pltpu.HBM(frames.shape, BF16),
        [VMEM] * len(args),
        *args,
        out_specs=pl.BlockSpec(memory_space=pltpu.HBM),
        scratch=[
            pltpu.VMEM((depth, width), BF16),
            pltpu.VMEM((depth // blocks, width), F32),
            pltpu.SemaphoreType.DMA((blocks,)),
        ],
        flops=2 * group * cost,
    )
    texts, loss = call(
        close_kernel,
        [shape((owned, w, width), BF16), shape((1, 128), F32)],
        [VMEM] * 4,
        pair, *got,
    )
    return loss[0, 0], total, texts


def body(frames, texts, pair_rec, pair_text, pair_label):
    recs, group = lax.axis_size("rec"), lax.axis_size("frame")
    owned, w, _ = texts.shape
    if group != 4 or w % 8 or recs != 8 or 3 * owned > 2 * group or owned * recs > 32:
        return general_body(frames, texts, pair_rec, pair_text, pair_label)
    fetched = []
    for to in (near_of, far_of, cross_of):
        fetched.append(permute(texts, recs, group, lambda r, g: (to(r, recs), g)))
    near, far, cross = fetched
    n_cand = 3 * owned
    table, most = pl.pallas_call(
        functools.partial(table_kernel, recs=recs, owned=owned),
        name="table",
        out_shape=[jax.ShapeDtypeStruct((8, 128), F32), jax.ShapeDtypeStruct((1,), jnp.int32)],
        in_specs=[SMEM] * 3,
        out_specs=[VMEM, SMEM],
        scratch_shapes=[pltpu.SMEM((n,), jnp.int32) for n in (2 * n_cand + 1, recs, recs)],
    )(pair_rec[:, 0], pair_text, pair_label)

    def run(slots, *args):
        return slot_body(slots, *args, tokens=w * group, recs=recs, group=group)

    args = (frames, near, far, cross, table)
    return lax.cond(
        most[0] <= group, functools.partial(run, group), functools.partial(run, n_cand), *args
    )


def solution(mesh):
    return jax.shard_map(
        body,
        mesh=mesh,
        in_specs=(P("rec", "frame", None), P("rec", "frame", None), P(), P(), P()),
        out_specs=(P(), P("rec", "frame", None), P("rec", "frame", None)),
        check_vma=False,
    )
```
